256 devices in a mesh: ctx: 16 (over z, core), exp: 16 (over x, y).
Axes of the slice: x: 4, y: 4, z: 8, core: 2. Of those that a mesh axis runs over, the one named last changes fastest.
Arguments:
- mixer_input: bfloat16 [2048, 4096], P('ctx', 'exp'), may hold values from -6 to 6
- mixer_gate: bfloat16 [2048, 4096], P('ctx', 'exp'), may hold values from -6 to 6
- step_low: bfloat16 [2048, 128], P('ctx'), may hold values from -16 to 16
- step_proj: bfloat16 [128, 4096], P(None, 'exp'), may hold values from -0.5 to 0.5
- step_bias: float32 [4096], P('exp'), may hold values from -1 to 1
- decay_rate: float32 [16, 4096], P(None, 'exp'), may hold values from 2.4414063e-05 to 0.1
- input_coef: float32 [16, 2048], P(None, 'ctx'), may hold values from -6 to 6
- output_coef: float32 [16, 2048], P(None, 'ctx'), may hold values from -0.625 to 0.625
- conv_taps: float32 [4, 4096], P(None, 'exp'), may hold values from -3 to 3
- conv_bias: float32 [4096], P('exp'), may hold values from -0.5 to 0.5
- skip_gain: float32 [4096], P('exp'), may hold values from 0.5 to 1.5
- out_weight: bfloat16 [4096, 2048], P('exp'), may hold values from -0.09375 to 0.09375
- residual: bfloat16 [2048, 2048], P(('ctx', 'exp')), may hold values from -6 to 6
- norm_gain: float32 [2048], replicated, may hold values from 0.5 to 1.5
- expert_ids: int32 [2048, 2], P(('ctx', 'exp')), may hold values from 0 to 15, all different within a row; in each aligned block of 8 rows (0 to 7, 8 to 15, ...) at most 2 rows name the same one
- gate_scores: float32 [2048, 2], P(('ctx', 'exp')), may hold values from 0.1 to 1
- gate_weight: bfloat16 [16, 2048, 14336], P('exp', None, 'ctx'), may hold values from -0.125 to 0.125
- up_weight: bfloat16 [16, 2048, 14336], P('exp', None, 'ctx'), may hold values from -0.125 to 0.125
- down_weight: bfloat16 [16, 14336, 2048], P('exp', 'ctx'), may hold values from -0.046875 to 0.046875
- cotangent: bfloat16 [2048, 2048], P(('ctx', 'exp')), may hold values from -6 to 6
Outputs:
- layer_out: bfloat16 [2048, 2048], P(('ctx', 'exp'))
- grad_hidden: float32 [2048, 2048], P(('ctx', 'exp'))
- grad_scores: float32 [2048, 2], P(('ctx', 'exp'))
The draws below stay inside these ranges and needn't reach their ends.
Inputs may be any that keep to these rules, and one draw needn't show every extreme that they name: `expert_ids`: A token's two experts differ. In each device's block of 8 consecutive tokens, no expert is named by more than 2 of the block's choices, and in every draw some expert is named exactly 2 times in some block.
All inputs are finite; a program needn't handle non-finite values.
Results may differ from the reference program's by a relative error of at most 0.013.
Values may be sent and summed in bfloat16 or wider, within the bound.
No kernel may reach another device: no remote copies, remote signals or barrier semaphores. Data moves between devices by JAX's collectives and lax.ppermute only.
A program may use at most 128 MiB of HBM per device.

```python
import math
import jax
import jax.numpy as jnp
import numpy as np
from jax import lax

D = 2048
DI = 4096
FFH = 14336
R = 128
NS = 16
KCONV = 4
TOK_DEV = 8
EXPERTS = 16
CAP = 2
SEQUENCE_LENGTH = 2048


def draw_step_low(key, part):
    key_noise = jax.random.fold_in(key, 11)
    key_dir = jax.random.fold_in(key, 12)
    key_level = jax.random.fold_in(key, 13)
    pulse_random_key = jax.random.fold_in(key, 14)
    span = TOK_DEV * EXPERTS
    blocks = SEQUENCE_LENGTH // span
    heading_vector = jax.random.normal(key_dir, (R,), jnp.float32)
    random_jitter = 0.6 * jax.random.normal(key_noise, (SEQUENCE_LENGTH, R), jnp.float32)
    level = jax.random.uniform(key_level, (blocks,), jnp.float32, -2.5, 2.5)
    level_of_rows = jnp.repeat(level, span)
    chosen_places = jax.random.randint(pulse_random_key, (4,), 0, SEQUENCE_LENGTH)
    token_positions = jnp.arange(SEQUENCE_LENGTH, dtype=jnp.int32)
    spike_pulse = jnp.sum((token_positions[:, None] == chosen_places[None, :]).astype(jnp.float32), axis=1)
    value_entries = random_jitter + (level_of_rows + 4.0 * spike_pulse)[:, None] * heading_vector[None, :]
    return jnp.clip(value_entries, -16.0, 16.0).astype(jnp.bfloat16)


def steps_of(stream_key, extent, shards, low, largest):
    factor_of = 1.0
    for dim, blocks in shards:
        heights = jax.random.uniform(jax.random.fold_in(jax.random.fold_in(stream_key, 6), dim), (blocks,), jnp.float32, low / len(shards), largest / len(shards))
        factor_of = factor_of * jnp.repeat(jnp.exp(heights), extent[dim] // blocks).reshape((-1,) + (1,) * (len(extent) - 1 - dim))
    return factor_of


def routed_block(own_key, own, number, rows, count, top, bound, skew):
    order = jax.random.permutation(own_key, count)
    crowded, common = portions_of(count, rows * top, bound, skew, True), portions_of(count, rows * top, bound, skew, False)
    places = jnp.arange(count)

    def named(sizes, turn):
        used = int((sizes > 0).sum())
        fixed = max(1, used // 4)
        moved = fixed + (places - fixed + turn * (used - fixed)) % max(1, count - fixed)
        return jnp.zeros((count,), jnp.int32).at[order[jnp.where(places < fixed, places, moved)]].set(jnp.asarray(sizes, jnp.int32))

    sizes = jnp.where(number % 4 == 0, named(crowded, number // 4), named(common, number - number // 4 - 1))
    mixed = jax.random.permutation(jax.random.fold_in(own, 3), count)
    source_of, taker = mixed[0:count // 2 * 2:2], mixed[1:count // 2 * 2:2]
    margin = jnp.minimum(sizes[source_of] - 1, bound - sizes[taker]) // 2
    margin = jnp.where((source_of == order[0]) | (taker == order[0]) | (sizes[taker] == 0), 0, jnp.maximum(margin, 0))
    moved = jax.random.randint(jax.random.fold_in(own, 4), (count // 2,), 0, 1 << 20) % (margin + 1)
    sizes = sizes.at[source_of].add(-moved).at[taker].add(moved)
    items = jnp.searchsorted(jnp.cumsum(sizes), jnp.arange(rows * top), side="right").astype(jnp.int32)
    listing = items.reshape(top, rows).T
    listing = listing[jax.random.permutation(jax.random.fold_in(own, 1), rows)]
    turn = jax.random.randint(jax.random.fold_in(own, 2), (rows, 1), 0, top)
    return jnp.take_along_axis(listing, (jnp.arange(top)[None, :] + turn) % top, axis=1)


def portions_of(count, total, reach, lean, full):
    weights = [(1 << 20) // math.isqrt(rank ** lean) + 1 for rank in range(1, count + 1)]
    largest = reach if full else min(reach, max(-(-total // count), total * weights[0] // sum(weights)))
    least = 1 if total - largest >= count - 1 else 0
    given, surplus = [largest] + [least] * (count - 1), total - largest - least * (count - 1)
    while surplus > 0:
        free = [i for i in range(1, count) if given[i] < largest] or [i for i in range(1, count) if given[i] < reach]
        pool, left = sum([weights[i] for i in free]), surplus
        for i in free:
            more = min(reach - given[i], max(1, left * weights[i] // pool), surplus)
            given[i] = given[i] + more
            surplus = surplus - more
    return np.array(given)


def bell_draw(own_key, extent, scale, most, split=(), kind=jnp.bfloat16):
    factor_of = steps_of(own_key, extent, split, -0.22, 0.18) if split else 1.0
    values = jax.random.normal(own_key, extent, jnp.float32) * scale * factor_of
    return jnp.minimum(jnp.maximum(values, -most), most).astype(kind)


def setup_inputs(seed: int = 0) -> dict:
    keys = jax.random.split(jax.random.key(seed), 21)
    mixer_input = bell_draw(keys[0], (SEQUENCE_LENGTH, DI), 1.0, 6.0, ((0, 16), (1, 16)))
    mixer_gate = bell_draw(keys[1], (SEQUENCE_LENGTH, DI), 1.0, 6.0, ((0, 16), (1, 16)))
    step_low = draw_step_low(jax.random.fold_in(keys[20], 71), 0)
    step_proj = bell_draw(keys[3], (R, DI), R ** -0.5, 0.5, ((1, 16),))
    step_bias = jnp.clip(jax.random.uniform(keys[4], (DI,), jnp.float32, -1.0, 1.0) * steps_of(keys[4], (DI,), ((0, 16),), -0.4, 0.0), -1.0, 1.0)
    decay_rate = jnp.clip(jnp.exp(math.log(0.1) - 8.317766 * jax.random.uniform(keys[5], (NS, DI), jnp.float32) ** steps_of(keys[5], (NS, DI), ((1, 16),), -0.2, 0.2)), 2.441406286379788e-05, 0.1)
    input_coef = bell_draw(keys[6], (NS, SEQUENCE_LENGTH), 1.0, 6.0, ((1, 16),), jnp.float32)
    output_coef = bell_draw(keys[7], (NS, SEQUENCE_LENGTH), 0.1, 0.625, ((1, 16),), jnp.float32)
    conv_taps = bell_draw(keys[8], (KCONV, DI), 0.5, 3.0, ((1, 16),), jnp.float32)
    conv_bias = jnp.clip(jax.random.uniform(keys[9], (DI,), jnp.float32, -0.5, 0.5) * steps_of(keys[9], (DI,), ((0, 16),), -0.4, 0.0), -0.5, 0.5)
    skip_gain = jnp.clip(0.5 + 1.0 * jax.random.uniform(keys[10], (DI,), jnp.float32) ** steps_of(keys[10], (DI,), ((0, 16),), -0.2, 0.2), 0.5, 1.5)
    out_weight = bell_draw(keys[11], (DI, D), DI ** -0.5, 0.09375, ((0, 16),))
    residual = bell_draw(keys[12], (SEQUENCE_LENGTH, D), 1.0, 6.0, ((0, 256),))
    norm_gain = jnp.clip(1.0 + 0.1 * jax.random.normal(keys[13], (D,), jnp.float32), 0.5, 1.5)
    expert_ids_keys = jax.random.split(jax.random.fold_in(keys[14], 1), SEQUENCE_LENGTH // TOK_DEV)
    expert_ids_turns = jax.random.permutation(jax.random.fold_in(keys[14], 3), SEQUENCE_LENGTH // TOK_DEV)
    expert_ids = jax.vmap(lambda own, number: routed_block(jax.random.fold_in(keys[14], 2), own, number, TOK_DEV, EXPERTS, 2, CAP, 2))(expert_ids_keys, expert_ids_turns).reshape((SEQUENCE_LENGTH, 2))
    gate_scores = jnp.clip(0.1 + 0.9 * jax.random.uniform(keys[15], (SEQUENCE_LENGTH, 2), jnp.float32) ** steps_of(keys[15], (SEQUENCE_LENGTH, 2), ((0, 256),), -0.2, 0.2), 0.1, 1.0)
    gate_weight = bell_draw(keys[16], (EXPERTS, D, FFH), D ** -0.5, 0.125, ((0, 16), (2, 16)))
    up_weight = bell_draw(keys[17], (EXPERTS, D, FFH), D ** -0.5, 0.125, ((0, 16), (2, 16)))
    down_weight = bell_draw(keys[18], (EXPERTS, FFH, D), FFH ** -0.5, 0.046875, ((0, 16), (1, 16)))
    cotangent = bell_draw(keys[19], (SEQUENCE_LENGTH, D), 1.0, 6.0, ((0, 256),))
    return {"mixer_input": mixer_input, "mixer_gate": mixer_gate, "step_low": step_low, "step_proj": step_proj, "step_bias": step_bias, "decay_rate": decay_rate, "input_coef": input_coef, "output_coef": output_coef, "conv_taps": conv_taps, "conv_bias": conv_bias, "skip_gain": skip_gain, "out_weight": out_weight, "residual": residual, "norm_gain": norm_gain, "expert_ids": expert_ids, "gate_scores": gate_scores, "gate_weight": gate_weight, "up_weight": up_weight, "down_weight": down_weight, "cotangent": cotangent}


def mixer_ref(mixer_input, mixer_gate, step_low, step_proj, step_bias, decay_rate, input_coef, output_coef, conv_taps, conv_bias, skip_gain):
    length = mixer_input.shape[0]
    taps = conv_taps.shape[0]
    signal = mixer_input.astype(jnp.float32)
    padded = jnp.concatenate([jnp.zeros((taps - 1, signal.shape[1]), jnp.float32), signal], axis=0)
    filtered = conv_bias + conv_taps[0] * padded[0:length]
    for offset in range(1, taps):
        filtered = filtered + conv_taps[offset] * padded[offset:offset + length]
    inner = jax.nn.silu(filtered)
    step = jax.nn.softplus(jnp.dot(step_low, step_proj, preferred_element_type=jnp.float32) + step_bias)

    def advance(state, items):
        step_now, inner_now, coef_in, coef_out = items
        state = jnp.exp(-step_now[None, :] * decay_rate) * state + (step_now * inner_now)[None, :] * coef_in[:, None]
        return (state, lax.optimization_barrier(jnp.sum(coef_out[:, None] * state, axis=0)))
    start = jnp.zeros(decay_rate.shape, jnp.float32)
    _, readout = lax.scan(advance, start, (step, inner, jnp.transpose(input_coef), jnp.transpose(output_coef)))
    output = (readout + skip_gain * inner) * jax.nn.silu(mixer_gate.astype(jnp.float32))
    return output.astype(jnp.bfloat16)

def expert_pass(items):
    gate_mat, up_mat, down_mat, rows_x, rows_d = items
    gate_pre = jnp.dot(rows_x, gate_mat, preferred_element_type=jnp.float32)
    up_pre = jnp.dot(rows_x, up_mat, preferred_element_type=jnp.float32)
    activated = (jax.nn.silu(gate_pre) * up_pre).astype(jnp.bfloat16)
    out_rows = jnp.dot(activated, down_mat, preferred_element_type=jnp.float32).astype(jnp.bfloat16)
    grad_act = jnp.dot(rows_d, jnp.transpose(down_mat), preferred_element_type=jnp.float32)
    sigma = jax.nn.sigmoid(gate_pre)
    grad_gate = (grad_act * up_pre * sigma * (1.0 + gate_pre * (1.0 - sigma))).astype(jnp.bfloat16)
    grad_up = (grad_act * (gate_pre * sigma)).astype(jnp.bfloat16)
    in_rows = jnp.dot(grad_gate, jnp.transpose(gate_mat), preferred_element_type=jnp.float32)
    in_rows = in_rows + jnp.dot(grad_up, jnp.transpose(up_mat), preferred_element_type=jnp.float32)
    return (out_rows, in_rows.astype(jnp.bfloat16))

def reference(mixer_input, mixer_gate, step_low, step_proj, step_bias, decay_rate, input_coef, output_coef, conv_taps, conv_bias, skip_gain, out_weight, residual, norm_gain, expert_ids, gate_scores, gate_weight, up_weight, down_weight, cotangent):
    mixed = mixer_ref(mixer_input, mixer_gate, step_low, step_proj, step_bias, decay_rate, input_coef, output_coef, conv_taps, conv_bias, skip_gain)
    hidden = residual.astype(jnp.float32) + jnp.dot(mixed, out_weight, preferred_element_type=jnp.float32)
    scale = lax.rsqrt(lax.optimization_barrier(jnp.mean(hidden * hidden, axis=1, keepdims=True)) + 1e-05)
    normed = (hidden * scale * norm_gain).astype(jnp.bfloat16)
    experts = gate_weight.shape[0]
    width = hidden.shape[1]
    blocks = hidden.shape[0] // TOK_DEV
    choices = 2 * TOK_DEV
    ids = expert_ids.reshape(blocks, choices)
    member = (ids[:, :, None] == jnp.arange(experts, dtype=jnp.int32)[None, None, :]).astype(jnp.int32)
    before = jnp.cumsum(member, axis=1) - member
    slot = lax.optimization_barrier(jnp.sum(before * member, axis=2))
    target = ids * CAP + slot
    placing = (target[:, :, None] == jnp.arange(experts * CAP, dtype=jnp.int32)[None, None, :]).astype(jnp.float32)
    rows_norm = jnp.repeat(normed, 2, axis=0).astype(jnp.float32).reshape(blocks, choices, width)
    send_x = jnp.einsum('bas,bad->bsd', placing, rows_norm, precision=lax.Precision.HIGHEST).astype(jnp.bfloat16)
    outer = cotangent.astype(jnp.float32)
    grad_rows = (gate_scores[:, :, None] * outer[:, None, :]).astype(jnp.bfloat16)
    grad_rows = grad_rows.astype(jnp.float32).reshape(blocks, choices, width)
    send_d = jnp.einsum('bas,bad->bsd', placing, grad_rows, precision=lax.Precision.HIGHEST).astype(jnp.bfloat16)

    def by_expert(buffer):
        return jnp.transpose(buffer.reshape(blocks, experts, CAP, width), (1, 0, 2, 3)).reshape(experts, blocks * CAP, width)

    def by_block(buffer):
        return jnp.transpose(buffer.reshape(experts, blocks, CAP, width), (1, 0, 2, 3)).reshape(blocks, experts * CAP, width)
    out_all, in_all = lax.map(expert_pass, (gate_weight, up_weight, down_weight, by_expert(send_x), by_expert(send_d)))
    out_back = by_block(out_all).astype(jnp.float32)
    in_back = by_block(in_all).astype(jnp.float32)
    per_choice = jnp.einsum('bas,bsd->bad', placing, out_back, precision=lax.Precision.HIGHEST).reshape(-1, 2, width)
    grad_each = jnp.einsum('bas,bsd->bad', placing, in_back, precision=lax.Precision.HIGHEST).reshape(-1, 2, width)
    moe = lax.optimization_barrier(jnp.sum(gate_scores[:, :, None] * per_choice, axis=1))
    layer_out = (hidden + moe).astype(jnp.bfloat16)
    grad_scores = lax.optimization_barrier(jnp.sum(outer[:, None, :] * per_choice, axis=2))
    grad_normed = lax.optimization_barrier(jnp.sum(grad_each, axis=1))
    scaled = grad_normed * norm_gain
    grad_hidden = outer + scale * scaled - hidden * scale ** 3 * lax.optimization_barrier(jnp.mean(hidden * scaled, axis=1, keepdims=True))
    return (layer_out, grad_hidden, grad_scores)
```

```python
import jax
import jax.numpy as jnp
from jax import lax
from jax.sharding import PartitionSpec as P


def carried_in(value, axis, join, neutral):
    count, mine = (lax.axis_size(axis), lax.axis_index(axis))
    pieces = jax.tree.map(lambda part: lax.all_gather(part, axis), value)
    so_far = jax.tree.map(
        lambda part, zero: jnp.full_like(part, 0) + jnp.asarray(zero, part.dtype), value, neutral
    )

    def step(position, so_far):
        longer = join(so_far, jax.tree.map(lambda part: part[position], pieces))
        return jax.tree.map(lambda new, old: jnp.where(position < mine, new, old), longer, so_far)

    return lax.fori_loop(0, count - 1, step, so_far)


def affine_join(earlier, later):
    return (earlier[0] * later[0], earlier[1] * later[0] + later[1])


def carried(factor, offset):
    identity = (jnp.ones_like(factor), jnp.zeros_like(offset))
    return carried_in((factor, offset), "ctx", affine_join, identity)


def to_owner(slots):
    return lax.all_to_all(slots, "exp", split_axis=0, concat_axis=0, tiled=True)


def across_ctx(rows, kernel):
    return kernel(lax.all_gather(rows, "ctx", axis=0, tiled=True), jnp.int32(0))


def summed_ctx(kernel, count):
    return lax.psum_scatter(
        kernel(jnp.int32(0), lax.axis_size("ctx") * count), "ctx", scatter_dimension=0, tiled=True
    )


def contract_last(left, right):
    return lax.dot_general(
        left, right, (((1,), (1,)), ((), ())), preferred_element_type=jnp.float32
    )


def contract_first(left, right):
    return lax.dot_general(
        left, right, (((0,), (0,)), ((), ())), preferred_element_type=jnp.float32
    )


def gated_grads(gate_pre, up_pre, grad_act):
    sigma = jax.nn.sigmoid(gate_pre)
    grad_gate = (grad_act * up_pre * sigma * (1.0 + gate_pre * (1.0 - sigma))).astype(jnp.bfloat16)
    grad_up = (grad_act * (gate_pre * sigma)).astype(jnp.bfloat16)
    return (grad_gate, grad_up)


def mixer(
    mixer_input,
    mixer_gate,
    step_low,
    step_proj,
    step_bias,
    decay_rate,
    input_coef,
    output_coef,
    conv_taps,
    conv_bias,
    skip_gain,
):
    taps = conv_taps.shape[0]
    length = mixer_input.shape[0]
    signal = mixer_input.astype(jnp.float32)
    tail = signal[length - taps + 1 :]
    previous = carried(jnp.zeros_like(tail), tail)[1]
    padded = jnp.concatenate([previous, signal], axis=0)
    filtered = conv_bias + conv_taps[0] * padded[0:length]
    for offset in range(1, taps):
        filtered = filtered + conv_taps[offset] * padded[offset : offset + length]
    inner = jax.nn.silu(filtered)
    step = jax.nn.softplus(
        jnp.dot(step_low, step_proj, preferred_element_type=jnp.float32) + step_bias
    )
    factor = jnp.exp(-step[:, None, :] * decay_rate[None, :, :])
    drive = (step * inner)[:, None, :] * jnp.transpose(input_coef)[:, :, None]
    factor_cum, drive_cum = lax.associative_scan(affine_join, (factor, drive), axis=0)
    incoming = carried(factor_cum[length - 1], drive_cum[length - 1])[1]
    states = factor_cum * incoming[None] + drive_cum
    output = jnp.sum(states * jnp.transpose(output_coef)[:, :, None], axis=1) + skip_gain * inner
    output = output * jax.nn.silu(mixer_gate.astype(jnp.float32))
    return output.astype(jnp.bfloat16)


def per_device(
    mixer_input,
    mixer_gate,
    step_low,
    step_proj,
    step_bias,
    decay_rate,
    input_coef,
    output_coef,
    conv_taps,
    conv_bias,
    skip_gain,
    out_weight,
    residual,
    norm_gain,
    expert_ids,
    gate_scores,
    gate_weight,
    up_weight,
    down_weight,
    cotangent,
):
    mixed = mixer(
        mixer_input,
        mixer_gate,
        step_low,
        step_proj,
        step_bias,
        decay_rate,
        input_coef,
        output_coef,
        conv_taps,
        conv_bias,
        skip_gain,
    )
    tok_rows = residual.shape[0]
    width = residual.shape[1]
    hidden = residual.astype(jnp.float32) + lax.psum_scatter(
        jnp.dot(mixed, out_weight, preferred_element_type=jnp.float32),
        "exp",
        scatter_dimension=0,
        tiled=True,
    )
    scale = lax.rsqrt(jnp.mean(hidden * hidden, axis=1, keepdims=True) + 1e-05)
    normed = (hidden * scale * norm_gain).astype(jnp.bfloat16)
    experts = lax.axis_size("exp")
    capacity = 4 * tok_rows // experts
    slot_count = experts * capacity
    flat_ids = expert_ids.reshape(-1)
    choice = jnp.arange(flat_ids.shape[0], dtype=jnp.int32)
    same = (flat_ids[:, None] == flat_ids[None, :]) & (choice[None, :] < choice[:, None])
    slot = jnp.sum(same.astype(jnp.int32), axis=1)
    target = flat_ids * capacity + slot
    placing = (target[:, None] == jnp.arange(slot_count, dtype=jnp.int32)[None, :]).astype(
        jnp.bfloat16
    )
    send_x = contract_first(placing, jnp.repeat(normed, 2, axis=0)).astype(jnp.bfloat16)
    outer = cotangent.astype(jnp.float32)
    grad_rows = (
        (gate_scores[:, :, None] * outer[:, None, :]).reshape(-1, width).astype(jnp.bfloat16)
    )
    send_d = contract_first(placing, grad_rows).astype(jnp.bfloat16)
    gate_mat = gate_weight[0]
    up_mat = up_weight[0]
    down_mat = down_weight[0]
    units = gate_mat.shape[1]
    arrived = to_owner(send_x.reshape(experts, capacity, width)).reshape(slot_count, width)

    def pre_kernel(piece, start):
        return jnp.concatenate(
            [
                jnp.dot(piece, gate_mat, preferred_element_type=jnp.float32),
                jnp.dot(piece, up_mat, preferred_element_type=jnp.float32),
            ],
            axis=1,
        )

    gathered = across_ctx(arrived, pre_kernel)
    gate_pre = gathered[:, :units]
    up_pre = gathered[:, units:]
    activated = (jax.nn.silu(gate_pre) * up_pre).astype(jnp.bfloat16)

    def down_sums(start, count):
        return jnp.dot(activated, down_mat, preferred_element_type=jnp.float32)

    finished = summed_ctx(down_sums, slot_count).astype(jnp.bfloat16)
    expert_out = to_owner(finished.reshape(experts, capacity, width)).reshape(slot_count, width)
    arrived_grad = to_owner(send_d.reshape(experts, capacity, width)).reshape(slot_count, width)

    def back_kernel(piece, start):
        return contract_last(piece, down_mat)

    grad_act = across_ctx(arrived_grad, back_kernel)
    grad_gate, grad_up = gated_grads(gate_pre, up_pre, grad_act)

    def input_sums(start, count):
        return contract_last(grad_gate, gate_mat) + contract_last(grad_up, up_mat)

    grad_sent = summed_ctx(input_sums, slot_count).astype(jnp.bfloat16)
    grad_in = to_owner(grad_sent.reshape(experts, capacity, width)).reshape(slot_count, width)
    per_choice = jnp.dot(placing, expert_out, preferred_element_type=jnp.float32).reshape(
        tok_rows, 2, width
    )
    moe = jnp.sum(gate_scores[:, :, None] * per_choice, axis=1)
    layer_out = (hidden + moe).astype(jnp.bfloat16)
    grad_scores = jnp.sum(outer[:, None, :] * per_choice, axis=2)
    grad_normed = jnp.sum(
        jnp.dot(placing, grad_in, preferred_element_type=jnp.float32).reshape(tok_rows, 2, width),
        axis=1,
    )
    scaled = grad_normed * norm_gain
    grad_hidden = (
        outer
        + scale * scaled
        - hidden * scale**3 * jnp.mean(hidden * scaled, axis=1, keepdims=True)
    )
    return (layer_out, grad_hidden, grad_scores)


def solution(mesh):
    in_specs = (
        P("ctx", "exp"),
        P("ctx", "exp"),
        P("ctx", None),
        P(None, "exp"),
        P("exp"),
        P(None, "exp"),
        P(None, "ctx"),
        P(None, "ctx"),
        P(None, "exp"),
        P("exp"),
        P("exp"),
        P("exp", None),
        P(("ctx", "exp"), None),
        P(),
        P(("ctx", "exp"), None),
        P(("ctx", "exp"), None),
        P("exp", None, "ctx"),
        P("exp", None, "ctx"),
        P("exp", "ctx", None),
        P(("ctx", "exp"), None),
    )
    out_specs = (P(("ctx", "exp"), None), P(("ctx", "exp"), None), P(("ctx", "exp"), None))
    return jax.shard_map(
        per_device, mesh=mesh, in_specs=in_specs, out_specs=out_specs, check_vma=False
    )
```

```python
import jax
import jax.numpy as jnp
from jax import lax
from jax.experimental import pallas as pl
from jax.experimental.pallas import tpu as pltpu
from jax.sharding import Mesh
from jax.sharding import PartitionSpec as P

BF16 = jnp.bfloat16
F32 = jnp.float32
VMEM = pl.BlockSpec(memory_space=pltpu.VMEM)
SMEM = pl.BlockSpec(memory_space=pltpu.SMEM)
GROUP = 8


def contract_last(left, right):
    return lax.dot_general(left, right, (((1,), (1,)), ((), ())), preferred_element_type=F32)


def contract_first(left, right):
    return lax.dot_general(left, right, (((0,), (0,)), ((), ())), preferred_element_type=F32)


def local_state_body(
    x_ref, halo_ref, low_ref, proj_ref, bias_ref, decay_ref, bcoef_ref, taps_ref, cbias_ref,
    summary_ref, step_ref, inner_ref, pad_ref, drive_ref,
):
    length = x_ref.shape[0]
    taps = taps_ref.shape[0]
    halo = halo_ref.shape[0]
    pad_ref[0:halo] = halo_ref[...].astype(F32)
    pad_ref[halo:] = x_ref[...].astype(F32)
    filtered = cbias_ref[...]
    for k in range(taps):
        first = halo - taps + 1 + k
        filtered = filtered + taps_ref[k : k + 1] * pad_ref[first : first + length]
    inner = jax.nn.silu(filtered)
    inner_ref[...] = inner
    pre = jnp.dot(low_ref[...], proj_ref[...], preferred_element_type=F32) + bias_ref[...]
    step = jnp.maximum(pre, 0.0) + jnp.log1p(jnp.exp(-jnp.abs(pre)))
    step_ref[...] = step
    drive_ref[...] = step * inner
    rate = -decay_ref[...]
    shape = rate.shape

    def group(g, carry):
        state, coef = carry
        rows = pl.ds(pl.multiple_of(g * GROUP, GROUP), GROUP)
        steps = step_ref[rows]
        drives = drive_ref[rows]
        for k in range(GROUP):
            factor = jnp.exp(jnp.broadcast_to(steps[k : k + 1], shape) * rate)
            push = jnp.broadcast_to(drives[k : k + 1], shape) * jnp.broadcast_to(
                coef[:, k : k + 1], shape
            )
            state = factor * state + push
        return state, pltpu.roll(coef, coef.shape[1] - GROUP, 1)

    state, _ = lax.fori_loop(0, length // GROUP, group, (jnp.zeros(shape, F32), bcoef_ref[...]))
    count = shape[0]
    summary_ref[0:count] = state
    summary_ref[count:] = jnp.broadcast_to(
        jnp.sum(step, axis=0, keepdims=True), (summary_ref.shape[0] - count, shape[1])
    )


def readout_body(
    mine_ref, gathered_ref, decay_ref, bcoef_ref, ccoef_ref, step_ref, inner_ref, skip_ref,
    gate_ref, weight_ref, out_ref, drive_ref, read_ref,
):
    rate = -decay_ref[...]
    shape = rate.shape
    count = shape[0]
    length = step_ref.shape[0]
    block = gathered_ref.shape[1]
    mine = mine_ref[0]
    state = jnp.zeros(shape, F32)
    for c in range(gathered_ref.shape[0] - 1):
        total = gathered_ref[c, count : count + 1]
        longer = jnp.exp(jnp.broadcast_to(total, shape) * rate) * state + gathered_ref[c, 0:count]
        state = jnp.where(c < mine, longer, state)
    drive_ref[...] = step_ref[...] * inner_ref[...]

    def group(g, carry):
        state, bcoef, ccoef = carry
        rows = pl.ds(pl.multiple_of(g * GROUP, GROUP), GROUP)
        steps = step_ref[rows]
        drives = drive_ref[rows]
        reads = []
        for k in range(GROUP):
            factor = jnp.exp(jnp.broadcast_to(steps[k : k + 1], shape) * rate)
            push = jnp.broadcast_to(drives[k : k + 1], shape) * jnp.broadcast_to(
                bcoef[:, k : k + 1], shape
            )
            state = factor * state + push
            reads.append(
                jnp.sum(state * jnp.broadcast_to(ccoef[:, k : k + 1], shape), axis=0, keepdims=True)
            )
        read_ref[rows] = jnp.concatenate(reads, axis=0)
        turn = bcoef.shape[1] - GROUP
        return state, pltpu.roll(bcoef, turn, 1), pltpu.roll(ccoef, turn, 1)

    lax.fori_loop(0, length // GROUP, group, (state, bcoef_ref[...], ccoef_ref[...]))
    output = read_ref[...] + skip_ref[...] * inner_ref[...]
    output = output * jax.nn.silu(gate_ref[...].astype(F32))
    out_ref[...] = jnp.dot(
        output.astype(BF16), weight_ref[...], preferred_element_type=F32
    ).astype(BF16)


def gated_grads(gate_pre, up_pre, grad_act):
    sigma = jax.nn.sigmoid(gate_pre)
    grad_gate = (grad_act * up_pre * sigma * (1.0 + gate_pre * (1.0 - sigma))).astype(BF16)
    grad_up = (grad_act * (gate_pre * sigma)).astype(BF16)
    return (grad_gate, grad_up)


def make_per_device(interpret):
    def mixer_share(
        mixer_input, mixer_gate, step_low, step_proj, step_bias, decay_rate, input_coef,
        output_coef, conv_taps, conv_bias, skip_gain, out_weight,
    ):
        length, width = mixer_input.shape
        count = decay_rate.shape[0]
        halo = 8
        ranks = lax.axis_size("z") * lax.axis_size("core")
        tail = lax.ppermute(
            mixer_input[length - halo :], ("z", "core"), [(i, i + 1) for i in range(ranks - 1)]
        )
        sums = jax.ShapeDtypeStruct((count + 8, width), F32)
        rows = jax.ShapeDtypeStruct((length, width), F32)
        summary, step, inner = pl.pallas_call(
            local_state_body,
            out_shape=(sums, rows, rows),
            in_specs=[VMEM] * 9,
            out_specs=(VMEM, VMEM, VMEM),
            scratch_shapes=[pltpu.VMEM((length + halo, width), F32), pltpu.VMEM((length, width), F32)],
            interpret=interpret,
            name="local_state",
        )(
            mixer_input, tail, step_low, step_proj, step_bias[None], decay_rate, input_coef,
            conv_taps, conv_bias[None],
        )
        gathered = lax.all_gather(summary, ("z", "core"), axis=0)
        mine = lax.axis_index(("z", "core")).astype(jnp.int32).reshape(1)
        return pl.pallas_call(
            readout_body,
            out_shape=jax.ShapeDtypeStruct((length, out_weight.shape[1]), BF16),
            in_specs=[SMEM] + [VMEM] * 9,
            out_specs=VMEM,
            scratch_shapes=[pltpu.VMEM((length, width), F32), pltpu.VMEM((length, width), F32)],
            interpret=interpret,
            name="readout",
        )(
            mine, gathered, decay_rate, input_coef, output_coef, step, inner, skip_gain[None],
            mixer_gate, out_weight,
        )

    def per_device(
        mixer_input, mixer_gate, step_low, step_proj, step_bias, decay_rate, input_coef,
        output_coef, conv_taps, conv_bias, skip_gain, out_weight, residual, norm_gain,
        expert_ids, gate_scores, gate_weight, up_weight, down_weight, cotangent,
    ):
        tok_rows, width = residual.shape
        experts = lax.axis_size("exp")
        depth = lax.axis_size("z")
        capacity = 4 * tok_rows // experts
        slot_count = experts * capacity
        swap = [(0, 1), (1, 0)]

        def sibling(value):
            return lax.ppermute(value, "core", swap)

        def exchange(slots):
            return lax.all_to_all(slots, ("z", "exp"), split_axis=0, concat_axis=0, tiled=True)

        def to_all(rows):
            return exchange(jnp.broadcast_to(rows[None], (depth,) + rows.shape).reshape(-1, width))

        def from_all(rows):
            back = exchange(rows).reshape(depth, slot_count, width)
            return jnp.sum(back.astype(F32), axis=0).astype(BF16)

        flat_ids = expert_ids.reshape(-1)
        choice = jnp.arange(flat_ids.shape[0], dtype=jnp.int32)
        same = (flat_ids[:, None] == flat_ids[None, :]) & (choice[None, :] < choice[:, None])
        slot = jnp.sum(same.astype(jnp.int32), axis=1)
        target = flat_ids * capacity + slot
        placing = (target[:, None] == jnp.arange(slot_count, dtype=jnp.int32)[None, :]).astype(BF16)

        outer = cotangent.astype(F32)
        grad_rows = (gate_scores[:, :, None] * outer[:, None, :]).reshape(-1, width).astype(BF16)
        rows_d = to_all(contract_first(placing, grad_rows).astype(BF16))

        gates = (gate_weight[0], sibling(gate_weight[0]))
        ups = (up_weight[0], sibling(up_weight[0]))
        downs = (down_weight[0], sibling(down_weight[0]))

        share = mixer_share(
            mixer_input, mixer_gate, step_low, step_proj, step_bias, decay_rate, input_coef,
            output_coef, conv_taps, conv_bias, skip_gain, out_weight,
        )
        shares = lax.all_to_all(share, "exp", split_axis=0, concat_axis=0, tiled=True)
        shares = shares.reshape(experts, tok_rows, width).astype(F32)
        hidden = residual.astype(F32) + jnp.sum(shares, axis=0)
        scale = lax.rsqrt(jnp.mean(hidden * hidden, axis=1, keepdims=True) + 1e-05)
        normed = (hidden * scale * norm_gain).astype(BF16)
        rows_x = to_all(contract_first(placing, jnp.repeat(normed, 2, axis=0)).astype(BF16))

        grad_acts = [contract_last(rows_d, down) for down in downs]
        partial_out = 0.0
        grads = []
        for gate_mat, up_mat, down_mat, grad_act in zip(gates, ups, downs, grad_acts):
            gate_pre = jnp.dot(rows_x, gate_mat, preferred_element_type=F32)
            up_pre = jnp.dot(rows_x, up_mat, preferred_element_type=F32)
            activated = (jax.nn.silu(gate_pre) * up_pre).astype(BF16)
            grads.append(gated_grads(gate_pre, up_pre, grad_act))
            partial_out = partial_out + jnp.dot(activated, down_mat, preferred_element_type=F32)
        expert_out = from_all(partial_out.astype(BF16))
        partial_in = 0.0
        for gate_mat, up_mat, (grad_gate, grad_up) in zip(gates, ups, grads):
            partial_in = partial_in + contract_last(grad_gate, gate_mat)
            partial_in = partial_in + contract_last(grad_up, up_mat)
        grad_in = from_all(partial_in.astype(BF16))

        per_choice = jnp.dot(placing, expert_out, preferred_element_type=F32)
        per_choice = per_choice.reshape(tok_rows, 2, width)
        moe = jnp.sum(gate_scores[:, :, None] * per_choice, axis=1)
        layer_out = (hidden + moe).astype(BF16)
        grad_scores = jnp.sum(outer[:, None, :] * per_choice, axis=2)
        grad_normed = jnp.sum(
            jnp.dot(placing, grad_in, preferred_element_type=F32).reshape(tok_rows, 2, width),
            axis=1,
        )
        scaled = grad_normed * norm_gain
        grad_hidden = (
            outer
            + scale * scaled
            - hidden * scale**3 * jnp.mean(hidden * scaled, axis=1, keepdims=True)
        )
        return (layer_out, grad_hidden, grad_scores)

    return per_device


def solution(mesh, interpret=False):
    ctx, exp = mesh.devices.shape
    split = Mesh(mesh.devices.reshape(ctx // 2, 2, exp), ("z", "core", "exp"))
    both = ("z", "core")
    rows = P(("z", "core", "exp"), None)
    in_specs = (
        P(both, "exp"),
        P(both, "exp"),
        P(both, None),
        P(None, "exp"),
        P("exp"),
        P(None, "exp"),
        P(None, both),
        P(None, both),
        P(None, "exp"),
        P("exp"),
        P("exp"),
        P("exp", None),
        rows,
        P(),
        rows,
        rows,
        P("exp", None, both),
        P("exp", None, both),
        P("exp", both, None),
        rows,
    )
    return jax.shard_map(
        make_per_device(interpret),
        mesh=split,
        in_specs=in_specs,
        out_specs=(rows, rows, rows),
        check_vma=False,
    )
```

```python
from functools import partial

import jax
import jax.numpy as jnp
from jax import lax
from jax.experimental import pallas as pl
from jax.experimental.pallas import tpu as pltpu
from jax.sharding import Mesh
from jax.sharding import PartitionSpec as P

BF16 = jnp.bfloat16
F32 = jnp.float32
VMEM = pl.BlockSpec(memory_space=pltpu.VMEM)
SMEM = pl.BlockSpec(memory_space=pltpu.SMEM)
GROUP = 8
LANES = 128


def contract_last(left, right):
    return lax.dot_general(left, right, (((1,), (1,)), ((), ())), preferred_element_type=F32)


def contract_first(left, right):
    return lax.dot_general(left, right, (((0,), (0,)), ((), ())), preferred_element_type=F32)


def local_state_body(
    x_ref, halo_ref, low_ref, proj_ref, bias_ref, decay_ref, bcoef_ref, taps_ref, cbias_ref,
    summary_ref, step_ref, inner_ref, pad_ref, drive_ref,
):
    length = x_ref.shape[0]
    taps = taps_ref.shape[0]
    halo = halo_ref.shape[0]
    pad_ref[0:halo] = halo_ref[...].astype(F32)
    pad_ref[halo:] = x_ref[...].astype(F32)
    filtered = cbias_ref[...]
    for k in range(taps):
        first = halo - taps + 1 + k
        filtered = filtered + taps_ref[k : k + 1] * pad_ref[first : first + length]
    inner = jax.nn.silu(filtered)
    inner_ref[...] = inner
    pre = jnp.dot(low_ref[...], proj_ref[...], preferred_element_type=F32) + bias_ref[...]
    step = jnp.maximum(pre, 0.0) + jnp.log1p(jnp.exp(-jnp.abs(pre)))
    step_ref[...] = step
    drive_ref[...] = step * inner
    rate = -decay_ref[...]
    shape = rate.shape

    def group(g, carry):
        state, coef = carry
        rows = pl.ds(pl.multiple_of(g * GROUP, GROUP), GROUP)
        steps = step_ref[rows]
        drives = drive_ref[rows]
        for k in range(GROUP):
            factor = jnp.exp(jnp.broadcast_to(steps[k : k + 1], shape) * rate)
            push = jnp.broadcast_to(drives[k : k + 1], shape) * jnp.broadcast_to(
                coef[:, k : k + 1], shape
            )
            state = factor * state + push
        return state, pltpu.roll(coef, coef.shape[1] - GROUP, 1)

    state, _ = lax.fori_loop(0, length // GROUP, group, (jnp.zeros(shape, F32), bcoef_ref[...]))
    count = shape[0]
    summary_ref[0:count] = state
    summary_ref[count:] = jnp.broadcast_to(
        jnp.sum(step, axis=0, keepdims=True), (summary_ref.shape[0] - count, shape[1])
    )


def readout_body(
    mine_ref, gathered_ref, decay_ref, bcoef_ref, ccoef_ref, step_ref, inner_ref, skip_ref,
    gate_ref, weight_ref, out_ref, drive_ref, read_ref,
):
    rate = -decay_ref[...]
    shape = rate.shape
    count = shape[0]
    length = step_ref.shape[0]
    block = gathered_ref.shape[1]
    mine = mine_ref[0]
    state = jnp.zeros(shape, F32)
    for c in range(gathered_ref.shape[0] - 1):
        total = gathered_ref[c, count : count + 1]
        longer = jnp.exp(jnp.broadcast_to(total, shape) * rate) * state + gathered_ref[c, 0:count]
        state = jnp.where(c < mine, longer, state)
    drive_ref[...] = step_ref[...] * inner_ref[...]

    def group(g, carry):
        state, bcoef, ccoef = carry
        rows = pl.ds(pl.multiple_of(g * GROUP, GROUP), GROUP)
        steps = step_ref[rows]
        drives = drive_ref[rows]
        reads = []
        for k in range(GROUP):
            factor = jnp.exp(jnp.broadcast_to(steps[k : k + 1], shape) * rate)
            push = jnp.broadcast_to(drives[k : k + 1], shape) * jnp.broadcast_to(
                bcoef[:, k : k + 1], shape
            )
            state = factor * state + push
            reads.append(
                jnp.sum(state * jnp.broadcast_to(ccoef[:, k : k + 1], shape), axis=0, keepdims=True)
            )
        read_ref[rows] = jnp.concatenate(reads, axis=0)
        turn = bcoef.shape[1] - GROUP
        return state, pltpu.roll(bcoef, turn, 1), pltpu.roll(ccoef, turn, 1)

    lax.fori_loop(0, length // GROUP, group, (state, bcoef_ref[...], ccoef_ref[...]))
    output = read_ref[...] + skip_ref[...] * inner_ref[...]
    output = output * jax.nn.silu(gate_ref[...].astype(F32))
    out_ref[...] = jnp.dot(
        output.astype(BF16), weight_ref[...], preferred_element_type=F32
    ).astype(BF16)


def slot_maps(info, slots):
    lane = lax.broadcasted_iota(jnp.int32, (info.shape[0], slots), 1)
    block = lax.broadcasted_iota(jnp.int32, (info.shape[0], slots), 0) // GROUP
    maps = []
    for k in range(2):
        base = jnp.broadcast_to(info[:, k : k + 1].astype(jnp.int32), lane.shape)
        maps.append(jnp.where(lane == base + 2 * block, 1.0, 0.0))
    return maps


def prepare_body(ids_ref, scores_ref, cotangent_ref, rows_ref, info_ref, *, stride):
    shape = (cotangent_ref.shape[0], LANES)
    width = cotangent_ref.shape[1]
    row = lax.broadcasted_iota(jnp.int32, shape, 0)
    lane = lax.broadcasted_iota(jnp.int32, shape, 1)
    ids = [jnp.broadcast_to(ids_ref[:, k : k + 1], shape) for k in range(2)]
    fields = []
    for k in range(2):
        slot = jnp.zeros(shape, jnp.int32)
        for back in range(1, shape[0]):
            for other in ids:
                hit = (pltpu.roll(other, back, 0) == ids[k]) & (row >= back)
                slot = slot + hit.astype(jnp.int32)
        fields.append((stride * ids[k] + slot).astype(F32))
    for k in range(2):
        score = jnp.broadcast_to(scores_ref[:, k : k + 1], shape)
        high = score.astype(BF16).astype(F32)
        fields += [high, score - high]
    info = jnp.zeros(shape, F32)
    for place, field in enumerate(fields):
        info = jnp.where(lane == place, field, info)
    info = info.astype(BF16)
    info_ref[...] = info
    outer = cotangent_ref[...].astype(F32)
    for k in range(2):
        rows_ref[:, k * width : (k + 1) * width] = (scores_ref[:, k : k + 1] * outer).astype(BF16)
    rows_ref[:, 2 * width :] = info


def select_body(mine_ref, gathered_ref, rows_ref, *, stride):
    slots, width = rows_ref.shape
    tokens = gathered_ref.shape[0]
    info = gathered_ref[:, 2 * width :].astype(F32)
    lane = lax.broadcasted_iota(jnp.int32, (tokens, LANES), 1)
    block = lax.broadcasted_iota(jnp.int32, (tokens, LANES), 0) // GROUP
    rows = jnp.zeros((LANES, width), F32)
    for k in range(2):
        base = jnp.broadcast_to(info[:, k : k + 1].astype(jnp.int32), lane.shape)
        slot = base - stride * mine_ref[0]
        chosen = (slot >= 0) & (slot < 2) & (lane == slot + 2 * block)
        chosen = jnp.where(chosen, 1.0, 0.0).astype(BF16)
        rows = rows + contract_first(chosen, gathered_ref[:, k * width : (k + 1) * width])
    rows_ref[...] = rows[:slots].astype(BF16)


def norm_body(shares_ref, residual_ref, gain_ref, info_ref, hidden_ref, send_ref):
    width = residual_ref.shape[1]
    hidden = residual_ref[...].astype(F32)
    total = shares_ref[0].astype(F32)
    for c in range(1, shares_ref.shape[0]):
        total = total + shares_ref[c].astype(F32)
    hidden = hidden + total
    hidden_ref[...] = hidden
    scale = lax.rsqrt(jnp.mean(hidden * hidden, axis=1, keepdims=True) + 1e-05)
    normed = (hidden * scale * gain_ref[...]).astype(BF16)
    for c in range(send_ref.shape[0]):
        send_ref[c, :, 0:width] = normed
        send_ref[c, :, width:] = info_ref[...]


def pack_body(tokens_ref, slots_ref):
    slots, width = slots_ref.shape
    first, second = slot_maps(tokens_ref[:, width:].astype(F32), slots)
    slots_ref[...] = contract_first((first + second).astype(BF16), tokens_ref[:, 0:width]).astype(BF16)


def grad_act_body(rows_ref, own_ref, sib_ref, out_ref, *, depth):
    slots = rows_ref.shape[0]
    units = own_ref.shape[0]
    to = lax.broadcasted_iota(jnp.int32, (slots, slots), 0)
    source = lax.broadcasted_iota(jnp.int32, (slots, slots), 1)
    span = 2 * depth
    per_block = slots // depth
    wanted = ((to % span) // 2) * per_block + (to // span) * 2 + to % 2
    order = jnp.where(source == wanted, 1.0, 0.0).astype(BF16)
    rows = jnp.dot(order, rows_ref[...], preferred_element_type=F32).astype(BF16)
    out_ref[:, 0:units] = contract_last(rows, own_ref[...])
    out_ref[:, units:] = contract_last(rows, sib_ref[...])


def expert_body(
    rows_ref, grad_act_ref, gate_hbm, gate_sib_hbm, up_hbm, up_sib_hbm, down_hbm, down_sib_hbm,
    out_ref, gate_ref, up_ref, down_ref, gate_pre_ref, up_pre_ref, act_ref, grad_gate_ref,
    grad_up_ref, dots_ref, sems,
):
    width = rows_ref.shape[1]
    units = gate_ref.shape[2]
    slots = rows_ref.shape[0]
    copies = []
    order = (
        (gate_hbm, gate_ref, 0), (up_hbm, up_ref, 0), (gate_sib_hbm, gate_ref, 1),
        (up_sib_hbm, up_ref, 1), (down_hbm, down_ref, 0), (down_sib_hbm, down_ref, 1),
    )
    for index, (source, target, half) in enumerate(order):
        copies.append(pltpu.make_async_copy(source, target.at[half], sems.at[index]))
        copies[-1].start()
    rows = rows_ref[...]
    dots_ref[...] = jnp.zeros(dots_ref.shape, F32)
    tall = 16
    for half in range(2):
        copies[2 * half].wait()
        gate_pre_ref[...] = jnp.dot(rows, gate_ref[half], preferred_element_type=F32)
        copies[2 * half + 1].wait()
        up_pre_ref[...] = jnp.dot(rows, up_ref[half], preferred_element_type=F32)

        def chunk(r, carry):
            at = pl.ds(pl.multiple_of(r * tall, tall), tall)
            dots = dots_ref[at]
            for c in range(units // LANES):
                lanes = slice(c * LANES, (c + 1) * LANES)
                far = slice(half * units + c * LANES, half * units + (c + 1) * LANES)
                gate_pre = gate_pre_ref[at, lanes]
                up_pre = up_pre_ref[at, lanes]
                grad_act = grad_act_ref[at, far]
                sigma = jax.nn.sigmoid(gate_pre)
                gated = gate_pre * sigma
                act = (gated * up_pre).astype(BF16)
                act_ref[half, at, lanes] = act
                grad_gate_ref[half, at, lanes] = (
                    grad_act * up_pre * sigma * (1.0 + gate_pre * (1.0 - sigma))
                ).astype(BF16)
                grad_up_ref[half, at, lanes] = (grad_act * gated).astype(BF16)
                dots = dots + act.astype(F32) * grad_act
            dots_ref[at] = dots
            return carry

        lax.fori_loop(0, slots // tall, chunk, 0)
    copies[4].wait()
    share = jnp.dot(act_ref[0], down_ref[0], preferred_element_type=F32)
    copies[5].wait()
    share = share + jnp.dot(act_ref[1], down_ref[1], preferred_element_type=F32)
    out_ref[:, 0:width] = share.astype(BF16)
    share = contract_last(grad_gate_ref[0], gate_ref[0]) + contract_last(grad_up_ref[0], up_ref[0])
    share = share + contract_last(grad_gate_ref[1], gate_ref[1])
    share = share + contract_last(grad_up_ref[1], up_ref[1])
    out_ref[:, width : 2 * width] = share.astype(BF16)
    dots = jnp.broadcast_to(jnp.sum(dots_ref[...], axis=1, keepdims=True), (slots, LANES))
    high = dots.astype(BF16).astype(F32)
    lane = lax.broadcasted_iota(jnp.int32, (slots, LANES), 1)
    out_ref[:, 2 * width :] = jnp.where(lane == 0, high, dots - high).astype(BF16)


def combine_body(back_ref, tokens_ref, out_ref):
    slots = back_ref.shape[0]
    width = (back_ref.shape[1] - LANES) // 2
    info = tokens_ref[:, width:].astype(F32)
    first, second = slot_maps(info, slots)
    back = back_ref[:, 0:width]
    total = jnp.zeros((info.shape[0], width), F32)
    for part in range(2):
        weighted = first * info[:, 2 + part : 3 + part] + second * info[:, 4 + part : 5 + part]
        total = total + jnp.dot(weighted.astype(BF16), back, preferred_element_type=F32)
    out_ref[:, 0:width] = total.astype(BF16)
    both = (first + second).astype(BF16)
    out_ref[:, width : 2 * width] = jnp.dot(
        both, back_ref[:, width : 2 * width], preferred_element_type=F32
    ).astype(BF16)
    lane = lax.broadcasted_iota(jnp.int32, (info.shape[0], LANES), 1)
    for k, chosen in enumerate((first, second)):
        dots = jnp.dot(chosen.astype(BF16), back_ref[:, 2 * width :], preferred_element_type=F32)
        dots = jnp.broadcast_to(dots[:, 0:1] + dots[:, 1:2], dots.shape)
        high = dots.astype(BF16).astype(F32)
        start = 2 * width + k * LANES
        out_ref[:, start : start + LANES] = jnp.where(lane == 0, high, dots - high).astype(BF16)


def finish_body(
    back_ref, hidden_ref, gain_ref, cotangent_ref, scores_ref, layer_ref, grad_ref, dots_ref
):
    width = hidden_ref.shape[1]
    total = back_ref[0].astype(F32)
    for c in range(1, back_ref.shape[0]):
        total = total + back_ref[c].astype(F32)
    hidden = hidden_ref[...]
    layer_ref[...] = (hidden + total[:, 0:width]).astype(BF16)
    scale = lax.rsqrt(jnp.mean(hidden * hidden, axis=1, keepdims=True) + 1e-05)
    scaled = total[:, width : 2 * width] * gain_ref[...]
    outer = cotangent_ref[...].astype(F32)
    grad_ref[...] = (
        outer
        + scale * scaled
        - hidden * (scale * scale * scale) * jnp.mean(hidden * scaled, axis=1, keepdims=True)
    )
    for k in range(2):
        start = 2 * width + k * LANES
        dots = total[:, start : start + 1] + total[:, start + 1 : start + 2]
        dots_ref[:, k : k + 1] = dots / scores_ref[:, k : k + 1]


def make_per_device(interpret):
    def call(body, name, outs, ins, scratch=(), operands=(), **options):
        params = {}
        if options:
            body = partial(body, **options)
        return pl.pallas_call(
            body,
            out_shape=outs,
            in_specs=ins,
            out_specs=jax.tree.map(lambda _: VMEM, outs),
            scratch_shapes=list(scratch),
            interpret=interpret,
            name=name,
            compiler_params=pltpu.CompilerParams(vmem_limit_bytes=60 * 1024 * 1024),
            **params,
        )(*operands)

    def per_device(
        mixer_input, mixer_gate, step_low, step_proj, step_bias, decay_rate, input_coef,
        output_coef, conv_taps, conv_bias, skip_gain, out_weight, residual, norm_gain,
        expert_ids, gate_scores, gate_weight, up_weight, down_weight, cotangent,
    ):
        length, channels = mixer_input.shape
        count = decay_rate.shape[0]
        tok_rows, width = residual.shape
        units = gate_weight.shape[2]
        experts = lax.axis_size("exp")
        depth = lax.axis_size("z")
        ranks = depth * lax.axis_size("core")
        slots = 2 * experts * depth
        stride = 2 * depth
        swap = [(0, 1), (1, 0)]
        shape = jax.ShapeDtypeStruct

        def sibling(value):
            return lax.ppermute(value, "core", swap)

        def exchange(rows, axis):
            return lax.all_to_all(rows, axis, split_axis=0, concat_axis=0, tiled=True)

        grad_rows, info = call(
            prepare_body, "prepare",
            (shape((tok_rows, 2 * width + LANES), BF16), shape((tok_rows, LANES), BF16)),
            [VMEM] * 3, operands=(expert_ids, gate_scores, cotangent), stride=stride,
        )
        block_rows = lax.all_gather(grad_rows, "exp", axis=0, tiled=True)

        halo = 8
        tail = lax.ppermute(
            mixer_input[length - halo :], ("z", "core"), [(i, i + 1) for i in range(ranks - 1)]
        )
        gates = (gate_weight[0], sibling(gate_weight[0]))
        ups = (up_weight[0], sibling(up_weight[0]))
        downs = (down_weight[0], sibling(down_weight[0]))

        rows = shape((length, channels), F32)
        summary, step, inner = call(
            local_state_body, "local_state", (shape((count + 8, channels), F32), rows, rows),
            [VMEM] * 9,
            (pltpu.VMEM((length + halo, channels), F32), pltpu.VMEM((length, channels), F32)),
            (
                mixer_input, tail, step_low, step_proj, step_bias[None], decay_rate, input_coef,
                conv_taps, conv_bias[None],
            ),
        )
        gathered = lax.all_gather(summary, ("z", "core"), axis=0)
        mine = lax.axis_index(("z", "core")).astype(jnp.int32).reshape(1)
        share = call(
            readout_body, "readout", shape((length, width), BF16), [SMEM] + [VMEM] * 9,
            (pltpu.VMEM((length, channels), F32), pltpu.VMEM((length, channels), F32)),
            (
                mine, gathered, decay_rate, input_coef, output_coef, step, inner,
                skip_gain[None], mixer_gate, out_weight,
            ),
        )
        shares = exchange(share, "exp").reshape(experts, tok_rows, width)
        hidden, send = call(
            norm_body, "norm",
            (shape((tok_rows, width), F32), shape((depth, tok_rows, width + LANES), BF16)),
            [VMEM] * 4, operands=(shares, residual, norm_gain[None], info),
        )
        tokens = exchange(send.reshape(depth * tok_rows, width + LANES), "z")
        packed = call(pack_body, "pack", shape((slots, width), BF16), [VMEM], operands=(tokens,))
        rows_x = exchange(packed, "exp")

        expert = lax.axis_index("exp").astype(jnp.int32).reshape(1)
        chosen = call(
            select_body, "select", shape((2 * experts, width), BF16), [SMEM, VMEM],
            operands=(expert, block_rows), stride=stride,
        )
        rows_d = lax.all_gather(chosen, "z", axis=0, tiled=True)
        grad_act = call(
            grad_act_body, "grad_act", shape((slots, 2 * units), F32), [VMEM] * 3,
            operands=(rows_d,) + downs, depth=depth,
        )
        result = call(
            expert_body, "expert", shape((slots, 2 * width + LANES), BF16),
            [VMEM] * 2 + [pl.BlockSpec(memory_space=pl.ANY)] * 6,
            (
                pltpu.VMEM((2, width, units), BF16),
                pltpu.VMEM((2, width, units), BF16),
                pltpu.VMEM((2, units, width), BF16),
                pltpu.VMEM((slots, units), F32),
                pltpu.VMEM((slots, units), F32),
                pltpu.VMEM((2, slots, units), BF16),
                pltpu.VMEM((2, slots, units), BF16),
                pltpu.VMEM((2, slots, units), BF16),
                pltpu.VMEM((slots, LANES), F32),
                pltpu.SemaphoreType.DMA((6,)),
            ),
            (rows_x, grad_act) + gates + ups + downs,
        )
        back = exchange(result, "exp")
        shares_back = call(
            combine_body, "combine", shape((depth * tok_rows, 2 * width + 2 * LANES), BF16),
            [VMEM] * 2, operands=(back, tokens),
        )
        mine_back = exchange(shares_back, "z").reshape(depth, tok_rows, 2 * width + 2 * LANES)
        return call(
            finish_body, "finish",
            (
                shape((tok_rows, width), BF16), shape((tok_rows, width), F32),
                shape(gate_scores.shape, F32),
            ),
            [VMEM] * 5,
            operands=(mine_back, hidden, norm_gain[None], cotangent, gate_scores),
        )

    return per_device


def solution(mesh, interpret=False):
    ctx, exp = mesh.devices.shape
    split = Mesh(mesh.devices.reshape(ctx // 2, 2, exp), ("z", "core", "exp"))
    both = ("z", "core")
    rows = P(("z", "core", "exp"), None)
    in_specs = (
        P(both, "exp"),
        P(both, "exp"),
        P(both, None),
        P(None, "exp"),
        P("exp"),
        P(None, "exp"),
        P(None, both),
        P(None, both),
        P(None, "exp"),
        P("exp"),
        P("exp"),
        P("exp", None),
        rows,
        P(),
        rows,
        rows,
        P("exp", None, both),
        P("exp", None, both),
        P("exp", both, None),
        rows,
    )
    return jax.shard_map(
        make_per_device(interpret),
        mesh=split,
        in_specs=in_specs,
        out_specs=(rows, rows, rows),
        check_vma=False,
    )
```

```python
from functools import partial

import jax
import jax.numpy as jnp
from jax import lax
from jax.experimental import pallas as pl
from jax.experimental.pallas import tpu as pltpu
from jax.sharding import Mesh
from jax.sharding import PartitionSpec as P

BF16 = jnp.bfloat16
F32 = jnp.float32
VMEM = pl.BlockSpec(memory_space=pltpu.VMEM)
SMEM = pl.BlockSpec(memory_space=pltpu.SMEM)
GROUP = 8
LANES = 128


def contract_last(left, right):
    return lax.dot_general(left, right, (((1,), (1,)), ((), ())), preferred_element_type=F32)


def contract_first(left, right):
    return lax.dot_general(left, right, (((0,), (0,)), ((), ())), preferred_element_type=F32)


def column(row):
    count = row.shape[1]
    lane = lax.broadcasted_iota(jnp.int32, (count, count), 1)
    sub = lax.broadcasted_iota(jnp.int32, (count, count), 0)
    spread = jnp.where(lane == sub, jnp.broadcast_to(row, (count, count)), 0.0)
    return jnp.sum(spread, axis=1, keepdims=True)


def parts_of(value, count):
    parts = []
    for _ in range(count):
        part = value.astype(BF16).astype(F32)
        parts.append(part)
        value = value - part
    return parts


def advance(state, steps, drives, coef, rate, k):
    shape = rate.shape
    factor = jnp.exp(jnp.broadcast_to(steps[k : k + 1], shape) * rate)
    push = jnp.broadcast_to(drives[k : k + 1], shape) * jnp.broadcast_to(coef[:, k : k + 1], shape)
    return factor * state + push


def convolved(pad_ref, taps_ref, bias_ref, first, rows):
    taps = taps_ref.shape[0]
    filtered = bias_ref[...]
    for k in range(taps):
        start = first - taps + 1 + k
        filtered = filtered + taps_ref[k : k + 1] * pad_ref[start : start + rows]
    return jax.nn.silu(filtered)


def token_info(ids_ref, scores_ref, stride):
    rows = ids_ref.shape[1]
    shape = (rows, LANES)
    row = lax.broadcasted_iota(jnp.int32, shape, 0)
    lane = lax.broadcasted_iota(jnp.int32, shape, 1)
    ids = [jnp.broadcast_to(column(ids_ref[k : k + 1].astype(F32)), shape) for k in range(2)]
    fields = []
    for k in range(2):
        slot = jnp.zeros(shape, F32)
        for back in range(1, rows):
            for other in ids:
                hit = (pltpu.roll(other, back, 0) == ids[k]) & (row >= back)
                slot = slot + jnp.where(hit, 1.0, 0.0)
        fields.append(stride * ids[k] + slot)
    for k in range(2):
        fields += parts_of(jnp.broadcast_to(column(scores_ref[k : k + 1]), shape), 3)
    info = jnp.zeros(shape, F32)
    for place, field in enumerate(fields):
        info = jnp.where(lane == place, field, info)
    return info


def local_state_body(
    x_ref, low_ref, proj_ref, bias_ref, decay_ref, bcoef_ref, taps_ref, cbias_ref, ids_ref,
    scores_ref, cotangent_ref, late_ref, step_ref, inner_ref, extra_ref, pad_ref, drive_ref,
    *, stride,
):
    length, channels = x_ref.shape
    pad_ref[0:GROUP] = jnp.zeros((GROUP, channels), F32)
    pad_ref[GROUP:] = x_ref[...].astype(F32)
    inner = convolved(pad_ref, taps_ref, cbias_ref, GROUP, length)
    inner_ref[...] = inner
    pre = jnp.dot(low_ref[...], proj_ref[...], preferred_element_type=F32) + bias_ref[...]
    step = jnp.maximum(pre, 0.0) + jnp.log1p(jnp.exp(-jnp.abs(pre)))
    step_ref[...] = step
    drive_ref[...] = step * inner
    rate = -decay_ref[...]
    count = rate.shape[0]
    turn = bcoef_ref.shape[1] - GROUP

    def group(g, carry):
        state, coef = carry
        rows = pl.ds(pl.multiple_of(g * GROUP, GROUP), GROUP)
        steps = step_ref[rows]
        drives = drive_ref[rows]
        for k in range(GROUP):
            state = advance(state, steps, drives, coef, rate, k)
        return state, pltpu.roll(coef, turn, 1)

    first = (jnp.zeros(rate.shape, F32), pltpu.roll(bcoef_ref[...], turn, 1))
    state, _ = lax.fori_loop(1, length // GROUP, group, first)
    late_ref[0:count] = state
    late_ref[count:] = jnp.broadcast_to(
        jnp.sum(step[GROUP:], axis=0, keepdims=True), (GROUP, channels)
    )
    tokens = cotangent_ref.shape[0]
    info = token_info(ids_ref, scores_ref, stride)
    extra_ref[0:tokens, 0:LANES] = info.astype(BF16)
    extra_ref[0:tokens, LANES:] = jnp.zeros((tokens, channels - LANES), BF16)
    for b in range(cotangent_ref.shape[1] // channels):
        rows = slice((b + 1) * tokens, (b + 2) * tokens)
        extra_ref[rows] = cotangent_ref[:, b * channels : (b + 1) * channels]


def first_group_body(
    before_ref, x_ref, taps_ref, cbias_ref, step_ref, decay_ref, bcoef_ref, late_ref, extra_ref,
    send_ref, inner_ref, pad_ref,
):
    length = x_ref.shape[0]
    pad_ref[0:GROUP] = before_ref[length - GROUP :].astype(F32)
    pad_ref[GROUP:] = x_ref[0:GROUP].astype(F32)
    inner = convolved(pad_ref, taps_ref, cbias_ref, GROUP, GROUP)
    inner_ref[...] = inner
    steps = step_ref[0:GROUP]
    drives = steps * inner
    rate = -decay_ref[...]
    count = rate.shape[0]
    coef = bcoef_ref[...]
    state = jnp.zeros(rate.shape, F32)
    for k in range(GROUP):
        state = advance(state, steps, drives, coef, rate, k)
    after = late_ref[count : count + 1]
    state = jnp.exp(jnp.broadcast_to(after, rate.shape) * rate) * state + late_ref[0:count]
    high, low = parts_of(state, 2)
    send_ref[0:count] = high.astype(BF16)
    send_ref[count : 2 * count] = low.astype(BF16)
    total = jnp.broadcast_to(
        after + jnp.sum(steps, axis=0, keepdims=True), (GROUP, rate.shape[1])
    )
    high, low = parts_of(total, 2)
    sub = lax.broadcasted_iota(jnp.int32, total.shape, 0)
    total = jnp.where(sub == 0, high, low)
    extra = extra_ref[0:GROUP].astype(F32)
    send_ref[2 * count : 2 * count + 2 * GROUP] = jnp.concatenate([total, extra], 0).astype(BF16)
    send_ref[2 * count + 2 * GROUP :] = extra_ref[GROUP:]


def readout_body(
    mine_ref, gathered_ref, decay_ref, bcoef_ref, ccoef_ref, step_ref, inner_ref, first_ref,
    skip_ref, gate_ref, weight_ref, out_ref, info_ref, drive_ref, read_ref, inner_all_ref,
    tokens_ref,
):
    rate = -decay_ref[...]
    shape = rate.shape
    count, channels = shape
    length = step_ref.shape[0]
    ranks = gathered_ref.shape[0]
    mine = mine_ref[0]
    state = jnp.zeros(shape, F32)
    for c in range(ranks - 1):
        piece = gathered_ref[c, 0 : 2 * count].astype(F32)
        sums = gathered_ref[c, 2 * count : 2 * count + 2 * GROUP].astype(F32)
        total = jnp.broadcast_to(sums[0:1] + sums[1:2], shape)
        longer = jnp.exp(total * rate) * state + (piece[0:count] + piece[count:])
        state = jnp.where(c < mine, longer, state)
    inner_all_ref[...] = inner_ref[...]
    inner_all_ref[0:GROUP] = first_ref[...]
    drive_ref[...] = step_ref[...] * inner_all_ref[...]
    turn = bcoef_ref.shape[1] - GROUP

    def group(g, carry):
        state, bcoef, ccoef = carry
        rows = pl.ds(pl.multiple_of(g * GROUP, GROUP), GROUP)
        steps = step_ref[rows]
        drives = drive_ref[rows]
        reads = []
        for k in range(GROUP):
            state = advance(state, steps, drives, bcoef, rate, k)
            reads.append(
                jnp.sum(state * jnp.broadcast_to(ccoef[:, k : k + 1], shape), axis=0, keepdims=True)
            )
        read_ref[rows] = jnp.concatenate(reads, axis=0)
        return state, pltpu.roll(bcoef, turn, 1), pltpu.roll(ccoef, turn, 1)

    lax.fori_loop(0, length // GROUP, group, (state, bcoef_ref[...], ccoef_ref[...]))
    output = read_ref[...] + skip_ref[...] * inner_all_ref[...]
    output = output * jax.nn.silu(gate_ref[...].astype(F32))
    share = jnp.dot(output.astype(BF16), weight_ref[...], preferred_element_type=F32).astype(BF16)
    experts, tall, width = out_ref.shape
    rows = length // experts
    slots = tall - rows
    depth = slots // 2
    tokens = info_ref.shape[0] // depth
    core = lax.rem(mine, ranks // depth)
    start = 2 * count + GROUP
    for z in range(depth):
        at = slice(z * tokens, (z + 1) * tokens)
        place = z * (ranks // depth) + core
        extra = gathered_ref[place, 2 * count : 2 * count + 2 * GROUP].astype(F32)
        info_ref[at] = extra[GROUP:, 0:LANES]
        for b in range(width // channels):
            first = start + (b + 1) * tokens
            tokens_ref[at, b * channels : (b + 1) * channels] = gathered_ref[
                place, first : first + tokens
            ].astype(F32)
    info = info_ref[...]
    chosen = slot_maps(info, experts * slots)
    packed = jnp.zeros((experts * slots, width), F32)
    for k in range(2):
        at = 2 + 3 * k
        score = info[:, at : at + 1] + info[:, at + 1 : at + 2] + info[:, at + 2 : at + 3]
        grad_rows = (score * tokens_ref[...]).astype(BF16)
        packed = packed + contract_first(chosen[k].astype(BF16), grad_rows)
    packed = packed.astype(BF16)
    for e in range(experts):
        out_ref[e, 0:slots] = packed[e * slots : (e + 1) * slots]
        out_ref[e, slots:] = share[e * rows : (e + 1) * rows]


def slot_maps(info, slots):
    lane = lax.broadcasted_iota(jnp.int32, (info.shape[0], slots), 1)
    block = lax.broadcasted_iota(jnp.int32, (info.shape[0], slots), 0) // GROUP
    maps = []
    for k in range(2):
        base = jnp.broadcast_to(info[:, k : k + 1].astype(jnp.int32), lane.shape)
        maps.append(jnp.where(lane == base + 2 * block, 1.0, 0.0))
    return maps


def norm_body(shares_ref, residual_ref, gain_ref, hidden_ref, send_ref):
    rows = residual_ref.shape[0]
    start = shares_ref.shape[1] - rows
    total = shares_ref[0, start:].astype(F32)
    for c in range(1, shares_ref.shape[0]):
        total = total + shares_ref[c, start:].astype(F32)
    hidden = residual_ref[...].astype(F32) + total
    hidden_ref[...] = hidden
    scale = lax.rsqrt(jnp.mean(hidden * hidden, axis=1, keepdims=True) + 1e-05)
    normed = (hidden * scale * gain_ref[...]).astype(BF16)
    for c in range(send_ref.shape[0]):
        send_ref[c] = normed


def pack_body(tokens_ref, info_ref, slots_ref):
    first, second = slot_maps(info_ref[...], slots_ref.shape[0])
    slots_ref[...] = contract_first((first + second).astype(BF16), tokens_ref[...]).astype(BF16)


def grad_act_body(shares_ref, own_ref, sib_ref, out_ref, rows_ref):
    units = own_ref.shape[0]
    experts = shares_ref.shape[0]
    slots = rows_ref.shape[0] // experts
    for e in range(experts):
        rows_ref[e * slots : (e + 1) * slots] = shares_ref[e, 0:slots]
    rows = rows_ref[...]
    out_ref[:, 0:units] = contract_last(rows, own_ref[...])
    out_ref[:, units:] = contract_last(rows, sib_ref[...])


def expert_body(
    rows_ref, grad_act_ref, gate_hbm, gate_sib_hbm, up_hbm, up_sib_hbm, down_hbm, down_sib_hbm,
    out_ref, gate_ref, up_ref, down_ref, gate_pre_ref, up_pre_ref, act_ref, grad_gate_ref,
    grad_up_ref, dots_ref, sems,
):
    width = rows_ref.shape[1]
    units = gate_ref.shape[2]
    slots = rows_ref.shape[0]
    copies = []
    order = (
        (gate_hbm, gate_ref, 0), (up_hbm, up_ref, 0), (gate_sib_hbm, gate_ref, 1),
        (up_sib_hbm, up_ref, 1), (down_hbm, down_ref, 0), (down_sib_hbm, down_ref, 1),
    )
    for index, (source, target, half) in enumerate(order):
        copies.append(pltpu.make_async_copy(source, target.at[half], sems.at[index]))
        copies[-1].start()
    rows = rows_ref[...]
    dots_ref[...] = jnp.zeros(dots_ref.shape, F32)
    tall = 16
    for half in range(2):
        copies[2 * half].wait()
        gate_pre_ref[...] = jnp.dot(rows, gate_ref[half], preferred_element_type=F32)
        copies[2 * half + 1].wait()
        up_pre_ref[...] = jnp.dot(rows, up_ref[half], preferred_element_type=F32)

        def chunk(r, carry):
            at = pl.ds(pl.multiple_of(r * tall, tall), tall)
            dots = dots_ref[at]
            for c in range(units // LANES):
                lanes = slice(c * LANES, (c + 1) * LANES)
                far = slice(half * units + c * LANES, half * units + (c + 1) * LANES)
                gate_pre = gate_pre_ref[at, lanes]
                up_pre = up_pre_ref[at, lanes]
                grad_act = grad_act_ref[at, far]
                sigma = jax.nn.sigmoid(gate_pre)
                gated = gate_pre * sigma
                act = (gated * up_pre).astype(BF16)
                act_ref[half, at, lanes] = act
                grad_gate_ref[half, at, lanes] = (
                    grad_act * up_pre * sigma * (1.0 + gate_pre * (1.0 - sigma))
                ).astype(BF16)
                grad_up_ref[half, at, lanes] = (grad_act * gated).astype(BF16)
                dots = dots + act.astype(F32) * grad_act
            dots_ref[at] = dots
            return carry

        lax.fori_loop(0, slots // tall, chunk, 0)
    copies[4].wait()
    share = jnp.dot(act_ref[0], down_ref[0], preferred_element_type=F32)
    copies[5].wait()
    share = share + jnp.dot(act_ref[1], down_ref[1], preferred_element_type=F32)
    out_ref[:, 0:width] = share.astype(BF16)
    share = contract_last(grad_gate_ref[0], gate_ref[0]) + contract_last(grad_up_ref[0], up_ref[0])
    share = share + contract_last(grad_gate_ref[1], gate_ref[1])
    share = share + contract_last(grad_up_ref[1], up_ref[1])
    out_ref[:, width : 2 * width] = share.astype(BF16)
    dots = jnp.broadcast_to(jnp.sum(dots_ref[...], axis=1, keepdims=True), (slots, LANES))
    high = dots.astype(BF16).astype(F32)
    lane = lax.broadcasted_iota(jnp.int32, (slots, LANES), 1)
    out_ref[:, 2 * width :] = jnp.where(lane == 0, high, dots - high).astype(BF16)


def combine_body(back_ref, info_ref, out_ref):
    slots = back_ref.shape[0]
    width = (back_ref.shape[1] - LANES) // 2
    info = info_ref[...]
    tokens = info.shape[0]
    first, second = slot_maps(info, slots)
    weights = [
        first * info[:, 2 + part : 3 + part] + second * info[:, 5 + part : 6 + part]
        for part in range(2)
    ]
    total = jnp.dot(
        jnp.concatenate(weights, 0).astype(BF16), back_ref[:, 0:width], preferred_element_type=F32
    )
    out_ref[:, 0:width] = (total[0:tokens] + total[tokens:]).astype(BF16)
    both = (first + second).astype(BF16)
    out_ref[:, width : 2 * width] = jnp.dot(
        both, back_ref[:, width : 2 * width], preferred_element_type=F32
    ).astype(BF16)
    lane = lax.broadcasted_iota(jnp.int32, (tokens, LANES), 1)
    for k, chosen in enumerate((first, second)):
        dots = jnp.dot(chosen.astype(BF16), back_ref[:, 2 * width :], preferred_element_type=F32)
        dots = jnp.broadcast_to(dots[:, 0:1] + dots[:, 1:2], dots.shape)
        high = dots.astype(BF16).astype(F32)
        start = 2 * width + k * LANES
        out_ref[:, start : start + LANES] = jnp.where(lane == 0, high, dots - high).astype(BF16)


def finish_body(
    back_ref, hidden_ref, gain_ref, cotangent_ref, scores_ref, layer_ref, grad_ref, dots_ref
):
    rows, width = hidden_ref.shape
    total = back_ref[0].astype(F32)
    for c in range(1, back_ref.shape[0]):
        total = total + back_ref[c].astype(F32)
    hidden = hidden_ref[...]
    layer_ref[...] = (hidden + total[:, 0:width]).astype(BF16)
    scale = lax.rsqrt(jnp.mean(hidden * hidden, axis=1, keepdims=True) + 1e-05)
    scaled = total[:, width : 2 * width] * gain_ref[...]
    outer = cotangent_ref[...].astype(F32)
    grad_ref[...] = (
        outer
        + scale * scaled
        - hidden * (scale * scale * scale) * jnp.mean(hidden * scaled, axis=1, keepdims=True)
    )
    lane = lax.broadcasted_iota(jnp.int32, (rows, rows), 1)
    sub = lax.broadcasted_iota(jnp.int32, (rows, rows), 0)
    for k in range(2):
        start = 2 * width + k * LANES
        dots = total[:, start : start + 1] + total[:, start + 1 : start + 2]
        spread = jnp.where(lane == sub, jnp.broadcast_to(dots, lane.shape), 0.0)
        dots = jnp.sum(spread, axis=0, keepdims=True)
        dots_ref[k : k + 1] = dots / scores_ref[k : k + 1]


def make_per_device(interpret):
    def call(body, name, outs, ins, scratch=(), operands=(), **options):
        params = {}
        if options:
            body = partial(body, **options)
        return pl.pallas_call(
            body,
            out_shape=outs,
            in_specs=ins,
            out_specs=jax.tree.map(lambda _: VMEM, outs),
            scratch_shapes=list(scratch),
            interpret=interpret,
            name=name,
            compiler_params=pltpu.CompilerParams(vmem_limit_bytes=60 * 1024 * 1024),
            **params,
        )(*operands)

    def per_device(
        mixer_input, mixer_gate, step_low, step_proj, step_bias, decay_rate, input_coef,
        output_coef, conv_taps, conv_bias, skip_gain, out_weight, residual, norm_gain,
        expert_ids, gate_scores, gate_weight, up_weight, down_weight, cotangent,
    ):
        length, channels = mixer_input.shape
        count = decay_rate.shape[0]
        tok_rows, width = residual.shape
        units = gate_weight.shape[2]
        experts = lax.axis_size("exp")
        depth = lax.axis_size("z")
        ranks = depth * lax.axis_size("core")
        slots = 2 * experts * depth
        stride = 2 * depth
        swap = [(0, 1), (1, 0)]
        shape = jax.ShapeDtypeStruct

        def sibling(value):
            return lax.ppermute(value, "core", swap)

        def exchange(rows, axis):
            return lax.all_to_all(rows, axis, split_axis=0, concat_axis=0, tiled=True)

        before = lax.ppermute(mixer_input, ("z", "core"), [(i, i + 1) for i in range(ranks - 1)])
        gates = (gate_weight[0], sibling(gate_weight[0]))
        ups = (up_weight[0], sibling(up_weight[0]))
        downs = (down_weight[0], sibling(down_weight[0]))
        scores = gate_scores.T

        rows = shape((length, channels), F32)
        extra_rows = tok_rows * (1 + width // channels)
        late, step, inner, extra = call(
            local_state_body, "local_state",
            (
                shape((count + GROUP, channels), F32), rows, rows,
                shape((extra_rows, channels), BF16),
            ),
            [VMEM] * 11,
            (pltpu.VMEM((length + GROUP, channels), F32), pltpu.VMEM((length, channels), F32)),
            (
                mixer_input, step_low, step_proj, step_bias[None], decay_rate, input_coef,
                conv_taps, conv_bias[None], expert_ids.T, scores, cotangent,
            ),
            stride=stride,
        )
        summary, inner_first = call(
            first_group_body, "first_group",
            (
                shape((2 * count + GROUP + extra_rows, channels), BF16),
                shape((GROUP, channels), F32),
            ),
            [VMEM] * 9, (pltpu.VMEM((2 * GROUP, channels), F32),),
            (
                before, mixer_input, conv_taps, conv_bias[None], step, decay_rate, input_coef,
                late, extra,
            ),
        )
        gathered = lax.all_gather(summary, ("z", "core"), axis=0)
        mine = lax.axis_index(("z", "core")).astype(jnp.int32).reshape(1)
        tall = tok_rows + stride
        share, info = call(
            readout_body, "readout",
            (shape((experts, tall, width), BF16), shape((depth * tok_rows, LANES), F32)),
            [SMEM] + [VMEM] * 10,
            (
                pltpu.VMEM((length, channels), F32), pltpu.VMEM((length, channels), F32),
                pltpu.VMEM((length, channels), F32), pltpu.VMEM((depth * tok_rows, width), F32),
            ),
            (
                mine, gathered, decay_rate, input_coef, output_coef, step, inner, inner_first,
                skip_gain[None], mixer_gate, out_weight,
            ),
        )
        shares = exchange(share.reshape(experts * tall, width), "exp")
        shares = shares.reshape(experts, tall, width)
        hidden, send = call(
            norm_body, "norm",
            (shape((tok_rows, width), F32), shape((depth, tok_rows, width), BF16)),
            [VMEM] * 3, operands=(shares, residual, norm_gain[None]),
        )
        tokens = exchange(send.reshape(depth * tok_rows, width), "z")
        packed = call(
            pack_body, "pack", shape((slots, width), BF16), [VMEM] * 2, operands=(tokens, info)
        )
        rows_x = exchange(packed, "exp")
        grad_act = call(
            grad_act_body, "grad_act", shape((slots, 2 * units), F32), [VMEM] * 3,
            (pltpu.VMEM((slots, width), BF16),), (shares,) + downs,
        )
        result = call(
            expert_body, "expert", shape((slots, 2 * width + LANES), BF16),
            [VMEM] * 2 + [pl.BlockSpec(memory_space=pl.ANY)] * 6,
            (
                pltpu.VMEM((2, width, units), BF16),
                pltpu.VMEM((2, width, units), BF16),
                pltpu.VMEM((2, units, width), BF16),
                pltpu.VMEM((slots, units), F32),
                pltpu.VMEM((slots, units), F32),
                pltpu.VMEM((2, slots, units), BF16),
                pltpu.VMEM((2, slots, units), BF16),
                pltpu.VMEM((2, slots, units), BF16),
                pltpu.VMEM((slots, LANES), F32),
                pltpu.SemaphoreType.DMA((6,)),
            ),
            (rows_x, grad_act) + gates + ups + downs,
        )
        back = exchange(result, "exp")
        shares_back = call(
            combine_body, "combine", shape((depth * tok_rows, 2 * width + 2 * LANES), BF16),
            [VMEM] * 2, operands=(back, info),
        )
        mine_back = exchange(shares_back, "z").reshape(depth, tok_rows, 2 * width + 2 * LANES)
        layer_out, grad_hidden, dots = call(
            finish_body, "finish",
            (
                shape((tok_rows, width), BF16), shape((tok_rows, width), F32),
                shape(scores.shape, F32),
            ),
            [VMEM] * 5,
            operands=(mine_back, hidden, norm_gain[None], cotangent, scores),
        )
        return layer_out, grad_hidden, dots.T

    return per_device


def solution(mesh, interpret=False):
    ctx, exp = mesh.devices.shape
    split = Mesh(mesh.devices.reshape(ctx // 2, 2, exp), ("z", "core", "exp"))
    both = ("z", "core")
    rows = P(("z", "core", "exp"), None)
    in_specs = (
        P(both, "exp"),
        P(both, "exp"),
        P(both, None),
        P(None, "exp"),
        P("exp"),
        P(None, "exp"),
        P(None, both),
        P(None, both),
        P(None, "exp"),
        P("exp"),
        P("exp"),
        P("exp", None),
        rows,
        P(),
        rows,
        rows,
        P("exp", None, both),
        P("exp", None, both),
        P("exp", both, None),
        rows,
    )
    return jax.shard_map(
        make_per_device(interpret),
        mesh=split,
        in_specs=in_specs,
        out_specs=(rows, rows, rows),
        check_vma=False,
    )
```

```python
from functools import partial

import jax
import jax.numpy as jnp
from jax import lax
from jax.experimental import pallas as pl
from jax.experimental.pallas import tpu as pltpu
from jax.sharding import Mesh
from jax.sharding import PartitionSpec as P

BF16 = jnp.bfloat16
F32 = jnp.float32
VMEM = pl.BlockSpec(memory_space=pltpu.VMEM)
SMEM = pl.BlockSpec(memory_space=pltpu.SMEM)
ANY = pl.BlockSpec(memory_space=pl.ANY)
GROUP = 8
LANES = 128


def contract_last(left, right):
    return lax.dot_general(left, right, (((1,), (1,)), ((), ())), preferred_element_type=F32)


def contract_first(left, right):
    return lax.dot_general(left, right, (((0,), (0,)), ((), ())), preferred_element_type=F32)


def column(row):
    count = row.shape[1]
    lane = lax.broadcasted_iota(jnp.int32, (count, count), 1)
    sub = lax.broadcasted_iota(jnp.int32, (count, count), 0)
    spread = jnp.where(lane == sub, jnp.broadcast_to(row, (count, count)), 0.0)
    return jnp.sum(spread, axis=1, keepdims=True)


def parts_of(value, count):
    parts = []
    for _ in range(count):
        part = value.astype(BF16).astype(F32)
        parts.append(part)
        value = value - part
    return parts


def advance(state, steps, drives, coef, rate, k):
    shape = rate.shape
    factor = jnp.exp(jnp.broadcast_to(steps[k : k + 1], shape) * rate)
    push = jnp.broadcast_to(drives[k : k + 1], shape) * jnp.broadcast_to(coef[:, k : k + 1], shape)
    return factor * state + push


def convolved(pad_ref, taps_ref, bias_ref, first, rows):
    taps = taps_ref.shape[0]
    filtered = bias_ref[...]
    for k in range(taps):
        start = first - taps + 1 + k
        filtered = filtered + taps_ref[k : k + 1] * pad_ref[start : start + rows]
    return jax.nn.silu(filtered)


def token_info(ids_ref, scores_ref, stride):
    rows = ids_ref.shape[1]
    shape = (rows, LANES)
    row = lax.broadcasted_iota(jnp.int32, shape, 0)
    lane = lax.broadcasted_iota(jnp.int32, shape, 1)
    ids = [jnp.broadcast_to(column(ids_ref[k : k + 1].astype(F32)), shape) for k in range(2)]
    fields = []
    for k in range(2):
        slot = jnp.zeros(shape, F32)
        for back in range(1, rows):
            for other in ids:
                hit = (pltpu.roll(other, back, 0) == ids[k]) & (row >= back)
                slot = slot + jnp.where(hit, 1.0, 0.0)
        fields.append(stride * ids[k] + slot)
    for k in range(2):
        fields += parts_of(jnp.broadcast_to(column(scores_ref[k : k + 1]), shape), 3)
    info = jnp.zeros(shape, F32)
    for place, field in enumerate(fields):
        info = jnp.where(lane == place, field, info)
    return info


def local_state_body(
    x_ref, low_ref, proj_ref, bias_ref, decay_ref, bcoef_ref, taps_ref, cbias_ref, ids_ref,
    scores_ref, cotangent_ref, late_ref, step_ref, inner_ref, extra_ref, pad_ref, drive_ref,
    *, stride,
):
    length, channels = x_ref.shape
    pad_ref[0:GROUP] = jnp.zeros((GROUP, channels), F32)
    pad_ref[GROUP:] = x_ref[...].astype(F32)
    inner = convolved(pad_ref, taps_ref, cbias_ref, GROUP, length)
    inner_ref[...] = inner
    pre = jnp.dot(low_ref[...], proj_ref[...], preferred_element_type=F32) + bias_ref[...]
    step = jnp.maximum(pre, 0.0) + jnp.log1p(jnp.exp(-jnp.abs(pre)))
    step_ref[...] = step
    drive_ref[...] = step * inner
    rate = -decay_ref[...]
    count = rate.shape[0]
    turn = bcoef_ref.shape[1] - GROUP

    def group(g, carry):
        state, coef = carry
        rows = pl.ds(pl.multiple_of(g * GROUP, GROUP), GROUP)
        steps = step_ref[rows]
        drives = drive_ref[rows]
        for k in range(GROUP):
            state = advance(state, steps, drives, coef, rate, k)
        return state, pltpu.roll(coef, turn, 1)

    first = (jnp.zeros(rate.shape, F32), pltpu.roll(bcoef_ref[...], turn, 1))
    state, _ = lax.fori_loop(1, length // GROUP, group, first)
    late_ref[0:count] = state
    late_ref[count:] = jnp.broadcast_to(
        jnp.sum(step[GROUP:], axis=0, keepdims=True), (GROUP, channels)
    )
    tokens = cotangent_ref.shape[0]
    info = token_info(ids_ref, scores_ref, stride)
    extra_ref[0:tokens, 0:LANES] = info.astype(BF16)
    extra_ref[0:tokens, LANES:] = jnp.zeros((tokens, channels - LANES), BF16)
    for b in range(cotangent_ref.shape[1] // channels):
        rows = slice((b + 1) * tokens, (b + 2) * tokens)
        extra_ref[rows] = cotangent_ref[:, b * channels : (b + 1) * channels]


def first_group_body(
    before_ref, x_ref, taps_ref, cbias_ref, step_ref, decay_ref, bcoef_ref, late_ref, extra_ref,
    send_ref, inner_ref, pad_ref,
):
    length = x_ref.shape[0]
    pad_ref[0:GROUP] = before_ref[length - GROUP :].astype(F32)
    pad_ref[GROUP:] = x_ref[0:GROUP].astype(F32)
    inner = convolved(pad_ref, taps_ref, cbias_ref, GROUP, GROUP)
    inner_ref[...] = inner
    steps = step_ref[0:GROUP]
    drives = steps * inner
    rate = -decay_ref[...]
    count = rate.shape[0]
    coef = bcoef_ref[...]
    state = jnp.zeros(rate.shape, F32)
    for k in range(GROUP):
        state = advance(state, steps, drives, coef, rate, k)
    after = late_ref[count : count + 1]
    state = jnp.exp(jnp.broadcast_to(after, rate.shape) * rate) * state + late_ref[0:count]
    high, low = parts_of(state, 2)
    states = jnp.concatenate([high, low], 0).astype(BF16)
    total = jnp.broadcast_to(
        after + jnp.sum(steps, axis=0, keepdims=True), (GROUP, rate.shape[1])
    )
    high, low = parts_of(total, 2)
    sub = lax.broadcasted_iota(jnp.int32, total.shape, 0)
    total = jnp.where(sub == 0, high, low)
    extra = extra_ref[0:GROUP].astype(F32)
    sums = jnp.concatenate([total, extra], 0).astype(BF16)
    rest = extra_ref[GROUP:]
    for z in range(send_ref.shape[0]):
        send_ref[z, 0 : 2 * count] = states
        send_ref[z, 2 * count : 2 * count + 2 * GROUP] = sums
        send_ref[z, 2 * count + 2 * GROUP :] = rest


def readout_body(
    mine_ref, own_ref, sib_ref, decay_ref, bcoef_ref, ccoef_ref, step_ref, inner_ref, first_ref,
    skip_ref, gate_ref, weight_ref, out_ref, info_ref, drive_ref, read_ref, inner_all_ref,
    tokens_ref,
):
    rate = -decay_ref[...]
    shape = rate.shape
    count, channels = shape
    length = step_ref.shape[0]
    depth = own_ref.shape[0]
    mine = mine_ref[0]
    core = lax.rem(mine, 2)
    state = jnp.zeros(shape, F32)
    for z in range(depth):
        pair = []
        for ref in (own_ref, sib_ref):
            piece = ref[z, 0 : 2 * count].astype(F32)
            sums = ref[z, 2 * count : 2 * count + 2 * GROUP].astype(F32)
            total = jnp.broadcast_to(sums[0:1] + sums[1:2], shape)
            pair.append((jnp.exp(total * rate), piece[0:count] + piece[count:]))
        for k in range(2):
            factor = jnp.where(core == k, pair[0][0], pair[1][0])
            offset = jnp.where(core == k, pair[0][1], pair[1][1])
            state = jnp.where(2 * z + k < mine, factor * state + offset, state)
    inner_all_ref[...] = inner_ref[...]
    inner_all_ref[0:GROUP] = first_ref[...]
    drive_ref[...] = step_ref[...] * inner_all_ref[...]
    turn = bcoef_ref.shape[1] - GROUP

    def group(g, carry):
        state, bcoef, ccoef = carry
        rows = pl.ds(pl.multiple_of(g * GROUP, GROUP), GROUP)
        steps = step_ref[rows]
        drives = drive_ref[rows]
        reads = []
        for k in range(GROUP):
            state = advance(state, steps, drives, bcoef, rate, k)
            reads.append(
                jnp.sum(state * jnp.broadcast_to(ccoef[:, k : k + 1], shape), axis=0, keepdims=True)
            )
        read_ref[rows] = jnp.concatenate(reads, axis=0)
        return state, pltpu.roll(bcoef, turn, 1), pltpu.roll(ccoef, turn, 1)

    lax.fori_loop(0, length // GROUP, group, (state, bcoef_ref[...], ccoef_ref[...]))
    output = read_ref[...] + skip_ref[...] * inner_all_ref[...]
    output = output * jax.nn.silu(gate_ref[...].astype(F32))
    share = jnp.dot(output.astype(BF16), weight_ref[...], preferred_element_type=F32).astype(BF16)
    experts, tall, width = out_ref.shape
    rows = length // experts
    slots = tall - rows
    tokens = info_ref.shape[0] // depth
    start = 2 * count + GROUP
    for z in range(depth):
        at = slice(z * tokens, (z + 1) * tokens)
        extra = own_ref[z, 2 * count : 2 * count + 2 * GROUP].astype(F32)
        info_ref[at] = extra[GROUP:, 0:LANES]
        for b in range(width // channels):
            first = start + (b + 1) * tokens
            tokens_ref[at, b * channels : (b + 1) * channels] = own_ref[
                z, first : first + tokens
            ].astype(F32)
    info = info_ref[...]
    chosen = slot_maps(info, experts * slots)
    packed = jnp.zeros((experts * slots, width), F32)
    for k in range(2):
        at = 2 + 3 * k
        score = info[:, at : at + 1] + info[:, at + 1 : at + 2] + info[:, at + 2 : at + 3]
        grad_rows = (score * tokens_ref[...]).astype(BF16)
        packed = packed + contract_first(chosen[k].astype(BF16), grad_rows)
    packed = packed.astype(BF16)
    for e in range(experts):
        out_ref[e, 0:slots] = packed[e * slots : (e + 1) * slots]
        out_ref[e, slots:] = share[e * rows : (e + 1) * rows]


def slot_maps(info, slots):
    lane = lax.broadcasted_iota(jnp.int32, (info.shape[0], slots), 1)
    block = lax.broadcasted_iota(jnp.int32, (info.shape[0], slots), 0) // GROUP
    maps = []
    for k in range(2):
        base = jnp.broadcast_to(info[:, k : k + 1].astype(jnp.int32), lane.shape)
        maps.append(jnp.where(lane == base + 2 * block, 1.0, 0.0))
    return maps


def norm_body(shares_hbm, residual_ref, gain_ref, hidden_ref, send_ref, shares_ref, sem):
    rows = residual_ref.shape[0]
    start = shares_hbm.shape[1] - rows
    copy = pltpu.make_async_copy(shares_hbm.at[:, start : start + rows], shares_ref, sem)
    copy.start()
    copy.wait()
    total = shares_ref[0].astype(F32)
    for c in range(1, shares_ref.shape[0]):
        total = total + shares_ref[c].astype(F32)
    hidden = residual_ref[...].astype(F32) + total
    hidden_ref[...] = hidden
    scale = lax.rsqrt(jnp.mean(hidden * hidden, axis=1, keepdims=True) + 1e-05)
    normed = (hidden * scale * gain_ref[...]).astype(BF16)
    for c in range(send_ref.shape[0]):
        send_ref[c] = normed


def pack_body(tokens_ref, info_ref, slots_ref):
    first, second = slot_maps(info_ref[...], slots_ref.shape[0])
    slots_ref[...] = contract_first((first + second).astype(BF16), tokens_ref[...]).astype(BF16)


def grad_act_body(shares_hbm, own_hbm, sib_hbm, out_hbm, rows_ref, down_ref, out_ref, sems):
    experts, slots, width = rows_ref.shape
    units = down_ref.shape[1]
    copies = [
        pltpu.make_async_copy(shares_hbm.at[:, 0:slots], rows_ref, sems.at[0]),
        pltpu.make_async_copy(own_hbm, down_ref.at[0], sems.at[1]),
        pltpu.make_async_copy(sib_hbm, down_ref.at[1], sems.at[2]),
    ]
    for copy in copies:
        copy.start()
    copies[0].wait()
    rows = rows_ref[...].reshape(experts * slots, width)
    sends = []
    for half in range(2):
        copies[1 + half].wait()
        out_ref[half] = contract_last(rows, down_ref[half])
        sends.append(pltpu.make_async_copy(out_ref.at[half], out_hbm.at[half], sems.at[3 + half]))
        sends[-1].start()
    for send in sends:
        send.wait()


def expert_body(
    rows_hbm, grad_act_hbm, gate_hbm, gate_sib_hbm, up_hbm, up_sib_hbm, down_hbm, down_sib_hbm,
    out_hbm, rows_ref, grad_act_ref, gate_ref, up_ref, down_ref, gate_pre_ref, up_pre_ref, act_ref,
    grad_gate_ref, grad_up_ref, dots_ref, out_ref, sems, out_sems,
):
    slots, width = rows_ref.shape
    units = gate_ref.shape[2]
    half_width = width // 2
    plan = (
        ("rows", rows_hbm, rows_ref),
        ("gate_top", gate_hbm.at[0:half_width], gate_ref.at[0, 0:half_width]),
        ("gate_end", gate_hbm.at[half_width:width], gate_ref.at[0, half_width:width]),
        ("up0", up_hbm, up_ref.at[0]),
        ("grad_act", grad_act_hbm, grad_act_ref),
        ("gate1", gate_sib_hbm, gate_ref.at[1]),
        ("up1", up_sib_hbm, up_ref.at[1]),
        ("down0", down_hbm, down_ref.at[0]),
        ("down1", down_sib_hbm, down_ref.at[1]),
    )
    copies = {}
    for index, (name, source, target) in enumerate(plan):
        copies[name] = pltpu.make_async_copy(source, target, sems.at[index])
        copies[name].start()
    dots_ref[...] = jnp.zeros(dots_ref.shape, F32)
    tall = 16
    copies["rows"].wait()
    rows = rows_ref[...]
    for half in range(2):
        if half == 0:
            copies["gate_top"].wait()
            top = jnp.dot(
                rows[:, 0:half_width], gate_ref[0, 0:half_width], preferred_element_type=F32
            )
            copies["gate_end"].wait()
            gate_pre_ref[...] = top + jnp.dot(
                rows[:, half_width:], gate_ref[0, half_width:], preferred_element_type=F32
            )
            copies["up0"].wait()
            up_pre_ref[...] = jnp.dot(rows, up_ref[0], preferred_element_type=F32)
            copies["grad_act"].wait()
        else:
            copies["gate1"].wait()
            gate_pre_ref[...] = jnp.dot(rows, gate_ref[1], preferred_element_type=F32)
            copies["up1"].wait()
            up_pre_ref[...] = jnp.dot(rows, up_ref[1], preferred_element_type=F32)

        def chunk(r, carry):
            at = pl.ds(pl.multiple_of(r * tall, tall), tall)
            dots = dots_ref[at]
            for c in range(units // LANES):
                lanes = slice(c * LANES, (c + 1) * LANES)
                gate_pre = gate_pre_ref[at, lanes]
                up_pre = up_pre_ref[at, lanes]
                grad_act = grad_act_ref[half, at, lanes]
                sigma = jax.nn.sigmoid(gate_pre)
                gated = gate_pre * sigma
                act = (gated * up_pre).astype(BF16)
                act_ref[half, at, lanes] = act
                grad_gate_ref[half, at, lanes] = (
                    grad_act * up_pre * sigma * (1.0 + gate_pre * (1.0 - sigma))
                ).astype(BF16)
                grad_up_ref[half, at, lanes] = (grad_act * gated).astype(BF16)
                dots = dots + act.astype(F32) * grad_act
            dots_ref[at] = dots
            return carry

        lax.fori_loop(0, slots // tall, chunk, 0)
    sends = []

    def send(first, last):
        piece = pltpu.make_async_copy(
            out_ref.at[:, first:last], out_hbm.at[:, first:last], out_sems.at[len(sends)]
        )
        piece.start()
        sends.append(piece)

    dots = jnp.broadcast_to(jnp.sum(dots_ref[...], axis=1, keepdims=True), (slots, LANES))
    high = dots.astype(BF16).astype(F32)
    lane = lax.broadcasted_iota(jnp.int32, (slots, LANES), 1)
    out_ref[:, 2 * width :] = jnp.where(lane == 0, high, dots - high).astype(BF16)
    send(2 * width, 2 * width + LANES)
    copies["down0"].wait()
    share = jnp.dot(act_ref[0], down_ref[0], preferred_element_type=F32)
    copies["down1"].wait()
    share = share + jnp.dot(act_ref[1], down_ref[1], preferred_element_type=F32)
    out_ref[:, 0:width] = share.astype(BF16)
    send(0, width)
    for part in range(2):
        at = slice(part * half_width, (part + 1) * half_width)
        share = contract_last(grad_gate_ref[0], gate_ref[0, at])
        share = share + contract_last(grad_up_ref[0], up_ref[0, at])
        share = share + contract_last(grad_gate_ref[1], gate_ref[1, at])
        share = share + contract_last(grad_up_ref[1], up_ref[1, at])
        first = width + part * half_width
        out_ref[:, first : first + half_width] = share.astype(BF16)
        send(first, first + half_width)
    for piece in sends:
        piece.wait()


def combine_body(back_ref, info_ref, out_ref):
    slots = back_ref.shape[0]
    width = (back_ref.shape[1] - LANES) // 2
    info = info_ref[...]
    tokens = info.shape[0]
    first, second = slot_maps(info, slots)
    weights = [
        first * info[:, 2 + part : 3 + part] + second * info[:, 5 + part : 6 + part]
        for part in range(2)
    ]
    total = jnp.dot(
        jnp.concatenate(weights, 0).astype(BF16), back_ref[:, 0:width], preferred_element_type=F32
    )
    out_ref[:, 0:width] = (total[0:tokens] + total[tokens:]).astype(BF16)
    both = (first + second).astype(BF16)
    out_ref[:, width : 2 * width] = jnp.dot(
        both, back_ref[:, width : 2 * width], preferred_element_type=F32
    ).astype(BF16)
    lane = lax.broadcasted_iota(jnp.int32, (tokens, LANES), 1)
    for k, chosen in enumerate((first, second)):
        dots = jnp.dot(chosen.astype(BF16), back_ref[:, 2 * width :], preferred_element_type=F32)
        dots = jnp.broadcast_to(dots[:, 0:1] + dots[:, 1:2], dots.shape)
        high = dots.astype(BF16).astype(F32)
        start = 2 * width + k * LANES
        out_ref[:, start : start + LANES] = jnp.where(lane == 0, high, dots - high).astype(BF16)


def finish_body(
    back_ref, hidden_ref, gain_ref, cotangent_ref, scores_ref, layer_ref, grad_ref, dots_ref
):
    rows, width = hidden_ref.shape
    total = back_ref[0].astype(F32)
    for c in range(1, back_ref.shape[0]):
        total = total + back_ref[c].astype(F32)
    hidden = hidden_ref[...]
    layer_ref[...] = (hidden + total[:, 0:width]).astype(BF16)
    scale = lax.rsqrt(jnp.mean(hidden * hidden, axis=1, keepdims=True) + 1e-05)
    scaled = total[:, width : 2 * width] * gain_ref[...]
    outer = cotangent_ref[...].astype(F32)
    grad_ref[...] = (
        outer
        + scale * scaled
        - hidden * (scale * scale * scale) * jnp.mean(hidden * scaled, axis=1, keepdims=True)
    )
    lane = lax.broadcasted_iota(jnp.int32, (rows, rows), 1)
    sub = lax.broadcasted_iota(jnp.int32, (rows, rows), 0)
    for k in range(2):
        start = 2 * width + k * LANES
        dots = total[:, start : start + 1] + total[:, start + 1 : start + 2]
        spread = jnp.where(lane == sub, jnp.broadcast_to(dots, lane.shape), 0.0)
        dots = jnp.sum(spread, axis=0, keepdims=True)
        dots_ref[k : k + 1] = dots / scores_ref[k : k + 1]


def make_per_device(interpret):
    def call(body, name, outs, ins, scratch=(), operands=(), out_spec=VMEM, **options):
        if options:
            body = partial(body, **options)
        return pl.pallas_call(
            body,
            out_shape=outs,
            in_specs=ins,
            out_specs=jax.tree.map(lambda _: out_spec, outs),
            scratch_shapes=list(scratch),
            interpret=interpret,
            name=name,
            compiler_params=pltpu.CompilerParams(vmem_limit_bytes=60 * 1024 * 1024),
        )(*operands)

    def per_device(
        mixer_input, mixer_gate, step_low, step_proj, step_bias, decay_rate, input_coef,
        output_coef, conv_taps, conv_bias, skip_gain, out_weight, residual, norm_gain,
        expert_ids, gate_scores, gate_weight, up_weight, down_weight, cotangent,
    ):
        length, channels = mixer_input.shape
        count = decay_rate.shape[0]
        tok_rows, width = residual.shape
        units = gate_weight.shape[2]
        experts = lax.axis_size("exp")
        depth = lax.axis_size("z")
        ranks = depth * lax.axis_size("core")
        slots = 2 * experts * depth
        stride = 2 * depth
        swap = [(0, 1), (1, 0)]
        shape = jax.ShapeDtypeStruct

        def sibling(value):
            return lax.ppermute(value, "core", swap)

        def exchange(rows, axis):
            return lax.all_to_all(rows, axis, split_axis=0, concat_axis=0, tiled=True)

        before = lax.ppermute(mixer_input, ("z", "core"), [(i, i + 1) for i in range(ranks - 1)])
        scores = gate_scores.T

        rows = shape((length, channels), F32)
        extra_rows = tok_rows * (1 + width // channels)
        late, step, inner, extra = call(
            local_state_body, "local_state",
            (
                shape((count + GROUP, channels), F32), rows, rows,
                shape((extra_rows, channels), BF16),
            ),
            [VMEM] * 11,
            (pltpu.VMEM((length + GROUP, channels), F32), pltpu.VMEM((length, channels), F32)),
            (
                mixer_input, step_low, step_proj, step_bias[None], decay_rate, input_coef,
                conv_taps, conv_bias[None], expert_ids.T, scores, cotangent,
            ),
            stride=stride,
        )
        summary, inner_first = call(
            first_group_body, "first_group",
            (
                shape((depth, 2 * count + GROUP + extra_rows, channels), BF16),
                shape((GROUP, channels), F32),
            ),
            [VMEM] * 9, (pltpu.VMEM((2 * GROUP, channels), F32),),
            (
                before, mixer_input, conv_taps, conv_bias[None], step, decay_rate, input_coef,
                late, extra,
            ),
        )
        tall = summary.shape[1]
        gathered = exchange(summary.reshape(depth * tall, channels), "z")
        gathered_sib = sibling(gathered)
        gathered_sib, gate_sent, up_sent, down_sent = lax.optimization_barrier(
            (gathered_sib, gate_weight[0], up_weight[0], down_weight[0])
        )
        gates = (gate_weight[0], sibling(gate_sent))
        ups = (up_weight[0], sibling(up_sent))
        downs = (down_weight[0], sibling(down_sent))
        mine = lax.axis_index(("z", "core")).astype(jnp.int32).reshape(1)
        tall = tok_rows + stride
        share, info = call(
            readout_body, "readout",
            (shape((experts, tall, width), BF16), shape((depth * tok_rows, LANES), F32)),
            [SMEM] + [VMEM] * 11,
            (
                pltpu.VMEM((length, channels), F32), pltpu.VMEM((length, channels), F32),
                pltpu.VMEM((length, channels), F32), pltpu.VMEM((depth * tok_rows, width), F32),
            ),
            (
                mine, gathered.reshape(summary.shape), gathered_sib.reshape(summary.shape),
                decay_rate, input_coef, output_coef, step, inner, inner_first,
                skip_gain[None], mixer_gate, out_weight,
            ),
        )
        shares = exchange(share.reshape(experts * tall, width), "exp")
        shares = shares.reshape(experts, tall, width)
        hidden, send = call(
            norm_body, "norm",
            (shape((tok_rows, width), F32), shape((depth, tok_rows, width), BF16)),
            [ANY] + [VMEM] * 2,
            (pltpu.VMEM((experts, tok_rows, width), BF16), pltpu.SemaphoreType.DMA(())),
            (shares, residual, norm_gain[None]),
        )
        tokens = exchange(send.reshape(depth * tok_rows, width), "z")
        packed = call(
            pack_body, "pack", shape((slots, width), BF16), [VMEM] * 2, operands=(tokens, info)
        )
        rows_x = exchange(packed, "exp")
        grad_act = call(
            grad_act_body, "grad_act", shape((2, slots, units), F32), [ANY] * 3,
            (
                pltpu.VMEM((experts, stride, width), BF16),
                pltpu.VMEM((2, units, width), BF16),
                pltpu.VMEM((2, slots, units), F32),
                pltpu.SemaphoreType.DMA((5,)),
            ),
            (shares,) + downs,
            ANY,
        )
        result = call(
            expert_body, "expert", shape((slots, 2 * width + LANES), BF16),
            [ANY] * 8,
            (
                pltpu.VMEM((slots, width), BF16),
                pltpu.VMEM((2, slots, units), F32),
                pltpu.VMEM((2, width, units), BF16),
                pltpu.VMEM((2, width, units), BF16),
                pltpu.VMEM((2, units, width), BF16),
                pltpu.VMEM((slots, units), F32),
                pltpu.VMEM((slots, units), F32),
                pltpu.VMEM((2, slots, units), BF16),
                pltpu.VMEM((2, slots, units), BF16),
                pltpu.VMEM((2, slots, units), BF16),
                pltpu.VMEM((slots, LANES), F32),
                pltpu.VMEM((slots, 2 * width + LANES), BF16),
                pltpu.SemaphoreType.DMA((9,)),
                pltpu.SemaphoreType.DMA((4,)),
            ),
            (rows_x, grad_act) + gates + ups + downs,
            ANY,
        )
        back = exchange(result, "exp")
        shares_back = call(
            combine_body, "combine", shape((depth * tok_rows, 2 * width + 2 * LANES), BF16),
            [VMEM] * 2, operands=(back, info),
        )
        mine_back = exchange(shares_back, "z").reshape(depth, tok_rows, 2 * width + 2 * LANES)
        layer_out, grad_hidden, dots = call(
            finish_body, "finish",
            (
                shape((tok_rows, width), BF16), shape((tok_rows, width), F32),
                shape(scores.shape, F32),
            ),
            [VMEM] * 5,
            operands=(mine_back, hidden, norm_gain[None], cotangent, scores),
        )
        return layer_out, grad_hidden, dots.T

    return per_device


def solution(mesh, interpret=False):
    ctx, exp = mesh.devices.shape
    split = Mesh(mesh.devices.reshape(ctx // 2, 2, exp), ("z", "core", "exp"))
    both = ("z", "core")
    rows = P(("z", "core", "exp"), None)
    in_specs = (
        P(both, "exp"),
        P(both, "exp"),
        P(both, None),
        P(None, "exp"),
        P("exp"),
        P(None, "exp"),
        P(None, both),
        P(None, both),
        P(None, "exp"),
        P("exp"),
        P("exp"),
        P("exp", None),
        rows,
        P(),
        rows,
        rows,
        P("exp", None, both),
        P("exp", None, both),
        P("exp", both, None),
        rows,
    )
    return jax.shard_map(
        make_per_device(interpret),
        mesh=split,
        in_specs=in_specs,
        out_specs=(rows, rows, rows),
        check_vma=False,
    )
```

```python
from functools import partial

import jax
import jax.numpy as jnp
from jax import lax
from jax.experimental import pallas as pl
from jax.experimental.pallas import tpu as pltpu
from jax.sharding import Mesh
from jax.sharding import PartitionSpec as P

BF16 = jnp.bfloat16
F32 = jnp.float32
VMEM = pl.BlockSpec(memory_space=pltpu.VMEM)
SMEM = pl.BlockSpec(memory_space=pltpu.SMEM)
ANY = pl.BlockSpec(memory_space=pl.ANY)
NEAR = "near"
GROUP = 8
LANES = 128


def contract_last(left, right):
    return lax.dot_general(left, right, (((1,), (1,)), ((), ())), preferred_element_type=F32)


def contract_first(left, right):
    return lax.dot_general(left, right, (((0,), (0,)), ((), ())), preferred_element_type=F32)


def column(row):
    count = row.shape[1]
    lane = lax.broadcasted_iota(jnp.int32, (count, count), 1)
    sub = lax.broadcasted_iota(jnp.int32, (count, count), 0)
    spread = jnp.where(lane == sub, jnp.broadcast_to(row, (count, count)), 0.0)
    return jnp.sum(spread, axis=1, keepdims=True)


def parts_of(value, count):
    parts = []
    for _ in range(count):
        part = value.astype(BF16).astype(F32)
        parts.append(part)
        value = value - part
    return parts


def advance(state, steps, drives, coef, rate, k):
    shape = rate.shape
    factor = jnp.exp(jnp.broadcast_to(steps[k : k + 1], shape) * rate)
    push = jnp.broadcast_to(drives[k : k + 1], shape) * jnp.broadcast_to(coef[:, k : k + 1], shape)
    return factor * state + push


def convolved(pad_ref, taps_ref, bias_ref, first, rows):
    taps = taps_ref.shape[0]
    filtered = bias_ref[...]
    for k in range(taps):
        start = first - taps + 1 + k
        filtered = filtered + taps_ref[k : k + 1] * pad_ref[start : start + rows]
    return jax.nn.silu(filtered)


def token_info(ids_ref, scores_ref, stride):
    rows = ids_ref.shape[1]
    shape = (rows, LANES)
    row = lax.broadcasted_iota(jnp.int32, shape, 0)
    lane = lax.broadcasted_iota(jnp.int32, shape, 1)
    ids = [jnp.broadcast_to(column(ids_ref[k : k + 1].astype(F32)), shape) for k in range(2)]
    fields = []
    for k in range(2):
        slot = jnp.zeros(shape, F32)
        for back in range(1, rows):
            for other in ids:
                hit = (pltpu.roll(other, back, 0) == ids[k]) & (row >= back)
                slot = slot + jnp.where(hit, 1.0, 0.0)
        fields.append(stride * ids[k] + slot)
    for k in range(2):
        fields += parts_of(jnp.broadcast_to(column(scores_ref[k : k + 1]), shape), 3)
    info = jnp.zeros(shape, F32)
    for place, field in enumerate(fields):
        info = jnp.where(lane == place, field, info)
    return info


def local_state_body(
    x_ref, low_ref, proj_ref, bias_ref, decay_ref, bcoef_ref, taps_ref, cbias_ref, ids_ref,
    scores_ref, cotangent_ref, late_ref, step_ref, inner_ref, extra_ref, pad_ref, drive_ref,
    *, stride,
):
    length, channels = x_ref.shape
    pad_ref[0:GROUP] = jnp.zeros((GROUP, channels), F32)
    pad_ref[GROUP:] = x_ref[...].astype(F32)
    inner = convolved(pad_ref, taps_ref, cbias_ref, GROUP, length)
    inner_ref[...] = inner
    pre = jnp.dot(low_ref[...], proj_ref[...], preferred_element_type=F32) + bias_ref[...]
    step = jnp.maximum(pre, 0.0) + jnp.log1p(jnp.exp(-jnp.abs(pre)))
    step_ref[...] = step
    drive_ref[...] = step * inner
    rate = -decay_ref[...]
    count = rate.shape[0]
    turn = bcoef_ref.shape[1] - GROUP

    def group(g, carry):
        state, coef = carry
        rows = pl.ds(pl.multiple_of(g * GROUP, GROUP), GROUP)
        steps = step_ref[rows]
        drives = drive_ref[rows]
        for k in range(GROUP):
            state = advance(state, steps, drives, coef, rate, k)
        return state, pltpu.roll(coef, turn, 1)

    first = (jnp.zeros(rate.shape, F32), pltpu.roll(bcoef_ref[...], turn, 1))
    state, _ = lax.fori_loop(1, length // GROUP, group, first)
    late_ref[0:count] = state
    late_ref[count:] = jnp.broadcast_to(
        jnp.sum(step[GROUP:], axis=0, keepdims=True), (GROUP, channels)
    )
    tokens = cotangent_ref.shape[0]
    info = token_info(ids_ref, scores_ref, stride)
    extra_ref[0:tokens, 0:LANES] = info.astype(BF16)
    extra_ref[0:tokens, LANES:] = jnp.zeros((tokens, channels - LANES), BF16)
    for b in range(cotangent_ref.shape[1] // channels):
        rows = slice((b + 1) * tokens, (b + 2) * tokens)
        extra_ref[rows] = cotangent_ref[:, b * channels : (b + 1) * channels]


def first_group_body(
    before_ref, x_ref, taps_ref, cbias_ref, step_ref, decay_ref, bcoef_ref, late_ref, extra_ref,
    send_ref, inner_ref, pad_ref,
):
    length = x_ref.shape[0]
    pad_ref[0:GROUP] = before_ref[length - GROUP :].astype(F32)
    pad_ref[GROUP:] = x_ref[0:GROUP].astype(F32)
    inner = convolved(pad_ref, taps_ref, cbias_ref, GROUP, GROUP)
    inner_ref[...] = inner
    steps = step_ref[0:GROUP]
    drives = steps * inner
    rate = -decay_ref[...]
    count = rate.shape[0]
    coef = bcoef_ref[...]
    state = jnp.zeros(rate.shape, F32)
    for k in range(GROUP):
        state = advance(state, steps, drives, coef, rate, k)
    after = late_ref[count : count + 1]
    state = jnp.exp(jnp.broadcast_to(after, rate.shape) * rate) * state + late_ref[0:count]
    high, low = parts_of(state, 2)
    states = jnp.concatenate([high, low], 0).astype(BF16)
    total = jnp.broadcast_to(
        after + jnp.sum(steps, axis=0, keepdims=True), (GROUP, rate.shape[1])
    )
    high, low = parts_of(total, 2)
    sub = lax.broadcasted_iota(jnp.int32, total.shape, 0)
    total = jnp.where(sub == 0, high, low)
    extra = extra_ref[0:GROUP].astype(F32)
    sums = jnp.concatenate([total, extra], 0).astype(BF16)
    rest = extra_ref[GROUP:]
    for z in range(send_ref.shape[0]):
        send_ref[z, 0 : 2 * count] = states
        send_ref[z, 2 * count : 2 * count + 2 * GROUP] = sums
        send_ref[z, 2 * count + 2 * GROUP :] = rest


def readout_body(
    mine_ref, own_ref, sib_ref, decay_ref, bcoef_ref, ccoef_ref, step_ref, inner_ref, first_ref,
    skip_ref, gate_ref, weight_ref, out_ref, info_ref, drive_ref, read_ref, inner_all_ref,
    tokens_ref,
):
    rate = -decay_ref[...]
    shape = rate.shape
    count, channels = shape
    length = step_ref.shape[0]
    depth = own_ref.shape[0]
    mine = mine_ref[0]
    core = lax.rem(mine, 2)
    state = jnp.zeros(shape, F32)
    for z in range(depth):
        pair = []
        for ref in (own_ref, sib_ref):
            piece = ref[z, 0 : 2 * count].astype(F32)
            sums = ref[z, 2 * count : 2 * count + 2 * GROUP].astype(F32)
            total = jnp.broadcast_to(sums[0:1] + sums[1:2], shape)
            pair.append((jnp.exp(total * rate), piece[0:count] + piece[count:]))
        for k in range(2):
            factor = jnp.where(core == k, pair[0][0], pair[1][0])
            offset = jnp.where(core == k, pair[0][1], pair[1][1])
            state = jnp.where(2 * z + k < mine, factor * state + offset, state)
    inner_all_ref[...] = inner_ref[...]
    inner_all_ref[0:GROUP] = first_ref[...]
    drive_ref[...] = step_ref[...] * inner_all_ref[...]
    turn = bcoef_ref.shape[1] - GROUP

    def group(g, carry):
        state, bcoef, ccoef = carry
        rows = pl.ds(pl.multiple_of(g * GROUP, GROUP), GROUP)
        steps = step_ref[rows]
        drives = drive_ref[rows]
        reads = []
        for k in range(GROUP):
            state = advance(state, steps, drives, bcoef, rate, k)
            reads.append(
                jnp.sum(state * jnp.broadcast_to(ccoef[:, k : k + 1], shape), axis=0, keepdims=True)
            )
        read_ref[rows] = jnp.concatenate(reads, axis=0)
        return state, pltpu.roll(bcoef, turn, 1), pltpu.roll(ccoef, turn, 1)

    lax.fori_loop(0, length // GROUP, group, (state, bcoef_ref[...], ccoef_ref[...]))
    output = read_ref[...] + skip_ref[...] * inner_all_ref[...]
    output = output * jax.nn.silu(gate_ref[...].astype(F32))
    share = jnp.dot(output.astype(BF16), weight_ref[...], preferred_element_type=F32).astype(BF16)
    experts, tall, width = out_ref.shape
    rows = length // experts
    slots = tall - rows
    tokens = info_ref.shape[0] // depth
    start = 2 * count + GROUP
    for z in range(depth):
        at = slice(z * tokens, (z + 1) * tokens)
        extra = own_ref[z, 2 * count : 2 * count + 2 * GROUP].astype(F32)
        info_ref[at] = extra[GROUP:, 0:LANES]
        for b in range(width // channels):
            first = start + (b + 1) * tokens
            tokens_ref[at, b * channels : (b + 1) * channels] = own_ref[
                z, first : first + tokens
            ].astype(F32)
    info = info_ref[...]
    chosen = slot_maps(info, experts * slots)
    packed = jnp.zeros((experts * slots, width), F32)
    for k in range(2):
        at = 2 + 3 * k
        score = info[:, at : at + 1] + info[:, at + 1 : at + 2] + info[:, at + 2 : at + 3]
        grad_rows = (score * tokens_ref[...]).astype(BF16)
        packed = packed + contract_first(chosen[k].astype(BF16), grad_rows)
    packed = packed.astype(BF16)
    for e in range(experts):
        out_ref[e, 0:slots] = packed[e * slots : (e + 1) * slots]
        out_ref[e, slots:] = share[e * rows : (e + 1) * rows]


def slot_maps(info, slots):
    lane = lax.broadcasted_iota(jnp.int32, (info.shape[0], slots), 1)
    block = lax.broadcasted_iota(jnp.int32, (info.shape[0], slots), 0) // GROUP
    maps = []
    for k in range(2):
        base = jnp.broadcast_to(info[:, k : k + 1].astype(jnp.int32), lane.shape)
        maps.append(jnp.where(lane == base + 2 * block, 1.0, 0.0))
    return maps


def norm_body(shares_ref, residual_ref, gain_ref, hidden_ref, send_ref):
    rows = residual_ref.shape[0]
    start = shares_ref.shape[1] - rows
    total = shares_ref[0, start:].astype(F32)
    for c in range(1, shares_ref.shape[0]):
        total = total + shares_ref[c, start:].astype(F32)
    hidden = residual_ref[...].astype(F32) + total
    hidden_ref[...] = hidden
    scale = lax.rsqrt(jnp.mean(hidden * hidden, axis=1, keepdims=True) + 1e-05)
    normed = (hidden * scale * gain_ref[...]).astype(BF16)
    for c in range(send_ref.shape[0]):
        send_ref[c] = normed


def pack_body(tokens_ref, info_ref, slots_ref):
    first, second = slot_maps(info_ref[...], slots_ref.shape[0])
    slots_ref[...] = contract_first((first + second).astype(BF16), tokens_ref[...]).astype(BF16)


def grad_act_body(shares_ref, own_hbm, sib_hbm, out_ref, down_ref, sems):
    experts = shares_ref.shape[0]
    slots = out_ref.shape[1] // experts
    copies = [
        pltpu.make_async_copy(source, down_ref.at[half], sems.at[half])
        for half, source in enumerate((own_hbm, sib_hbm))
    ]
    for copy in copies:
        copy.start()
    rows = shares_ref[:, 0:slots].reshape(experts * slots, shares_ref.shape[2])
    for half in range(2):
        copies[half].wait()
        out_ref[half] = contract_last(rows, down_ref[half])


def expert_body(
    rows_ref, grad_act_ref, gate_hbm, gate_sib_hbm, up_hbm, up_sib_hbm, down_hbm, down_sib_hbm,
    out_ref, gate_ref, up_ref, down_ref, gate_pre_ref, up_pre_ref, act_ref, grad_gate_ref,
    grad_up_ref, dots_ref, sems,
):
    slots, width = rows_ref.shape
    units = gate_ref.shape[2]
    half_width = width // 2
    plan = (
        ("gate_top", gate_hbm.at[0:half_width], gate_ref.at[0, 0:half_width]),
        ("gate_end", gate_hbm.at[half_width:width], gate_ref.at[0, half_width:width]),
        ("up0", up_hbm, up_ref.at[0]),
        ("gate1", gate_sib_hbm, gate_ref.at[1]),
        ("up1", up_sib_hbm, up_ref.at[1]),
        ("down0", down_hbm, down_ref.at[0]),
        ("down1", down_sib_hbm, down_ref.at[1]),
    )
    copies = {}
    for index, (name, source, target) in enumerate(plan):
        copies[name] = pltpu.make_async_copy(source, target, sems.at[index])
        copies[name].start()
    dots_ref[...] = jnp.zeros(dots_ref.shape, F32)
    tall = 16
    rows = rows_ref[...]
    for half in range(2):
        if half == 0:
            copies["gate_top"].wait()
            top = jnp.dot(
                rows[:, 0:half_width], gate_ref[0, 0:half_width], preferred_element_type=F32
            )
            copies["gate_end"].wait()
            gate_pre_ref[...] = top + jnp.dot(
                rows[:, half_width:], gate_ref[0, half_width:], preferred_element_type=F32
            )
            copies["up0"].wait()
            up_pre_ref[...] = jnp.dot(rows, up_ref[0], preferred_element_type=F32)
        else:
            copies["gate1"].wait()
            gate_pre_ref[...] = jnp.dot(rows, gate_ref[1], preferred_element_type=F32)
            copies["up1"].wait()
            up_pre_ref[...] = jnp.dot(rows, up_ref[1], preferred_element_type=F32)

        def chunk(r, carry):
            at = pl.ds(pl.multiple_of(r * tall, tall), tall)
            dots = dots_ref[at]
            for c in range(units // LANES):
                lanes = slice(c * LANES, (c + 1) * LANES)
                gate_pre = gate_pre_ref[at, lanes]
                up_pre = up_pre_ref[at, lanes]
                grad_act = grad_act_ref[half, at, lanes]
                sigma = jax.nn.sigmoid(gate_pre)
                gated = gate_pre * sigma
                act = (gated * up_pre).astype(BF16)
                act_ref[half, at, lanes] = act
                grad_gate_ref[half, at, lanes] = (
                    grad_act * up_pre * sigma * (1.0 + gate_pre * (1.0 - sigma))
                ).astype(BF16)
                grad_up_ref[half, at, lanes] = (grad_act * gated).astype(BF16)
                dots = dots + act.astype(F32) * grad_act
            dots_ref[at] = dots
            return carry

        lax.fori_loop(0, slots // tall, chunk, 0)
    dots = jnp.broadcast_to(jnp.sum(dots_ref[...], axis=1, keepdims=True), (slots, LANES))
    high = dots.astype(BF16).astype(F32)
    lane = lax.broadcasted_iota(jnp.int32, (slots, LANES), 1)
    out_ref[:, 2 * width :] = jnp.where(lane == 0, high, dots - high).astype(BF16)
    copies["down0"].wait()
    share = jnp.dot(act_ref[0], down_ref[0], preferred_element_type=F32)
    copies["down1"].wait()
    share = share + jnp.dot(act_ref[1], down_ref[1], preferred_element_type=F32)
    out_ref[:, 0:width] = share.astype(BF16)
    share = contract_last(grad_gate_ref[0], gate_ref[0]) + contract_last(grad_up_ref[0], up_ref[0])
    share = share + contract_last(grad_gate_ref[1], gate_ref[1])
    share = share + contract_last(grad_up_ref[1], up_ref[1])
    out_ref[:, width : 2 * width] = share.astype(BF16)


def combine_body(back_ref, info_ref, out_ref):
    slots = back_ref.shape[0]
    width = (back_ref.shape[1] - LANES) // 2
    info = info_ref[...]
    tokens = info.shape[0]
    first, second = slot_maps(info, slots)
    weights = [
        first * info[:, 2 + part : 3 + part] + second * info[:, 5 + part : 6 + part]
        for part in range(2)
    ]
    total = jnp.dot(
        jnp.concatenate(weights, 0).astype(BF16), back_ref[:, 0:width], preferred_element_type=F32
    )
    out_ref[:, 0:width] = (total[0:tokens] + total[tokens:]).astype(BF16)
    both = (first + second).astype(BF16)
    out_ref[:, width : 2 * width] = jnp.dot(
        both, back_ref[:, width : 2 * width], preferred_element_type=F32
    ).astype(BF16)
    lane = lax.broadcasted_iota(jnp.int32, (tokens, LANES), 1)
    for k, chosen in enumerate((first, second)):
        dots = jnp.dot(chosen.astype(BF16), back_ref[:, 2 * width :], preferred_element_type=F32)
        dots = jnp.broadcast_to(dots[:, 0:1] + dots[:, 1:2], dots.shape)
        high = dots.astype(BF16).astype(F32)
        start = 2 * width + k * LANES
        out_ref[:, start : start + LANES] = jnp.where(lane == 0, high, dots - high).astype(BF16)


def finish_body(
    back_ref, hidden_ref, gain_ref, cotangent_ref, scores_ref, layer_ref, grad_ref, dots_ref
):
    rows, width = hidden_ref.shape
    total = back_ref[0].astype(F32)
    for c in range(1, back_ref.shape[0]):
        total = total + back_ref[c].astype(F32)
    hidden = hidden_ref[...]
    layer_ref[...] = (hidden + total[:, 0:width]).astype(BF16)
    scale = lax.rsqrt(jnp.mean(hidden * hidden, axis=1, keepdims=True) + 1e-05)
    scaled = total[:, width : 2 * width] * gain_ref[...]
    outer = cotangent_ref[...].astype(F32)
    grad_ref[...] = (
        outer
        + scale * scaled
        - hidden * (scale * scale * scale) * jnp.mean(hidden * scaled, axis=1, keepdims=True)
    )
    lane = lax.broadcasted_iota(jnp.int32, (rows, rows), 1)
    sub = lax.broadcasted_iota(jnp.int32, (rows, rows), 0)
    for k in range(2):
        start = 2 * width + k * LANES
        dots = total[:, start : start + 1] + total[:, start + 1 : start + 2]
        spread = jnp.where(lane == sub, jnp.broadcast_to(dots, lane.shape), 0.0)
        dots = jnp.sum(spread, axis=0, keepdims=True)
        dots_ref[k : k + 1] = dots / scores_ref[k : k + 1]


def make_per_device(interpret):
    def call(body, name, outs, ins, scratch=(), operands=(), mib=24, **options):
        if options:
            body = partial(body, **options)
        near = operands
        if not interpret:
            near = [
                value if spec is SMEM else pltpu.with_memory_space_constraint(
                    value, pltpu.VMEM if spec is NEAR else pltpu.HBM
                )
                for spec, value in zip(ins, operands)
            ]
        else:
            outs = jax.tree.map(lambda out: jax.ShapeDtypeStruct(out.shape, out.dtype), outs)
        return pl.pallas_call(
            body,
            out_shape=outs,
            in_specs=[VMEM if spec is NEAR else spec for spec in ins],
            out_specs=jax.tree.map(lambda _: VMEM, outs),
            scratch_shapes=list(scratch),
            interpret=interpret,
            name=name,
            compiler_params=pltpu.CompilerParams(vmem_limit_bytes=mib * 1024 * 1024),
        )(*near)

    def per_device(
        mixer_input, mixer_gate, step_low, step_proj, step_bias, decay_rate, input_coef,
        output_coef, conv_taps, conv_bias, skip_gain, out_weight, residual, norm_gain,
        expert_ids, gate_scores, gate_weight, up_weight, down_weight, cotangent,
    ):
        length, channels = mixer_input.shape
        count = decay_rate.shape[0]
        tok_rows, width = residual.shape
        units = gate_weight.shape[2]
        experts = lax.axis_size("exp")
        depth = lax.axis_size("z")
        ranks = depth * lax.axis_size("core")
        slots = 2 * experts * depth
        stride = 2 * depth
        swap = [(0, 1), (1, 0)]
        shape = jax.ShapeDtypeStruct
        near = pltpu.VMEM

        def sibling(value):
            return lax.ppermute(value, "core", swap)

        def exchange(rows, axis):
            return lax.all_to_all(rows, axis, split_axis=0, concat_axis=0, tiled=True)

        before = lax.ppermute(mixer_input, ("z", "core"), [(i, i + 1) for i in range(ranks - 1)])
        scores = gate_scores.T

        rows = near((length, channels), F32)
        extra_rows = tok_rows * (1 + width // channels)
        late, step, inner, extra = call(
            local_state_body, "local_state",
            (
                near((count + GROUP, channels), F32), rows, rows,
                near((extra_rows, channels), BF16),
            ),
            [VMEM] * 11,
            (pltpu.VMEM((length + GROUP, channels), F32), pltpu.VMEM((length, channels), F32)),
            (
                mixer_input, step_low, step_proj, step_bias[None], decay_rate, input_coef,
                conv_taps, conv_bias[None], expert_ids.T, scores, cotangent,
            ),
            stride=stride,
        )
        summary, inner_first = call(
            first_group_body, "first_group",
            (
                near((depth, 2 * count + GROUP + extra_rows, channels), BF16),
                near((GROUP, channels), F32),
            ),
            [NEAR] + [VMEM] * 3 + [NEAR] + [VMEM] * 2 + [NEAR] * 2,
            (pltpu.VMEM((2 * GROUP, channels), F32),),
            (
                before, mixer_input, conv_taps, conv_bias[None], step, decay_rate, input_coef,
                late, extra,
            ),
        )
        tall = summary.shape[1]
        gathered = exchange(summary.reshape(depth * tall, channels), "z")
        gathered_sib = sibling(gathered)
        gathered_sib, gate_sent, up_sent, down_sent = lax.optimization_barrier(
            (gathered_sib, gate_weight[0], up_weight[0], down_weight[0])
        )
        gates = (gate_weight[0], sibling(gate_sent))
        ups = (up_weight[0], sibling(up_sent))
        downs = (down_weight[0], sibling(down_sent))
        mine = lax.axis_index(("z", "core")).astype(jnp.int32).reshape(1)
        tall = tok_rows + stride
        share, info = call(
            readout_body, "readout",
            (near((experts, tall, width), BF16), near((depth * tok_rows, LANES), F32)),
            [SMEM] + [NEAR] * 2 + [VMEM] * 3 + [NEAR] * 3 + [VMEM] * 3,
            (
                pltpu.VMEM((length, channels), F32), pltpu.VMEM((length, channels), F32),
                pltpu.VMEM((length, channels), F32), pltpu.VMEM((depth * tok_rows, width), F32),
            ),
            (
                mine, gathered.reshape(summary.shape), gathered_sib.reshape(summary.shape),
                decay_rate, input_coef, output_coef, step, inner, inner_first,
                skip_gain[None], mixer_gate, out_weight,
            ),
        )
        shares = exchange(share.reshape(experts * tall, width), "exp")
        shares = shares.reshape(experts, tall, width)
        hidden, send = call(
            norm_body, "norm",
            (near((tok_rows, width), F32), near((depth, tok_rows, width), BF16)),
            [NEAR] + [VMEM] * 2,
            operands=(shares, residual, norm_gain[None]),
        )
        tokens = exchange(send.reshape(depth * tok_rows, width), "z")
        packed = call(
            pack_body, "pack", near((slots, width), BF16), [NEAR] * 2, operands=(tokens, info)
        )
        rows_x = exchange(packed, "exp")
        grad_act = call(
            grad_act_body, "grad_act", near((2, slots, units), F32), [NEAR] + [ANY] * 2,
            (pltpu.VMEM((2, units, width), BF16), pltpu.SemaphoreType.DMA((2,))),
            (shares,) + downs,
        )
        result = call(
            expert_body, "expert", near((slots, 2 * width + LANES), BF16),
            [NEAR] * 2 + [ANY] * 6,
            (
                pltpu.VMEM((2, width, units), BF16),
                pltpu.VMEM((2, width, units), BF16),
                pltpu.VMEM((2, units, width), BF16),
                pltpu.VMEM((slots, units), F32),
                pltpu.VMEM((slots, units), F32),
                pltpu.VMEM((2, slots, units), BF16),
                pltpu.VMEM((2, slots, units), BF16),
                pltpu.VMEM((2, slots, units), BF16),
                pltpu.VMEM((slots, LANES), F32),
                pltpu.SemaphoreType.DMA((7,)),
            ),
            (rows_x, grad_act) + gates + ups + downs,
            48,
        )
        back = exchange(result, "exp")
        shares_back = call(
            combine_body, "combine", near((depth * tok_rows, 2 * width + 2 * LANES), BF16),
            [NEAR] * 2, operands=(back, info),
        )
        mine_back = exchange(shares_back, "z").reshape(depth, tok_rows, 2 * width + 2 * LANES)
        layer_out, grad_hidden, dots = call(
            finish_body, "finish",
            (
                shape((tok_rows, width), BF16), shape((tok_rows, width), F32),
                shape(scores.shape, F32),
            ),
            [NEAR] * 2 + [VMEM] * 3,
            operands=(mine_back, hidden, norm_gain[None], cotangent, scores),
        )
        return layer_out, grad_hidden, dots.T

    return per_device


def solution(mesh, interpret=False):
    ctx, exp = mesh.devices.shape
    split = Mesh(mesh.devices.reshape(ctx // 2, 2, exp), ("z", "core", "exp"))
    both = ("z", "core")
    rows = P(("z", "core", "exp"), None)
    in_specs = (
        P(both, "exp"),
        P(both, "exp"),
        P(both, None),
        P(None, "exp"),
        P("exp"),
        P(None, "exp"),
        P(None, both),
        P(None, both),
        P(None, "exp"),
        P("exp"),
        P("exp"),
        P("exp", None),
        rows,
        P(),
        rows,
        rows,
        P("exp", None, both),
        P("exp", None, both),
        P("exp", both, None),
        rows,
    )
    return jax.shard_map(
        make_per_device(interpret),
        mesh=split,
        in_specs=in_specs,
        out_specs=(rows, rows, rows),
        check_vma=False,
    )
```

```python
from functools import partial

import jax
import jax.numpy as jnp
from jax import lax
from jax.experimental import pallas as pl
from jax.experimental.pallas import tpu as pltpu
from jax.sharding import Mesh
from jax.sharding import PartitionSpec as P

BF16 = jnp.bfloat16
F32 = jnp.float32
VMEM = pl.BlockSpec(memory_space=pltpu.VMEM)
SMEM = pl.BlockSpec(memory_space=pltpu.SMEM)
ANY = pl.BlockSpec(memory_space=pl.ANY)
NEAR = "near"
GROUP = 8
LANES = 128


def contract_last(left, right):
    return lax.dot_general(left, right, (((1,), (1,)), ((), ())), preferred_element_type=F32)


def contract_first(left, right):
    return lax.dot_general(left, right, (((0,), (0,)), ((), ())), preferred_element_type=F32)


def column(row):
    count = row.shape[1]
    lane = lax.broadcasted_iota(jnp.int32, (count, count), 1)
    sub = lax.broadcasted_iota(jnp.int32, (count, count), 0)
    spread = jnp.where(lane == sub, jnp.broadcast_to(row, (count, count)), 0.0)
    return jnp.sum(spread, axis=1, keepdims=True)


def parts_of(value, count):
    parts = []
    for _ in range(count):
        part = value.astype(BF16).astype(F32)
        parts.append(part)
        value = value - part
    return parts


def advance(state, steps, drives, coef, rate, k):
    shape = rate.shape
    factor = jnp.exp(jnp.broadcast_to(steps[k : k + 1], shape) * rate)
    push = jnp.broadcast_to(drives[k : k + 1], shape) * jnp.broadcast_to(coef[:, k : k + 1], shape)
    return factor * state + push


def convolved(pad_ref, taps_ref, bias_ref, first, rows):
    taps = taps_ref.shape[0]
    filtered = bias_ref[...]
    for k in range(taps):
        start = first - taps + 1 + k
        filtered = filtered + taps_ref[k : k + 1] * pad_ref[start : start + rows]
    return jax.nn.silu(filtered)


def token_info(ids_ref, scores_ref, stride):
    rows = ids_ref.shape[1]
    shape = (rows, LANES)
    row = lax.broadcasted_iota(jnp.int32, shape, 0)
    lane = lax.broadcasted_iota(jnp.int32, shape, 1)
    ids = [jnp.broadcast_to(column(ids_ref[k : k + 1].astype(F32)), shape) for k in range(2)]
    fields = []
    for k in range(2):
        slot = jnp.zeros(shape, F32)
        for back in range(1, rows):
            for other in ids:
                hit = (pltpu.roll(other, back, 0) == ids[k]) & (row >= back)
                slot = slot + jnp.where(hit, 1.0, 0.0)
        fields.append(stride * ids[k] + slot)
    for k in range(2):
        fields += parts_of(jnp.broadcast_to(column(scores_ref[k : k + 1]), shape), 3)
    info = jnp.zeros(shape, F32)
    for place, field in enumerate(fields):
        info = jnp.where(lane == place, field, info)
    return info


def local_state_body(
    x_ref, low_ref, proj_ref, bias_ref, decay_ref, bcoef_ref, taps_ref, cbias_ref, ids_ref,
    scores_ref, cotangent_ref, late_ref, step_ref, inner_ref, extra_ref, pad_ref, drive_ref,
    *, stride,
):
    length, channels = x_ref.shape
    pad_ref[0:GROUP] = jnp.zeros((GROUP, channels), F32)
    pad_ref[GROUP:] = x_ref[...].astype(F32)
    inner = convolved(pad_ref, taps_ref, cbias_ref, GROUP, length)
    inner_ref[...] = inner
    pre = jnp.dot(low_ref[...], proj_ref[...], preferred_element_type=F32) + bias_ref[...]
    step = jnp.maximum(pre, 0.0) + jnp.log1p(jnp.exp(-jnp.abs(pre)))
    step_ref[...] = step
    drive_ref[...] = step * inner
    rate = -decay_ref[...]
    count = rate.shape[0]
    turn = bcoef_ref.shape[1] - GROUP

    def group(g, carry):
        state, coef = carry
        rows = pl.ds(pl.multiple_of(g * GROUP, GROUP), GROUP)
        steps = step_ref[rows]
        drives = drive_ref[rows]
        for k in range(GROUP):
            state = advance(state, steps, drives, coef, rate, k)
        return state, pltpu.roll(coef, turn, 1)

    first = (jnp.zeros(rate.shape, F32), pltpu.roll(bcoef_ref[...], turn, 1))
    state, _ = lax.fori_loop(1, length // GROUP, group, first)
    late_ref[0:count] = state
    late_ref[count:] = jnp.broadcast_to(
        jnp.sum(step[GROUP:], axis=0, keepdims=True), (GROUP, channels)
    )
    tokens = cotangent_ref.shape[0]
    info = token_info(ids_ref, scores_ref, stride)
    extra_ref[0:tokens, 0:LANES] = info.astype(BF16)
    extra_ref[0:tokens, LANES:] = jnp.zeros((tokens, channels - LANES), BF16)
    for b in range(cotangent_ref.shape[1] // channels):
        rows = slice((b + 1) * tokens, (b + 2) * tokens)
        extra_ref[rows] = cotangent_ref[:, b * channels : (b + 1) * channels]


def first_group_body(
    before_ref, x_ref, taps_ref, cbias_ref, step_ref, decay_ref, bcoef_ref, late_ref, extra_ref,
    send_ref, inner_ref, pad_ref,
):
    length = x_ref.shape[0]
    pad_ref[0:GROUP] = before_ref[length - GROUP :].astype(F32)
    pad_ref[GROUP:] = x_ref[0:GROUP].astype(F32)
    inner = convolved(pad_ref, taps_ref, cbias_ref, GROUP, GROUP)
    inner_ref[...] = inner
    steps = step_ref[0:GROUP]
    drives = steps * inner
    rate = -decay_ref[...]
    count = rate.shape[0]
    coef = bcoef_ref[...]
    state = jnp.zeros(rate.shape, F32)
    for k in range(GROUP):
        state = advance(state, steps, drives, coef, rate, k)
    after = late_ref[count : count + 1]
    state = jnp.exp(jnp.broadcast_to(after, rate.shape) * rate) * state + late_ref[0:count]
    high, low = parts_of(state, 2)
    states = jnp.concatenate([high, low], 0).astype(BF16)
    total = jnp.broadcast_to(
        after + jnp.sum(steps, axis=0, keepdims=True), (GROUP, rate.shape[1])
    )
    high, low = parts_of(total, 2)
    sub = lax.broadcasted_iota(jnp.int32, total.shape, 0)
    total = jnp.where(sub == 0, high, low)
    extra = extra_ref[0:GROUP].astype(F32)
    sums = jnp.concatenate([total, extra], 0).astype(BF16)
    rest = extra_ref[GROUP:]
    for z in range(send_ref.shape[0]):
        send_ref[z, 0 : 2 * count] = states
        send_ref[z, 2 * count : 2 * count + 2 * GROUP] = sums
        send_ref[z, 2 * count + 2 * GROUP :] = rest


def readout_body(
    mine_ref, own_ref, sib_ref, decay_ref, bcoef_ref, ccoef_ref, step_ref, inner_ref, first_ref,
    skip_ref, gate_ref, weight_ref, out_ref, drive_ref, read_ref, inner_all_ref,
):
    rate = -decay_ref[...]
    shape = rate.shape
    count, channels = shape
    length = step_ref.shape[0]
    depth = own_ref.shape[0]
    mine = mine_ref[0]
    core = lax.rem(mine, 2)
    state = jnp.zeros(shape, F32)
    for z in range(depth):
        pair = []
        for ref in (own_ref, sib_ref):
            piece = ref[z, 0 : 2 * count].astype(F32)
            sums = ref[z, 2 * count : 2 * count + 2 * GROUP].astype(F32)
            total = jnp.broadcast_to(sums[0:1] + sums[1:2], shape)
            pair.append((jnp.exp(total * rate), piece[0:count] + piece[count:]))
        for k in range(2):
            factor = jnp.where(core == k, pair[0][0], pair[1][0])
            offset = jnp.where(core == k, pair[0][1], pair[1][1])
            state = jnp.where(2 * z + k < mine, factor * state + offset, state)
    inner_all_ref[...] = inner_ref[...]
    inner_all_ref[0:GROUP] = first_ref[...]
    drive_ref[...] = step_ref[...] * inner_all_ref[...]
    turn = bcoef_ref.shape[1] - GROUP

    def group(g, carry):
        state, bcoef, ccoef = carry
        rows = pl.ds(pl.multiple_of(g * GROUP, GROUP), GROUP)
        steps = step_ref[rows]
        drives = drive_ref[rows]
        reads = []
        for k in range(GROUP):
            state = advance(state, steps, drives, bcoef, rate, k)
            reads.append(
                jnp.sum(state * jnp.broadcast_to(ccoef[:, k : k + 1], shape), axis=0, keepdims=True)
            )
        read_ref[rows] = jnp.concatenate(reads, axis=0)
        return state, pltpu.roll(bcoef, turn, 1), pltpu.roll(ccoef, turn, 1)

    lax.fori_loop(0, length // GROUP, group, (state, bcoef_ref[...], ccoef_ref[...]))
    output = read_ref[...] + skip_ref[...] * inner_all_ref[...]
    output = output * jax.nn.silu(gate_ref[...].astype(F32))
    out_ref[...] = jnp.dot(
        output.astype(BF16), weight_ref[...], preferred_element_type=F32
    ).astype(BF16)


def pack_grad_body(own_ref, packed_ref, info_ref, tokens_ref, *, count):
    depth, _, channels = own_ref.shape
    slots, width = packed_ref.shape
    tokens = info_ref.shape[0] // depth
    start = 2 * count + GROUP
    for z in range(depth):
        at = slice(z * tokens, (z + 1) * tokens)
        extra = own_ref[z, 2 * count : 2 * count + 2 * GROUP].astype(F32)
        info_ref[at] = extra[GROUP:, 0:LANES]
        for b in range(width // channels):
            first = start + (b + 1) * tokens
            tokens_ref[at, b * channels : (b + 1) * channels] = own_ref[
                z, first : first + tokens
            ].astype(F32)
    info = info_ref[...]
    chosen = slot_maps(info, slots)
    packed = jnp.zeros((slots, width), F32)
    for k in range(2):
        at = 2 + 3 * k
        score = info[:, at : at + 1] + info[:, at + 1 : at + 2] + info[:, at + 2 : at + 3]
        grad_rows = (score * tokens_ref[...]).astype(BF16)
        packed = packed + contract_first(chosen[k].astype(BF16), grad_rows)
    packed_ref[...] = packed.astype(BF16)


def slot_maps(info, slots):
    lane = lax.broadcasted_iota(jnp.int32, (info.shape[0], slots), 1)
    block = lax.broadcasted_iota(jnp.int32, (info.shape[0], slots), 0) // GROUP
    maps = []
    for k in range(2):
        base = jnp.broadcast_to(info[:, k : k + 1].astype(jnp.int32), lane.shape)
        maps.append(jnp.where(lane == base + 2 * block, 1.0, 0.0))
    return maps


def norm_body(shares_ref, residual_ref, gain_ref, hidden_ref, send_ref):
    total = shares_ref[0].astype(F32)
    for c in range(1, shares_ref.shape[0]):
        total = total + shares_ref[c].astype(F32)
    hidden = residual_ref[...].astype(F32) + total
    hidden_ref[...] = hidden
    scale = lax.rsqrt(jnp.mean(hidden * hidden, axis=1, keepdims=True) + 1e-05)
    send_ref[...] = (hidden * scale * gain_ref[...]).astype(BF16)


def pack_body(mine_ref, blocks_ref, info_ref, slots_ref, tokens_ref):
    core = lax.rem(mine_ref[0], 2)
    rows = blocks_ref.shape[1]
    for z in range(tokens_ref.shape[0] // rows):
        at = slice(z * rows, (z + 1) * rows)
        tokens_ref[at] = jnp.where(core == 0, blocks_ref[2 * z], blocks_ref[2 * z + 1])
    first, second = slot_maps(info_ref[...], slots_ref.shape[0])
    slots_ref[...] = contract_first((first + second).astype(BF16), tokens_ref[...]).astype(BF16)


def grad_act_body(rows_ref, own_hbm, sib_hbm, out_ref, down_ref, sems):
    copies = [
        pltpu.make_async_copy(source, down_ref.at[half], sems.at[half])
        for half, source in enumerate((own_hbm, sib_hbm))
    ]
    for copy in copies:
        copy.start()
    rows = rows_ref[...]
    for half in range(2):
        copies[half].wait()
        out_ref[half] = contract_last(rows, down_ref[half])


def expert_body(
    rows_ref, grad_act_ref, gate_hbm, gate_sib_hbm, up_hbm, up_sib_hbm, down_hbm, down_sib_hbm,
    out_ref, gate_ref, up_ref, down_ref, gate_pre_ref, up_pre_ref, act_ref, grad_gate_ref,
    grad_up_ref, dots_ref, sems,
):
    slots, width = rows_ref.shape
    units = gate_ref.shape[2]
    half_width = width // 2
    plan = (
        ("gate_top", gate_hbm.at[0:half_width], gate_ref.at[0, 0:half_width]),
        ("gate_end", gate_hbm.at[half_width:width], gate_ref.at[0, half_width:width]),
        ("up0", up_hbm, up_ref.at[0]),
        ("gate1", gate_sib_hbm, gate_ref.at[1]),
        ("up1", up_sib_hbm, up_ref.at[1]),
        ("down0", down_hbm, down_ref.at[0]),
        ("down1", down_sib_hbm, down_ref.at[1]),
    )
    copies = {}
    for index, (name, source, target) in enumerate(plan):
        copies[name] = pltpu.make_async_copy(source, target, sems.at[index])
    queue = [copies[name] for name, _, _ in plan]
    for copy in queue[:3]:
        copy.start()
    waiting = queue[3:]

    def ready(name):
        copies[name].wait()
        if waiting:
            waiting.pop(0).start()

    dots_ref[...] = jnp.zeros(dots_ref.shape, F32)
    tall = 16
    rows = rows_ref[...]
    for half in range(2):
        if half == 0:
            ready("gate_top")
            top = jnp.dot(
                rows[:, 0:half_width], gate_ref[0, 0:half_width], preferred_element_type=F32
            )
            ready("gate_end")
            gate_pre_ref[...] = top + jnp.dot(
                rows[:, half_width:], gate_ref[0, half_width:], preferred_element_type=F32
            )
            ready("up0")
            up_pre_ref[...] = jnp.dot(rows, up_ref[0], preferred_element_type=F32)
        else:
            ready("gate1")
            gate_pre_ref[...] = jnp.dot(rows, gate_ref[1], preferred_element_type=F32)
            ready("up1")
            up_pre_ref[...] = jnp.dot(rows, up_ref[1], preferred_element_type=F32)

        def chunk(r, carry):
            at = pl.ds(pl.multiple_of(r * tall, tall), tall)
            dots = dots_ref[at]
            for c in range(units // LANES):
                lanes = slice(c * LANES, (c + 1) * LANES)
                gate_pre = gate_pre_ref[at, lanes]
                up_pre = up_pre_ref[at, lanes]
                grad_act = grad_act_ref[half, at, lanes]
                sigma = jax.nn.sigmoid(gate_pre)
                gated = gate_pre * sigma
                act = (gated * up_pre).astype(BF16)
                act_ref[half, at, lanes] = act
                grad_gate_ref[half, at, lanes] = (
                    grad_act * up_pre * sigma * (1.0 + gate_pre * (1.0 - sigma))
                ).astype(BF16)
                grad_up_ref[half, at, lanes] = (grad_act * gated).astype(BF16)
                dots = dots + act.astype(F32) * grad_act
            dots_ref[at] = dots
            return carry

        lax.fori_loop(0, slots // tall, chunk, 0)
    dots = jnp.broadcast_to(jnp.sum(dots_ref[...], axis=1, keepdims=True), (slots, LANES))
    high = dots.astype(BF16).astype(F32)
    lane = lax.broadcasted_iota(jnp.int32, (slots, LANES), 1)
    out_ref[:, 2 * width :] = jnp.where(lane == 0, high, dots - high).astype(BF16)
    ready("down0")
    share = jnp.dot(act_ref[0], down_ref[0], preferred_element_type=F32)
    ready("down1")
    share = share + jnp.dot(act_ref[1], down_ref[1], preferred_element_type=F32)
    out_ref[:, 0:width] = share.astype(BF16)
    share = contract_last(grad_gate_ref[0], gate_ref[0]) + contract_last(grad_up_ref[0], up_ref[0])
    share = share + contract_last(grad_gate_ref[1], gate_ref[1])
    share = share + contract_last(grad_up_ref[1], up_ref[1])
    out_ref[:, width : 2 * width] = share.astype(BF16)


def combine_body(back_ref, info_ref, out_ref):
    slots = back_ref.shape[0]
    width = (back_ref.shape[1] - LANES) // 2
    info = info_ref[...]
    tokens = info.shape[0]
    first, second = slot_maps(info, slots)
    weights = [
        first * info[:, 2 + part : 3 + part] + second * info[:, 5 + part : 6 + part]
        for part in range(2)
    ]
    total = jnp.dot(
        jnp.concatenate(weights, 0).astype(BF16), back_ref[:, 0:width], preferred_element_type=F32
    )
    out_ref[:, 0:width] = (total[0:tokens] + total[tokens:]).astype(BF16)
    both = (first + second).astype(BF16)
    out_ref[:, width : 2 * width] = jnp.dot(
        both, back_ref[:, width : 2 * width], preferred_element_type=F32
    ).astype(BF16)
    lane = lax.broadcasted_iota(jnp.int32, (tokens, LANES), 1)
    packed = jnp.zeros(lane.shape, F32)
    for k, chosen in enumerate((first, second)):
        dots = jnp.dot(chosen.astype(BF16), back_ref[:, 2 * width :], preferred_element_type=F32)
        dots = jnp.broadcast_to(dots[:, 0:1] + dots[:, 1:2], dots.shape)
        for part, value in enumerate(parts_of(dots, 2)):
            packed = jnp.where(lane == 2 * k + part, value, packed)
    out_ref[:, 2 * width :] = packed.astype(BF16)


def finish_body(
    back_ref, hidden_ref, gain_ref, cotangent_ref, scores_ref, layer_ref, grad_ref, dots_ref
):
    rows, width = hidden_ref.shape
    total = back_ref[0].astype(F32)
    for c in range(1, back_ref.shape[0]):
        total = total + back_ref[c].astype(F32)
    hidden = hidden_ref[...]
    layer_ref[...] = (hidden + total[:, 0:width]).astype(BF16)
    scale = lax.rsqrt(jnp.mean(hidden * hidden, axis=1, keepdims=True) + 1e-05)
    scaled = total[:, width : 2 * width] * gain_ref[...]
    outer = cotangent_ref[...].astype(F32)
    grad_ref[...] = (
        outer
        + scale * scaled
        - hidden * (scale * scale * scale) * jnp.mean(hidden * scaled, axis=1, keepdims=True)
    )
    lane = lax.broadcasted_iota(jnp.int32, (rows, rows), 1)
    sub = lax.broadcasted_iota(jnp.int32, (rows, rows), 0)
    for k in range(2):
        start = 2 * width + 2 * k
        dots = total[:, start : start + 1] + total[:, start + 1 : start + 2]
        spread = jnp.where(lane == sub, jnp.broadcast_to(dots, lane.shape), 0.0)
        dots = jnp.sum(spread, axis=0, keepdims=True)
        dots_ref[k : k + 1] = dots / scores_ref[k : k + 1]


def make_per_device(interpret):
    def call(body, name, outs, ins, scratch=(), operands=(), mib=24, **options):
        if options:
            body = partial(body, **options)
        near = operands
        if not interpret:
            near = [
                value if spec is SMEM else pltpu.with_memory_space_constraint(
                    value, pltpu.VMEM if spec is NEAR else pltpu.HBM
                )
                for spec, value in zip(ins, operands)
            ]
        else:
            outs = jax.tree.map(lambda out: jax.ShapeDtypeStruct(out.shape, out.dtype), outs)
        return pl.pallas_call(
            body,
            out_shape=outs,
            in_specs=[VMEM if spec is NEAR else spec for spec in ins],
            out_specs=jax.tree.map(lambda _: VMEM, outs),
            scratch_shapes=list(scratch),
            interpret=interpret,
            name=name,
            compiler_params=pltpu.CompilerParams(vmem_limit_bytes=mib * 1024 * 1024),
        )(*near)

    def per_device(
        mixer_input, mixer_gate, step_low, step_proj, step_bias, decay_rate, input_coef,
        output_coef, conv_taps, conv_bias, skip_gain, out_weight, residual, norm_gain,
        expert_ids, gate_scores, gate_weight, up_weight, down_weight, cotangent,
    ):
        length, channels = mixer_input.shape
        count = decay_rate.shape[0]
        tok_rows, width = residual.shape
        units = gate_weight.shape[2]
        experts = lax.axis_size("exp")
        depth = lax.axis_size("z")
        ranks = depth * lax.axis_size("core")
        slots = 2 * experts * depth
        stride = 2 * depth
        swap = [(0, 1), (1, 0)]
        shape = jax.ShapeDtypeStruct
        near = pltpu.VMEM

        def sibling(value):
            return lax.ppermute(value, "core", swap)

        def exchange(rows, axis):
            return lax.all_to_all(rows, axis, split_axis=0, concat_axis=0, tiled=True)

        before = lax.ppermute(mixer_input, ("z", "core"), [(i, i + 1) for i in range(ranks - 1)])
        scores = gate_scores.T

        rows = near((length, channels), F32)
        extra_rows = tok_rows * (1 + width // channels)
        late, step, inner, extra = call(
            local_state_body, "local_state",
            (
                near((count + GROUP, channels), F32), rows, rows,
                near((extra_rows, channels), BF16),
            ),
            [VMEM] * 11,
            (pltpu.VMEM((length + GROUP, channels), F32), pltpu.VMEM((length, channels), F32)),
            (
                mixer_input, step_low, step_proj, step_bias[None], decay_rate, input_coef,
                conv_taps, conv_bias[None], expert_ids.T, scores, cotangent,
            ),
            stride=stride,
        )
        summary, inner_first = call(
            first_group_body, "first_group",
            (
                near((depth, 2 * count + GROUP + extra_rows, channels), BF16),
                near((GROUP, channels), F32),
            ),
            [NEAR] + [VMEM] * 3 + [NEAR] + [VMEM] * 2 + [NEAR] * 2,
            (pltpu.VMEM((2 * GROUP, channels), F32),),
            (
                before, mixer_input, conv_taps, conv_bias[None], step, decay_rate, input_coef,
                late, extra,
            ),
        )
        tall = summary.shape[1]
        gathered = exchange(summary.reshape(depth * tall, channels), "z")
        gathered_sib = sibling(gathered)
        gathered_sib, gate_sent, up_sent, down_sent = lax.optimization_barrier(
            (gathered_sib, gate_weight[0], up_weight[0], down_weight[0])
        )
        gates = (gate_weight[0], sibling(gate_sent))
        ups = (up_weight[0], sibling(up_sent))
        downs = (down_weight[0], sibling(down_sent))
        mine = lax.axis_index(("z", "core")).astype(jnp.int32).reshape(1)
        own = gathered.reshape(summary.shape)
        share = call(
            readout_body, "readout", near((length, width), BF16),
            [SMEM] + [NEAR] * 2 + [VMEM] * 3 + [NEAR] * 3 + [VMEM] * 3,
            (
                pltpu.VMEM((length, channels), F32), pltpu.VMEM((length, channels), F32),
                pltpu.VMEM((length, channels), F32),
            ),
            (
                mine, own, gathered_sib.reshape(summary.shape), decay_rate, input_coef,
                output_coef, step, inner, inner_first, skip_gain[None], mixer_gate, out_weight,
            ),
        )
        packed_grad, info = call(
            pack_grad_body, "pack_grad",
            (near((slots, width), BF16), near((depth * tok_rows, LANES), F32)),
            [NEAR], (pltpu.VMEM((depth * tok_rows, width), F32),), (own,), count=count,
        )
        shares, packed_grad = lax.optimization_barrier((exchange(share, "exp"), packed_grad))
        rows_d = exchange(packed_grad, "exp")
        hidden, normed = call(
            norm_body, "norm", (near((tok_rows, width), F32), near((tok_rows, width), BF16)),
            [NEAR] + [VMEM] * 2,
            operands=(shares.reshape(experts, tok_rows, width), residual, norm_gain[None]),
        )
        blocks = lax.all_gather(normed, ("z", "core"), axis=0)
        packed = call(
            pack_body, "pack", near((slots, width), BF16), [SMEM] + [NEAR] * 2,
            (pltpu.VMEM((depth * tok_rows, width), BF16),), (mine, blocks, info),
        )
        rows_x = exchange(packed, "exp")
        grad_act = call(
            grad_act_body, "grad_act", near((2, slots, units), F32), [NEAR] + [ANY] * 2,
            (pltpu.VMEM((2, units, width), BF16), pltpu.SemaphoreType.DMA((2,))),
            (rows_d,) + downs,
        )
        result = call(
            expert_body, "expert", near((slots, 2 * width + LANES), BF16),
            [NEAR] * 2 + [ANY] * 6,
            (
                pltpu.VMEM((2, width, units), BF16),
                pltpu.VMEM((2, width, units), BF16),
                pltpu.VMEM((2, units, width), BF16),
                pltpu.VMEM((slots, units), F32),
                pltpu.VMEM((slots, units), F32),
                pltpu.VMEM((2, slots, units), BF16),
                pltpu.VMEM((2, slots, units), BF16),
                pltpu.VMEM((2, slots, units), BF16),
                pltpu.VMEM((slots, LANES), F32),
                pltpu.SemaphoreType.DMA((7,)),
            ),
            (rows_x, grad_act) + gates + ups + downs,
            48,
        )
        back = exchange(result, "exp")
        shares_back = call(
            combine_body, "combine", near((depth * tok_rows, 2 * width + LANES), BF16),
            [NEAR] * 2, operands=(back, info),
        )
        mine_back = exchange(shares_back, "z").reshape(depth, tok_rows, 2 * width + LANES)
        layer_out, grad_hidden, dots = call(
            finish_body, "finish",
            (
                shape((tok_rows, width), BF16), shape((tok_rows, width), F32),
                shape(scores.shape, F32),
            ),
            [NEAR] * 2 + [VMEM] * 3,
            operands=(mine_back, hidden, norm_gain[None], cotangent, scores),
        )
        return layer_out, grad_hidden, dots.T

    return per_device


def solution(mesh, interpret=False):
    ctx, exp = mesh.devices.shape
    split = Mesh(mesh.devices.reshape(ctx // 2, 2, exp), ("z", "core", "exp"))
    both = ("z", "core")
    rows = P(("z", "core", "exp"), None)
    in_specs = (
        P(both, "exp"),
        P(both, "exp"),
        P(both, None),
        P(None, "exp"),
        P("exp"),
        P(None, "exp"),
        P(None, both),
        P(None, both),
        P(None, "exp"),
        P("exp"),
        P("exp"),
        P("exp", None),
        rows,
        P(),
        rows,
        rows,
        P("exp", None, both),
        P("exp", None, both),
        P("exp", both, None),
        rows,
    )
    return jax.shard_map(
        make_per_device(interpret),
        mesh=split,
        in_specs=in_specs,
        out_specs=(rows, rows, rows),
        check_vma=False,
    )
```

```python
from functools import partial

import jax
import jax.numpy as jnp
from jax import lax
from jax.experimental import pallas as pl
from jax.experimental.pallas import tpu as pltpu
from jax.sharding import Mesh
from jax.sharding import PartitionSpec as P

BF16 = jnp.bfloat16
F32 = jnp.float32
VMEM = pl.BlockSpec(memory_space=pltpu.VMEM)
SMEM = pl.BlockSpec(memory_space=pltpu.SMEM)
ANY = pl.BlockSpec(memory_space=pl.ANY)
NEAR = "near"
GROUP = 8
LANES = 128


def contract_last(left, right):
    return lax.dot_general(left, right, (((1,), (1,)), ((), ())), preferred_element_type=F32)


def contract_first(left, right):
    return lax.dot_general(left, right, (((0,), (0,)), ((), ())), preferred_element_type=F32)


def column(row):
    count = row.shape[1]
    lane = lax.broadcasted_iota(jnp.int32, (count, count), 1)
    sub = lax.broadcasted_iota(jnp.int32, (count, count), 0)
    spread = jnp.where(lane == sub, jnp.broadcast_to(row, (count, count)), 0.0)
    return jnp.sum(spread, axis=1, keepdims=True)


def parts_of(value, count):
    parts = []
    for _ in range(count):
        part = value.astype(BF16).astype(F32)
        parts.append(part)
        value = value - part
    return parts


def advance(state, steps, drives, coef, rate, k):
    shape = rate.shape
    factor = jnp.exp(jnp.broadcast_to(steps[k : k + 1], shape) * rate)
    push = jnp.broadcast_to(drives[k : k + 1], shape) * jnp.broadcast_to(coef[:, k : k + 1], shape)
    return factor * state + push


def convolved(pad_ref, taps_ref, bias_ref, first, rows):
    taps = taps_ref.shape[0]
    filtered = bias_ref[...]
    for k in range(taps):
        start = first - taps + 1 + k
        filtered = filtered + taps_ref[k : k + 1] * pad_ref[start : start + rows]
    return jax.nn.silu(filtered)


def token_info(ids_ref, scores_ref, stride):
    rows = ids_ref.shape[1]
    shape = (rows, LANES)
    row = lax.broadcasted_iota(jnp.int32, shape, 0)
    lane = lax.broadcasted_iota(jnp.int32, shape, 1)
    ids = [jnp.broadcast_to(column(ids_ref[k : k + 1].astype(F32)), shape) for k in range(2)]
    fields = []
    for k in range(2):
        slot = jnp.zeros(shape, F32)
        for back in range(1, rows):
            for other in ids:
                hit = (pltpu.roll(other, back, 0) == ids[k]) & (row >= back)
                slot = slot + jnp.where(hit, 1.0, 0.0)
        fields.append(stride * ids[k] + slot)
    for k in range(2):
        fields += parts_of(jnp.broadcast_to(column(scores_ref[k : k + 1]), shape), 3)
    info = jnp.zeros(shape, F32)
    for place, field in enumerate(fields):
        info = jnp.where(lane == place, field, info)
    return info


def local_state_body(
    x_ref, low_ref, proj_ref, bias_ref, decay_ref, bcoef_ref, taps_ref, cbias_ref, ids_ref,
    scores_ref, cotangent_ref, late_ref, step_ref, inner_ref, extra_ref, pad_ref, drive_ref,
    *, stride,
):
    length, channels = x_ref.shape
    pad_ref[0:GROUP] = jnp.zeros((GROUP, channels), F32)
    pad_ref[GROUP:] = x_ref[...].astype(F32)
    inner = convolved(pad_ref, taps_ref, cbias_ref, GROUP, length)
    inner_ref[...] = inner
    pre = jnp.dot(low_ref[...], proj_ref[...], preferred_element_type=F32) + bias_ref[...]
    step = jnp.maximum(pre, 0.0) + jnp.log1p(jnp.exp(-jnp.abs(pre)))
    step_ref[...] = step
    drive_ref[...] = step * inner
    rate = -decay_ref[...]
    count = rate.shape[0]
    turn = bcoef_ref.shape[1] - GROUP

    def group(g, carry):
        state, coef = carry
        rows = pl.ds(pl.multiple_of(g * GROUP, GROUP), GROUP)
        steps = step_ref[rows]
        drives = drive_ref[rows]
        for k in range(GROUP):
            state = advance(state, steps, drives, coef, rate, k)
        return state, pltpu.roll(coef, turn, 1)

    first = (jnp.zeros(rate.shape, F32), pltpu.roll(bcoef_ref[...], turn, 1))
    state, _ = lax.fori_loop(1, length // GROUP, group, first)
    late_ref[0:count] = state
    late_ref[count:] = jnp.broadcast_to(
        jnp.sum(step[GROUP:], axis=0, keepdims=True), (GROUP, channels)
    )
    tokens = cotangent_ref.shape[0]
    info = token_info(ids_ref, scores_ref, stride)
    extra_ref[0:tokens, 0:LANES] = info.astype(BF16)
    extra_ref[0:tokens, LANES:] = jnp.zeros((tokens, channels - LANES), BF16)
    for b in range(cotangent_ref.shape[1] // channels):
        rows = slice((b + 1) * tokens, (b + 2) * tokens)
        extra_ref[rows] = cotangent_ref[:, b * channels : (b + 1) * channels]


def first_group_body(
    before_ref, x_ref, taps_ref, cbias_ref, step_ref, decay_ref, bcoef_ref, late_ref, extra_ref,
    send_ref, inner_ref, pad_ref,
):
    length = x_ref.shape[0]
    pad_ref[0:GROUP] = before_ref[length - GROUP :].astype(F32)
    pad_ref[GROUP:] = x_ref[0:GROUP].astype(F32)
    inner = convolved(pad_ref, taps_ref, cbias_ref, GROUP, GROUP)
    inner_ref[...] = inner
    steps = step_ref[0:GROUP]
    drives = steps * inner
    rate = -decay_ref[...]
    count = rate.shape[0]
    coef = bcoef_ref[...]
    state = jnp.zeros(rate.shape, F32)
    for k in range(GROUP):
        state = advance(state, steps, drives, coef, rate, k)
    after = late_ref[count : count + 1]
    state = jnp.exp(jnp.broadcast_to(after, rate.shape) * rate) * state + late_ref[0:count]
    high, low = parts_of(state, 2)
    states = jnp.concatenate([high, low], 0).astype(BF16)
    total = jnp.broadcast_to(
        after + jnp.sum(steps, axis=0, keepdims=True), (GROUP, rate.shape[1])
    )
    high, low = parts_of(total, 2)
    sub = lax.broadcasted_iota(jnp.int32, total.shape, 0)
    total = jnp.where(sub == 0, high, low)
    extra = extra_ref[0:GROUP].astype(F32)
    sums = jnp.concatenate([total, extra], 0).astype(BF16)
    rest = extra_ref[GROUP:]
    send_ref[0 : 2 * count] = states
    send_ref[2 * count : 2 * count + 2 * GROUP] = sums
    send_ref[2 * count + 2 * GROUP :] = rest


def readout_body(
    mine_ref, gathered_ref, decay_ref, bcoef_ref, ccoef_ref, step_ref, inner_ref, first_ref,
    skip_ref, gate_ref, weight_ref, out_ref, info_ref, drive_ref, read_ref, inner_all_ref,
    tokens_ref,
):
    rate = -decay_ref[...]
    shape = rate.shape
    count, channels = shape
    length = step_ref.shape[0]
    depth = gathered_ref.shape[0] // 2
    mine = mine_ref[0]
    core = lax.rem(mine, 2)
    state = jnp.zeros(shape, F32)
    for c in range(2 * depth - 1):
        piece = gathered_ref[c, 0 : 2 * count].astype(F32)
        sums = gathered_ref[c, 2 * count : 2 * count + 2 * GROUP].astype(F32)
        total = jnp.broadcast_to(sums[0:1] + sums[1:2], shape)
        longer = jnp.exp(total * rate) * state + (piece[0:count] + piece[count:])
        state = jnp.where(c < mine, longer, state)
    inner_all_ref[...] = inner_ref[...]
    inner_all_ref[0:GROUP] = first_ref[...]
    drive_ref[...] = step_ref[...] * inner_all_ref[...]
    turn = bcoef_ref.shape[1] - GROUP

    def group(g, carry):
        state, bcoef, ccoef = carry
        rows = pl.ds(pl.multiple_of(g * GROUP, GROUP), GROUP)
        steps = step_ref[rows]
        drives = drive_ref[rows]
        reads = []
        for k in range(GROUP):
            state = advance(state, steps, drives, bcoef, rate, k)
            reads.append(
                jnp.sum(state * jnp.broadcast_to(ccoef[:, k : k + 1], shape), axis=0, keepdims=True)
            )
        read_ref[rows] = jnp.concatenate(reads, axis=0)
        return state, pltpu.roll(bcoef, turn, 1), pltpu.roll(ccoef, turn, 1)

    lax.fori_loop(0, length // GROUP, group, (state, bcoef_ref[...], ccoef_ref[...]))
    output = read_ref[...] + skip_ref[...] * inner_all_ref[...]
    output = output * jax.nn.silu(gate_ref[...].astype(F32))
    share = jnp.dot(output.astype(BF16), weight_ref[...], preferred_element_type=F32).astype(BF16)
    experts, tall, width = out_ref.shape
    rows = length // experts
    slots = tall - rows
    tokens = info_ref.shape[0] // depth
    start = 2 * count + GROUP
    for z in range(depth):
        at = slice(z * tokens, (z + 1) * tokens)
        place = 2 * z + core
        extra = gathered_ref[place, 2 * count : 2 * count + 2 * GROUP].astype(F32)
        info_ref[at] = extra[GROUP:, 0:LANES]
        for b in range(width // channels):
            first = start + (b + 1) * tokens
            tokens_ref[at, b * channels : (b + 1) * channels] = gathered_ref[
                place, first : first + tokens
            ].astype(F32)
    info = info_ref[...]
    chosen = slot_maps(info, experts * slots)
    packed = jnp.zeros((experts * slots, width), F32)
    for k in range(2):
        at = 2 + 3 * k
        score = info[:, at : at + 1] + info[:, at + 1 : at + 2] + info[:, at + 2 : at + 3]
        grad_rows = (score * tokens_ref[...]).astype(BF16)
        packed = packed + contract_first(chosen[k].astype(BF16), grad_rows)
    packed = packed.astype(BF16)
    for e in range(experts):
        out_ref[e, 0:slots] = packed[e * slots : (e + 1) * slots]
        out_ref[e, slots:] = share[e * rows : (e + 1) * rows]


def slot_maps(info, slots):
    lane = lax.broadcasted_iota(jnp.int32, (info.shape[0], slots), 1)
    block = lax.broadcasted_iota(jnp.int32, (info.shape[0], slots), 0) // GROUP
    maps = []
    for k in range(2):
        base = jnp.broadcast_to(info[:, k : k + 1].astype(jnp.int32), lane.shape)
        maps.append(jnp.where(lane == base + 2 * block, 1.0, 0.0))
    return maps


def norm_body(shares_ref, residual_ref, gain_ref, hidden_ref, send_ref):
    rows = residual_ref.shape[0]
    start = shares_ref.shape[1] - rows
    total = shares_ref[0, start:].astype(F32)
    for c in range(1, shares_ref.shape[0]):
        total = total + shares_ref[c, start:].astype(F32)
    hidden = residual_ref[...].astype(F32) + total
    hidden_ref[...] = hidden
    scale = lax.rsqrt(jnp.mean(hidden * hidden, axis=1, keepdims=True) + 1e-05)
    normed = (hidden * scale * gain_ref[...]).astype(BF16)
    for c in range(send_ref.shape[0]):
        send_ref[c] = normed


def pack_body(tokens_ref, info_ref, slots_ref):
    first, second = slot_maps(info_ref[...], slots_ref.shape[0])
    slots_ref[...] = contract_first((first + second).astype(BF16), tokens_ref[...]).astype(BF16)


def expert_body(
    rows_ref, shares_ref, gate_hbm, gate_sib_hbm, up_hbm, up_sib_hbm, down_hbm, down_sib_hbm,
    out_ref, gate_ref, up_ref, down_ref, gate_pre_ref, up_pre_ref, act_ref, grad_gate_ref,
    grad_up_ref, dots_ref, grad_act_ref, sems,
):
    slots, width = rows_ref.shape
    units = gate_ref.shape[2]
    plan = (
        (down_hbm, down_ref, 0), (down_sib_hbm, down_ref, 1), (gate_hbm, gate_ref, 0),
        (up_hbm, up_ref, 0), (gate_sib_hbm, gate_ref, 1), (up_sib_hbm, up_ref, 1),
    )
    copies = [
        pltpu.make_async_copy(source, target.at[half], sems.at[index])
        for index, (source, target, half) in enumerate(plan)
    ]
    for copy in copies[:3]:
        copy.start()

    def ready(index):
        copies[index].wait()
        if index + 3 < len(copies):
            copies[index + 3].start()

    experts = shares_ref.shape[0]
    grad_rows = shares_ref[:, 0 : slots // experts].reshape(slots, width)
    for half in range(2):
        ready(half)
        grad_act_ref[half] = contract_last(grad_rows, down_ref[half])
    dots_ref[...] = jnp.zeros(dots_ref.shape, F32)
    tall = 16
    rows = rows_ref[...]
    for half in range(2):
        ready(2 + 2 * half)
        gate_pre_ref[...] = jnp.dot(rows, gate_ref[half], preferred_element_type=F32)
        ready(3 + 2 * half)
        up_pre_ref[...] = jnp.dot(rows, up_ref[half], preferred_element_type=F32)

        def chunk(r, carry):
            at = pl.ds(pl.multiple_of(r * tall, tall), tall)
            dots = dots_ref[at]
            for c in range(units // LANES):
                lanes = slice(c * LANES, (c + 1) * LANES)
                gate_pre = gate_pre_ref[at, lanes]
                up_pre = up_pre_ref[at, lanes]
                grad_act = grad_act_ref[half, at, lanes]
                sigma = jax.nn.sigmoid(gate_pre)
                gated = gate_pre * sigma
                act = (gated * up_pre).astype(BF16)
                act_ref[half, at, lanes] = act
                grad_gate_ref[half, at, lanes] = (
                    grad_act * up_pre * sigma * (1.0 + gate_pre * (1.0 - sigma))
                ).astype(BF16)
                grad_up_ref[half, at, lanes] = (grad_act * gated).astype(BF16)
                dots = dots + act.astype(F32) * grad_act
            dots_ref[at] = dots
            return carry

        lax.fori_loop(0, slots // tall, chunk, 0)
    dots = jnp.broadcast_to(jnp.sum(dots_ref[...], axis=1, keepdims=True), (slots, LANES))
    high = dots.astype(BF16).astype(F32)
    lane = lax.broadcasted_iota(jnp.int32, (slots, LANES), 1)
    out_ref[:, 2 * width :] = jnp.where(lane == 0, high, dots - high).astype(BF16)
    share = jnp.dot(act_ref[0], down_ref[0], preferred_element_type=F32)
    share = share + jnp.dot(act_ref[1], down_ref[1], preferred_element_type=F32)
    out_ref[:, 0:width] = share.astype(BF16)
    share = contract_last(grad_gate_ref[0], gate_ref[0]) + contract_last(grad_up_ref[0], up_ref[0])
    share = share + contract_last(grad_gate_ref[1], gate_ref[1])
    share = share + contract_last(grad_up_ref[1], up_ref[1])
    out_ref[:, width : 2 * width] = share.astype(BF16)


def combine_body(back_ref, info_ref, out_ref):
    slots = back_ref.shape[0]
    width = (back_ref.shape[1] - LANES) // 2
    info = info_ref[...]
    tokens = info.shape[0]
    first, second = slot_maps(info, slots)
    weights = [
        first * info[:, 2 + part : 3 + part] + second * info[:, 5 + part : 6 + part]
        for part in range(2)
    ]
    total = jnp.dot(
        jnp.concatenate(weights, 0).astype(BF16), back_ref[:, 0:width], preferred_element_type=F32
    )
    out_ref[:, 0:width] = (total[0:tokens] + total[tokens:]).astype(BF16)
    both = (first + second).astype(BF16)
    out_ref[:, width : 2 * width] = jnp.dot(
        both, back_ref[:, width : 2 * width], preferred_element_type=F32
    ).astype(BF16)
    lane = lax.broadcasted_iota(jnp.int32, (tokens, LANES), 1)
    packed = jnp.zeros(lane.shape, F32)
    for k, chosen in enumerate((first, second)):
        dots = jnp.dot(chosen.astype(BF16), back_ref[:, 2 * width :], preferred_element_type=F32)
        dots = jnp.broadcast_to(dots[:, 0:1] + dots[:, 1:2], dots.shape)
        for part, value in enumerate(parts_of(dots, 2)):
            packed = jnp.where(lane == 2 * k + part, value, packed)
    out_ref[:, 2 * width :] = packed.astype(BF16)


def finish_body(
    back_ref, hidden_ref, gain_ref, cotangent_ref, scores_ref, layer_ref, grad_ref, dots_ref
):
    rows, width = hidden_ref.shape
    total = back_ref[0].astype(F32)
    for c in range(1, back_ref.shape[0]):
        total = total + back_ref[c].astype(F32)
    hidden = hidden_ref[...]
    layer_ref[...] = (hidden + total[:, 0:width]).astype(BF16)
    scale = lax.rsqrt(jnp.mean(hidden * hidden, axis=1, keepdims=True) + 1e-05)
    scaled = total[:, width : 2 * width] * gain_ref[...]
    outer = cotangent_ref[...].astype(F32)
    grad_ref[...] = (
        outer
        + scale * scaled
        - hidden * (scale * scale * scale) * jnp.mean(hidden * scaled, axis=1, keepdims=True)
    )
    lane = lax.broadcasted_iota(jnp.int32, (rows, rows), 1)
    sub = lax.broadcasted_iota(jnp.int32, (rows, rows), 0)
    for k in range(2):
        start = 2 * width + 2 * k
        dots = total[:, start : start + 1] + total[:, start + 1 : start + 2]
        spread = jnp.where(lane == sub, jnp.broadcast_to(dots, lane.shape), 0.0)
        dots = jnp.sum(spread, axis=0, keepdims=True)
        dots_ref[k : k + 1] = dots / scores_ref[k : k + 1]


def make_per_device(interpret):
    def call(body, name, outs, ins, scratch=(), operands=(), mib=24, **options):
        if options:
            body = partial(body, **options)
        near = operands
        if not interpret:
            near = [
                value if spec is SMEM else pltpu.with_memory_space_constraint(
                    value, pltpu.VMEM if spec is NEAR else pltpu.HBM
                )
                for spec, value in zip(ins, operands)
            ]
        else:
            outs = jax.tree.map(lambda out: jax.ShapeDtypeStruct(out.shape, out.dtype), outs)
        return pl.pallas_call(
            body,
            out_shape=outs,
            in_specs=[VMEM if spec is NEAR else spec for spec in ins],
            out_specs=jax.tree.map(lambda _: VMEM, outs),
            scratch_shapes=list(scratch),
            interpret=interpret,
            name=name,
            compiler_params=pltpu.CompilerParams(vmem_limit_bytes=mib * 1024 * 1024),
        )(*near)

    def per_device(
        mixer_input, mixer_gate, step_low, step_proj, step_bias, decay_rate, input_coef,
        output_coef, conv_taps, conv_bias, skip_gain, out_weight, residual, norm_gain,
        expert_ids, gate_scores, gate_weight, up_weight, down_weight, cotangent,
    ):
        length, channels = mixer_input.shape
        count = decay_rate.shape[0]
        tok_rows, width = residual.shape
        units = gate_weight.shape[2]
        experts = lax.axis_size("exp")
        depth = lax.axis_size("z")
        ranks = depth * lax.axis_size("core")
        slots = 2 * experts * depth
        stride = 2 * depth
        swap = [(0, 1), (1, 0)]
        shape = jax.ShapeDtypeStruct
        near = pltpu.VMEM

        def sibling(value):
            return lax.ppermute(value, "core", swap)

        def exchange(rows, axis):
            return lax.all_to_all(rows, axis, split_axis=0, concat_axis=0, tiled=True)

        before = lax.ppermute(mixer_input, ("z", "core"), [(i, i + 1) for i in range(ranks - 1)])
        scores = gate_scores.T

        rows = near((length, channels), F32)
        extra_rows = tok_rows * (1 + width // channels)
        late, step, inner, extra = call(
            local_state_body, "local_state",
            (
                near((count + GROUP, channels), F32), rows, rows,
                near((extra_rows, channels), BF16),
            ),
            [VMEM] * 11,
            (pltpu.VMEM((length + GROUP, channels), F32), pltpu.VMEM((length, channels), F32)),
            (
                mixer_input, step_low, step_proj, step_bias[None], decay_rate, input_coef,
                conv_taps, conv_bias[None], expert_ids.T, scores, cotangent,
            ),
            stride=stride,
        )
        summary, inner_first = call(
            first_group_body, "first_group",
            (
                near((2 * count + GROUP + extra_rows, channels), BF16),
                near((GROUP, channels), F32),
            ),
            [NEAR] + [VMEM] * 3 + [NEAR] + [VMEM] * 2 + [NEAR] * 2,
            (pltpu.VMEM((2 * GROUP, channels), F32),),
            (
                before, mixer_input, conv_taps, conv_bias[None], step, decay_rate, input_coef,
                late, extra,
            ),
        )
        gathered = lax.all_gather(summary, ("z", "core"), axis=0)
        gathered, gate_sent, up_sent, down_sent = lax.optimization_barrier(
            (gathered, gate_weight[0], up_weight[0], down_weight[0])
        )
        gates = (gate_weight[0], sibling(gate_sent))
        ups = (up_weight[0], sibling(up_sent))
        downs = (down_weight[0], sibling(down_sent))
        mine = lax.axis_index(("z", "core")).astype(jnp.int32).reshape(1)
        tall = tok_rows + stride
        share, info = call(
            readout_body, "readout",
            (near((experts, tall, width), BF16), near((depth * tok_rows, LANES), F32)),
            [SMEM, NEAR] + [VMEM] * 3 + [NEAR] * 3 + [VMEM] * 3,
            (
                pltpu.VMEM((length, channels), F32), pltpu.VMEM((length, channels), F32),
                pltpu.VMEM((length, channels), F32), pltpu.VMEM((depth * tok_rows, width), F32),
            ),
            (
                mine, gathered, decay_rate, input_coef, output_coef, step, inner, inner_first,
                skip_gain[None], mixer_gate, out_weight,
            ),
        )
        shares = exchange(share.reshape(experts * tall, width), "exp")
        shares = shares.reshape(experts, tall, width)
        hidden, send = call(
            norm_body, "norm",
            (near((tok_rows, width), F32), near((depth, tok_rows, width), BF16)),
            [NEAR] + [VMEM] * 2,
            operands=(shares, residual, norm_gain[None]),
        )
        tokens = exchange(send.reshape(depth * tok_rows, width), "z")
        packed = call(
            pack_body, "pack", near((slots, width), BF16), [NEAR] * 2, operands=(tokens, info)
        )
        rows_x = exchange(packed, "exp")
        result = call(
            expert_body, "expert", near((slots, 2 * width + LANES), BF16),
            [NEAR] * 2 + [ANY] * 6,
            (
                pltpu.VMEM((2, width, units), BF16),
                pltpu.VMEM((2, width, units), BF16),
                pltpu.VMEM((2, units, width), BF16),
                pltpu.VMEM((slots, units), F32),
                pltpu.VMEM((slots, units), F32),
                pltpu.VMEM((2, slots, units), BF16),
                pltpu.VMEM((2, slots, units), BF16),
                pltpu.VMEM((2, slots, units), BF16),
                pltpu.VMEM((slots, LANES), F32),
                pltpu.VMEM((2, slots, units), F32),
                pltpu.SemaphoreType.DMA((6,)),
            ),
            (rows_x, shares) + gates + ups + downs,
            48,
        )
        back = exchange(result, "exp")
        shares_back = call(
            combine_body, "combine", near((depth * tok_rows, 2 * width + LANES), BF16),
            [NEAR] * 2, operands=(back, info),
        )
        mine_back = exchange(shares_back, "z").reshape(depth, tok_rows, 2 * width + LANES)
        layer_out, grad_hidden, dots = call(
            finish_body, "finish",
            (
                shape((tok_rows, width), BF16), shape((tok_rows, width), F32),
                shape(scores.shape, F32),
            ),
            [NEAR] * 2 + [VMEM] * 3,
            operands=(mine_back, hidden, norm_gain[None], cotangent, scores),
        )
        return layer_out, grad_hidden, dots.T

    return per_device


def solution(mesh, interpret=False):
    ctx, exp = mesh.devices.shape
    split = Mesh(mesh.devices.reshape(ctx // 2, 2, exp), ("z", "core", "exp"))
    both = ("z", "core")
    rows = P(("z", "core", "exp"), None)
    in_specs = (
        P(both, "exp"),
        P(both, "exp"),
        P(both, None),
        P(None, "exp"),
        P("exp"),
        P(None, "exp"),
        P(None, both),
        P(None, both),
        P(None, "exp"),
        P("exp"),
        P("exp"),
        P("exp", None),
        rows,
        P(),
        rows,
        rows,
        P("exp", None, both),
        P("exp", None, both),
        P("exp", both, None),
        rows,
    )
    return jax.shard_map(
        make_per_device(interpret),
        mesh=split,
        in_specs=in_specs,
        out_specs=(rows, rows, rows),
        check_vma=False,
    )
```

```python
from functools import partial

import jax
import jax.numpy as jnp
from jax import lax
from jax.experimental import pallas as pl
from jax.experimental.pallas import tpu as pltpu
from jax.sharding import Mesh
from jax.sharding import PartitionSpec as P

BF16 = jnp.bfloat16
F32 = jnp.float32
VMEM = pl.BlockSpec(memory_space=pltpu.VMEM)
SMEM = pl.BlockSpec(memory_space=pltpu.SMEM)
ANY = pl.BlockSpec(memory_space=pl.ANY)
NEAR = "near"
GROUP = 8
LANES = 128


def contract_last(left, right):
    return lax.dot_general(left, right, (((1,), (1,)), ((), ())), preferred_element_type=F32)


def contract_first(left, right):
    return lax.dot_general(left, right, (((0,), (0,)), ((), ())), preferred_element_type=F32)


def column(row):
    count = row.shape[1]
    lane = lax.broadcasted_iota(jnp.int32, (count, count), 1)
    sub = lax.broadcasted_iota(jnp.int32, (count, count), 0)
    spread = jnp.where(lane == sub, jnp.broadcast_to(row, (count, count)), 0.0)
    return jnp.sum(spread, axis=1, keepdims=True)


def parts_of(value, count):
    parts = []
    for _ in range(count):
        part = value.astype(BF16).astype(F32)
        parts.append(part)
        value = value - part
    return parts


def advance(state, steps, drives, coef, rate, k):
    shape = rate.shape
    factor = jnp.exp(jnp.broadcast_to(steps[k : k + 1], shape) * rate)
    push = jnp.broadcast_to(drives[k : k + 1], shape) * jnp.broadcast_to(coef[:, k : k + 1], shape)
    return factor * state + push


def convolved(pad_ref, taps_ref, bias_ref, first, rows):
    taps = taps_ref.shape[0]
    filtered = bias_ref[...]
    for k in range(taps):
        start = first - taps + 1 + k
        filtered = filtered + taps_ref[k : k + 1] * pad_ref[start : start + rows]
    return jax.nn.silu(filtered)


def token_info(ids_ref, scores_ref, stride):
    rows = ids_ref.shape[1]
    shape = (rows, LANES)
    row = lax.broadcasted_iota(jnp.int32, shape, 0)
    lane = lax.broadcasted_iota(jnp.int32, shape, 1)
    ids = [jnp.broadcast_to(column(ids_ref[k : k + 1].astype(F32)), shape) for k in range(2)]
    fields = []
    for k in range(2):
        slot = jnp.zeros(shape, F32)
        for back in range(1, rows):
            for other in ids:
                hit = (pltpu.roll(other, back, 0) == ids[k]) & (row >= back)
                slot = slot + jnp.where(hit, 1.0, 0.0)
        fields.append(stride * ids[k] + slot)
    for k in range(2):
        fields += parts_of(jnp.broadcast_to(column(scores_ref[k : k + 1]), shape), 3)
    info = jnp.zeros(shape, F32)
    for place, field in enumerate(fields):
        info = jnp.where(lane == place, field, info)
    return info


def local_state_body(
    x_ref, low_ref, proj_ref, bias_ref, decay_ref, bcoef_ref, taps_ref, cbias_ref, ids_ref,
    scores_ref, cotangent_ref, late_ref, step_ref, inner_ref, extra_ref, pad_ref, drive_ref,
    *, stride,
):
    length, channels = x_ref.shape
    pad_ref[0:GROUP] = jnp.zeros((GROUP, channels), F32)
    pad_ref[GROUP:] = x_ref[...].astype(F32)
    inner = convolved(pad_ref, taps_ref, cbias_ref, GROUP, length)
    inner_ref[...] = inner
    pre = jnp.dot(low_ref[...], proj_ref[...], preferred_element_type=F32) + bias_ref[...]
    step = jnp.maximum(pre, 0.0) + jnp.log1p(jnp.exp(-jnp.abs(pre)))
    step_ref[...] = step
    drive_ref[...] = step * inner
    rate = -decay_ref[...]
    count = rate.shape[0]
    turn = bcoef_ref.shape[1] - GROUP

    def group(g, carry):
        state, coef = carry
        rows = pl.ds(pl.multiple_of(g * GROUP, GROUP), GROUP)
        steps = step_ref[rows]
        drives = drive_ref[rows]
        for k in range(GROUP):
            state = advance(state, steps, drives, coef, rate, k)
        return state, pltpu.roll(coef, turn, 1)

    first = (jnp.zeros(rate.shape, F32), pltpu.roll(bcoef_ref[...], turn, 1))
    state, _ = lax.fori_loop(1, length // GROUP, group, first)
    late_ref[0:count] = state
    late_ref[count:] = jnp.broadcast_to(
        jnp.sum(step[GROUP:], axis=0, keepdims=True), (GROUP, channels)
    )
    tokens = cotangent_ref.shape[0]
    info = token_info(ids_ref, scores_ref, stride)
    extra_ref[0:tokens, 0:LANES] = info.astype(BF16)
    extra_ref[0:tokens, LANES:] = jnp.zeros((tokens, channels - LANES), BF16)
    for b in range(cotangent_ref.shape[1] // channels):
        rows = slice((b + 1) * tokens, (b + 2) * tokens)
        extra_ref[rows] = cotangent_ref[:, b * channels : (b + 1) * channels]


def first_group_body(
    before_ref, x_ref, taps_ref, cbias_ref, step_ref, decay_ref, bcoef_ref, late_ref, extra_ref,
    send_ref, inner_ref, pad_ref,
):
    length = x_ref.shape[0]
    pad_ref[0:GROUP] = before_ref[length - GROUP :].astype(F32)
    pad_ref[GROUP:] = x_ref[0:GROUP].astype(F32)
    inner = convolved(pad_ref, taps_ref, cbias_ref, GROUP, GROUP)
    inner_ref[...] = inner
    steps = step_ref[0:GROUP]
    drives = steps * inner
    rate = -decay_ref[...]
    count = rate.shape[0]
    coef = bcoef_ref[...]
    state = jnp.zeros(rate.shape, F32)
    for k in range(GROUP):
        state = advance(state, steps, drives, coef, rate, k)
    after = late_ref[count : count + 1]
    state = jnp.exp(jnp.broadcast_to(after, rate.shape) * rate) * state + late_ref[0:count]
    high, low = parts_of(state, 2)
    states = jnp.concatenate([high, low], 0).astype(BF16)
    total = jnp.broadcast_to(
        after + jnp.sum(steps, axis=0, keepdims=True), (GROUP, rate.shape[1])
    )
    high, low = parts_of(total, 2)
    sub = lax.broadcasted_iota(jnp.int32, total.shape, 0)
    total = jnp.where(sub == 0, high, low)
    extra = extra_ref[0:GROUP].astype(F32)
    sums = jnp.concatenate([total, extra], 0).astype(BF16)
    rest = extra_ref[GROUP:]
    send_ref[0 : 2 * count] = states
    send_ref[2 * count : 2 * count + 2 * GROUP] = sums
    send_ref[2 * count + 2 * GROUP :] = rest


def readout_body(
    mine_ref, gathered_ref, decay_ref, bcoef_ref, ccoef_ref, step_ref, inner_ref, first_ref,
    skip_ref, gate_ref, weight_ref, out_ref, packed_ref, info_ref, drive_ref, read_ref, inner_all_ref,
    tokens_ref,
):
    rate = -decay_ref[...]
    shape = rate.shape
    count, channels = shape
    length = step_ref.shape[0]
    depth = gathered_ref.shape[0] // 2
    mine = mine_ref[0]
    core = lax.rem(mine, 2)
    state = jnp.zeros(shape, F32)
    for c in range(2 * depth - 1):
        piece = gathered_ref[c, 0 : 2 * count].astype(F32)
        sums = gathered_ref[c, 2 * count : 2 * count + 2 * GROUP].astype(F32)
        total = jnp.broadcast_to(sums[0:1] + sums[1:2], shape)
        longer = jnp.exp(total * rate) * state + (piece[0:count] + piece[count:])
        state = jnp.where(c < mine, longer, state)
    inner_all_ref[...] = inner_ref[...]
    inner_all_ref[0:GROUP] = first_ref[...]
    drive_ref[...] = step_ref[...] * inner_all_ref[...]
    turn = bcoef_ref.shape[1] - GROUP

    def group(g, carry):
        state, bcoef, ccoef = carry
        rows = pl.ds(pl.multiple_of(g * GROUP, GROUP), GROUP)
        steps = step_ref[rows]
        drives = drive_ref[rows]
        reads = []
        for k in range(GROUP):
            state = advance(state, steps, drives, bcoef, rate, k)
            reads.append(
                jnp.sum(state * jnp.broadcast_to(ccoef[:, k : k + 1], shape), axis=0, keepdims=True)
            )
        read_ref[rows] = jnp.concatenate(reads, axis=0)
        return state, pltpu.roll(bcoef, turn, 1), pltpu.roll(ccoef, turn, 1)

    lax.fori_loop(0, length // GROUP, group, (state, bcoef_ref[...], ccoef_ref[...]))
    output = read_ref[...] + skip_ref[...] * inner_all_ref[...]
    output = output * jax.nn.silu(gate_ref[...].astype(F32))
    out_ref[...] = jnp.dot(
        output.astype(BF16), weight_ref[...], preferred_element_type=F32
    ).astype(BF16)
    slots, width = packed_ref.shape
    tokens = info_ref.shape[0] // depth
    start = 2 * count + GROUP
    for z in range(depth):
        at = slice(z * tokens, (z + 1) * tokens)
        place = 2 * z + core
        extra = gathered_ref[place, 2 * count : 2 * count + 2 * GROUP].astype(F32)
        info_ref[at] = extra[GROUP:, 0:LANES]
        for b in range(width // channels):
            first = start + (b + 1) * tokens
            tokens_ref[at, b * channels : (b + 1) * channels] = gathered_ref[
                place, first : first + tokens
            ].astype(F32)
    info = info_ref[...]
    chosen = slot_maps(info, slots)
    packed = jnp.zeros((slots, width), F32)
    for k in range(2):
        at = 2 + 3 * k
        score = info[:, at : at + 1] + info[:, at + 1 : at + 2] + info[:, at + 2 : at + 3]
        grad_rows = (score * tokens_ref[...]).astype(BF16)
        packed = packed + contract_first(chosen[k].astype(BF16), grad_rows)
    packed_ref[...] = packed.astype(BF16)


def slot_maps(info, slots):
    lane = lax.broadcasted_iota(jnp.int32, (info.shape[0], slots), 1)
    block = lax.broadcasted_iota(jnp.int32, (info.shape[0], slots), 0) // GROUP
    maps = []
    for k in range(2):
        base = jnp.broadcast_to(info[:, k : k + 1].astype(jnp.int32), lane.shape)
        maps.append(jnp.where(lane == base + 2 * block, 1.0, 0.0))
    return maps


def norm_body(shares_ref, residual_ref, gain_ref, hidden_ref, send_ref):
    total = shares_ref[0].astype(F32)
    for c in range(1, shares_ref.shape[0]):
        total = total + shares_ref[c].astype(F32)
    hidden = residual_ref[...].astype(F32) + total
    hidden_ref[...] = hidden
    scale = lax.rsqrt(jnp.mean(hidden * hidden, axis=1, keepdims=True) + 1e-05)
    normed = (hidden * scale * gain_ref[...]).astype(BF16)
    for c in range(send_ref.shape[0]):
        send_ref[c] = normed


def pack_body(tokens_ref, info_ref, packed_ref, slots_ref):
    slots, width = packed_ref.shape
    first, second = slot_maps(info_ref[...], slots)
    rows = contract_first((first + second).astype(BF16), tokens_ref[...])
    slots_ref[:, 0:width] = rows.astype(BF16)
    slots_ref[:, width:] = packed_ref[...]


def expert_body(
    rows_ref, gate_hbm, gate_sib_hbm, up_hbm, up_sib_hbm, down_hbm, down_sib_hbm,
    out_ref, gate_ref, up_ref, down_ref, gate_pre_ref, up_pre_ref, act_ref, grad_gate_ref,
    grad_up_ref, dots_ref, grad_act_ref, sems,
):
    slots = rows_ref.shape[0]
    width, units = gate_ref.shape[1:]
    plan = (
        (down_hbm, down_ref, 0), (down_sib_hbm, down_ref, 1), (gate_hbm, gate_ref, 0),
        (up_hbm, up_ref, 0), (gate_sib_hbm, gate_ref, 1), (up_sib_hbm, up_ref, 1),
    )
    copies = [
        pltpu.make_async_copy(source, target.at[half], sems.at[index])
        for index, (source, target, half) in enumerate(plan)
    ]
    for copy in copies[:3]:
        copy.start()

    def ready(index):
        copies[index].wait()
        if index + 3 < len(copies):
            copies[index + 3].start()

    grad_rows = rows_ref[:, width:]
    for half in range(2):
        ready(half)
        grad_act_ref[half] = contract_last(grad_rows, down_ref[half])
    dots_ref[...] = jnp.zeros(dots_ref.shape, F32)
    tall = 16
    rows = rows_ref[:, 0:width]
    for half in range(2):
        ready(2 + 2 * half)
        gate_pre_ref[...] = jnp.dot(rows, gate_ref[half], preferred_element_type=F32)
        ready(3 + 2 * half)
        up_pre_ref[...] = jnp.dot(rows, up_ref[half], preferred_element_type=F32)

        def chunk(r, carry):
            at = pl.ds(pl.multiple_of(r * tall, tall), tall)
            dots = dots_ref[at]
            for c in range(units // LANES):
                lanes = slice(c * LANES, (c + 1) * LANES)
                gate_pre = gate_pre_ref[at, lanes]
                up_pre = up_pre_ref[at, lanes]
                grad_act = grad_act_ref[half, at, lanes]
                sigma = jax.nn.sigmoid(gate_pre)
                gated = gate_pre * sigma
                act = (gated * up_pre).astype(BF16)
                act_ref[half, at, lanes] = act
                grad_gate_ref[half, at, lanes] = (
                    grad_act * up_pre * sigma * (1.0 + gate_pre * (1.0 - sigma))
                ).astype(BF16)
                grad_up_ref[half, at, lanes] = (grad_act * gated).astype(BF16)
                dots = dots + act.astype(F32) * grad_act
            dots_ref[at] = dots
            return carry

        lax.fori_loop(0, slots // tall, chunk, 0)
    dots = jnp.broadcast_to(jnp.sum(dots_ref[...], axis=1, keepdims=True), (slots, LANES))
    high = dots.astype(BF16).astype(F32)
    lane = lax.broadcasted_iota(jnp.int32, (slots, LANES), 1)
    out_ref[:, 2 * width :] = jnp.where(lane == 0, high, dots - high).astype(BF16)
    share = jnp.dot(act_ref[0], down_ref[0], preferred_element_type=F32)
    share = share + jnp.dot(act_ref[1], down_ref[1], preferred_element_type=F32)
    out_ref[:, 0:width] = share.astype(BF16)
    share = contract_last(grad_gate_ref[0], gate_ref[0]) + contract_last(grad_up_ref[0], up_ref[0])
    share = share + contract_last(grad_gate_ref[1], gate_ref[1])
    share = share + contract_last(grad_up_ref[1], up_ref[1])
    out_ref[:, width : 2 * width] = share.astype(BF16)


def combine_body(back_ref, info_ref, out_ref):
    slots = back_ref.shape[0]
    width = (back_ref.shape[1] - LANES) // 2
    info = info_ref[...]
    tokens = info.shape[0]
    first, second = slot_maps(info, slots)
    weights = [
        first * info[:, 2 + part : 3 + part] + second * info[:, 5 + part : 6 + part]
        for part in range(2)
    ]
    total = jnp.dot(
        jnp.concatenate(weights, 0).astype(BF16), back_ref[:, 0:width], preferred_element_type=F32
    )
    out_ref[:, 0:width] = (total[0:tokens] + total[tokens:]).astype(BF16)
    both = (first + second).astype(BF16)
    out_ref[:, width : 2 * width] = jnp.dot(
        both, back_ref[:, width : 2 * width], preferred_element_type=F32
    ).astype(BF16)
    lane = lax.broadcasted_iota(jnp.int32, (tokens, LANES), 1)
    packed = jnp.zeros(lane.shape, F32)
    for k, chosen in enumerate((first, second)):
        dots = jnp.dot(chosen.astype(BF16), back_ref[:, 2 * width :], preferred_element_type=F32)
        dots = jnp.broadcast_to(dots[:, 0:1] + dots[:, 1:2], dots.shape)
        for part, value in enumerate(parts_of(dots, 2)):
            packed = jnp.where(lane == 2 * k + part, value, packed)
    out_ref[:, 2 * width :] = packed.astype(BF16)


def finish_body(
    back_ref, hidden_ref, gain_ref, cotangent_ref, scores_ref, layer_ref, grad_ref, dots_ref
):
    rows, width = hidden_ref.shape
    total = back_ref[0].astype(F32)
    for c in range(1, back_ref.shape[0]):
        total = total + back_ref[c].astype(F32)
    hidden = hidden_ref[...]
    layer_ref[...] = (hidden + total[:, 0:width]).astype(BF16)
    scale = lax.rsqrt(jnp.mean(hidden * hidden, axis=1, keepdims=True) + 1e-05)
    scaled = total[:, width : 2 * width] * gain_ref[...]
    outer = cotangent_ref[...].astype(F32)
    grad_ref[...] = (
        outer
        + scale * scaled
        - hidden * (scale * scale * scale) * jnp.mean(hidden * scaled, axis=1, keepdims=True)
    )
    lane = lax.broadcasted_iota(jnp.int32, (rows, rows), 1)
    sub = lax.broadcasted_iota(jnp.int32, (rows, rows), 0)
    for k in range(2):
        start = 2 * width + 2 * k
        dots = total[:, start : start + 1] + total[:, start + 1 : start + 2]
        spread = jnp.where(lane == sub, jnp.broadcast_to(dots, lane.shape), 0.0)
        dots = jnp.sum(spread, axis=0, keepdims=True)
        dots_ref[k : k + 1] = dots / scores_ref[k : k + 1]


def make_per_device(interpret):
    def call(body, name, outs, ins, scratch=(), operands=(), mib=24, **options):
        if options:
            body = partial(body, **options)
        near = operands
        if not interpret:
            near = [
                value if spec is SMEM else pltpu.with_memory_space_constraint(
                    value, pltpu.VMEM if spec is NEAR else pltpu.HBM
                )
                for spec, value in zip(ins, operands)
            ]
        else:
            outs = jax.tree.map(lambda out: jax.ShapeDtypeStruct(out.shape, out.dtype), outs)
        return pl.pallas_call(
            body,
            out_shape=outs,
            in_specs=[VMEM if spec is NEAR else spec for spec in ins],
            out_specs=jax.tree.map(lambda _: VMEM, outs),
            scratch_shapes=list(scratch),
            interpret=interpret,
            name=name,
            compiler_params=pltpu.CompilerParams(vmem_limit_bytes=mib * 1024 * 1024),
        )(*near)

    def per_device(
        mixer_input, mixer_gate, step_low, step_proj, step_bias, decay_rate, input_coef,
        output_coef, conv_taps, conv_bias, skip_gain, out_weight, residual, norm_gain,
        expert_ids, gate_scores, gate_weight, up_weight, down_weight, cotangent,
    ):
        length, channels = mixer_input.shape
        count = decay_rate.shape[0]
        tok_rows, width = residual.shape
        units = gate_weight.shape[2]
        experts = lax.axis_size("exp")
        depth = lax.axis_size("z")
        ranks = depth * lax.axis_size("core")
        slots = 2 * experts * depth
        stride = 2 * depth
        swap = [(0, 1), (1, 0)]
        shape = jax.ShapeDtypeStruct
        near = pltpu.VMEM

        def sibling(value):
            return lax.ppermute(value, "core", swap)

        def exchange(rows, axis):
            return lax.all_to_all(rows, axis, split_axis=0, concat_axis=0, tiled=True)

        before = lax.ppermute(mixer_input, ("z", "core"), [(i, i + 1) for i in range(ranks - 1)])
        scores = gate_scores.T

        rows = near((length, channels), F32)
        extra_rows = tok_rows * (1 + width // channels)
        late, step, inner, extra = call(
            local_state_body, "local_state",
            (
                near((count + GROUP, channels), F32), rows, rows,
                near((extra_rows, channels), BF16),
            ),
            [VMEM] * 11,
            (pltpu.VMEM((length + GROUP, channels), F32), pltpu.VMEM((length, channels), F32)),
            (
                mixer_input, step_low, step_proj, step_bias[None], decay_rate, input_coef,
                conv_taps, conv_bias[None], expert_ids.T, scores, cotangent,
            ),
            stride=stride,
        )
        summary, inner_first = call(
            first_group_body, "first_group",
            (
                near((2 * count + GROUP + extra_rows, channels), BF16),
                near((GROUP, channels), F32),
            ),
            [NEAR] + [VMEM] * 3 + [NEAR] + [VMEM] * 2 + [NEAR] * 2,
            (pltpu.VMEM((2 * GROUP, channels), F32),),
            (
                before, mixer_input, conv_taps, conv_bias[None], step, decay_rate, input_coef,
                late, extra,
            ),
        )
        gathered = lax.all_gather(summary, ("z", "core"), axis=0)
        gathered, gate_sent, up_sent, down_sent = lax.optimization_barrier(
            (gathered, gate_weight[0], up_weight[0], down_weight[0])
        )
        gates = (gate_weight[0], sibling(gate_sent))
        ups = (up_weight[0], sibling(up_sent))
        downs = (down_weight[0], sibling(down_sent))
        mine = lax.axis_index(("z", "core")).astype(jnp.int32).reshape(1)
        share, packed_grad, info = call(
            readout_body, "readout",
            (
                near((length, width), BF16), near((slots, width), BF16),
                near((depth * tok_rows, LANES), F32),
            ),
            [SMEM, NEAR] + [VMEM] * 3 + [NEAR] * 3 + [VMEM] * 3,
            (
                pltpu.VMEM((length, channels), F32), pltpu.VMEM((length, channels), F32),
                pltpu.VMEM((length, channels), F32), pltpu.VMEM((depth * tok_rows, width), F32),
            ),
            (
                mine, gathered, decay_rate, input_coef, output_coef, step, inner, inner_first,
                skip_gain[None], mixer_gate, out_weight,
            ),
        )
        shares = exchange(share, "exp").reshape(experts, tok_rows, width)
        hidden, send = call(
            norm_body, "norm",
            (near((tok_rows, width), F32), near((depth, tok_rows, width), BF16)),
            [NEAR] + [VMEM] * 2,
            operands=(shares, residual, norm_gain[None]),
        )
        tokens = exchange(send.reshape(depth * tok_rows, width), "z")
        packed = call(
            pack_body, "pack", near((slots, 2 * width), BF16), [NEAR] * 3,
            operands=(tokens, info, packed_grad),
        )
        rows_x = exchange(packed, "exp")
        result = call(
            expert_body, "expert", near((slots, 2 * width + LANES), BF16),
            [NEAR] + [ANY] * 6,
            (
                pltpu.VMEM((2, width, units), BF16),
                pltpu.VMEM((2, width, units), BF16),
                pltpu.VMEM((2, units, width), BF16),
                pltpu.VMEM((slots, units), F32),
                pltpu.VMEM((slots, units), F32),
                pltpu.VMEM((2, slots, units), BF16),
                pltpu.VMEM((2, slots, units), BF16),
                pltpu.VMEM((2, slots, units), BF16),
                pltpu.VMEM((slots, LANES), F32),
                pltpu.VMEM((2, slots, units), F32),
                pltpu.SemaphoreType.DMA((6,)),
            ),
            (rows_x,) + gates + ups + downs,
            48,
        )
        back = exchange(result, "exp")
        shares_back = call(
            combine_body, "combine", near((depth * tok_rows, 2 * width + LANES), BF16),
            [NEAR] * 2, operands=(back, info),
        )
        mine_back = exchange(shares_back, "z").reshape(depth, tok_rows, 2 * width + LANES)
        layer_out, grad_hidden, dots = call(
            finish_body, "finish",
            (
                shape((tok_rows, width), BF16), shape((tok_rows, width), F32),
                shape(scores.shape, F32),
            ),
            [NEAR] * 2 + [VMEM] * 3,
            operands=(mine_back, hidden, norm_gain[None], cotangent, scores),
        )
        return layer_out, grad_hidden, dots.T

    return per_device


def solution(mesh, interpret=False):
    ctx, exp = mesh.devices.shape
    split = Mesh(mesh.devices.reshape(ctx // 2, 2, exp), ("z", "core", "exp"))
    both = ("z", "core")
    rows = P(("z", "core", "exp"), None)
    in_specs = (
        P(both, "exp"),
        P(both, "exp"),
        P(both, None),
        P(None, "exp"),
        P("exp"),
        P(None, "exp"),
        P(None, both),
        P(None, both),
        P(None, "exp"),
        P("exp"),
        P("exp"),
        P("exp", None),
        rows,
        P(),
        rows,
        rows,
        P("exp", None, both),
        P("exp", None, both),
        P("exp", both, None),
        rows,
    )
    return jax.shard_map(
        make_per_device(interpret),
        mesh=split,
        in_specs=in_specs,
        out_specs=(rows, rows, rows),
        check_vma=False,
    )
```
